128 devices in a mesh: seq: 8 (over z, y_hi), chan: 8 (over x, core), dp: 2 (over y_lo).
Axes of the slice: x: 4, y: 4 (y_hi: 2, y_lo: 2; y = y_hi * 2 + y_lo), z: 4, core: 2. Of those that a mesh axis runs over, the one named last changes fastest.
Arguments:
- tokens: bfloat16 [2, 1024, 8192], P('dp', 'seq'), may hold values from -6 to 6
- in_weight: bfloat16 [8192, 3, 4096], P('seq', None, 'chan'), may hold values from -0.0625 to 0.0625
- short_taps: float32 [3, 3, 4096], P(None, None, 'chan'), may hold values from -1 to 1
- long_filter: float32 [1024, 4096], P('seq', 'chan'), may hold values from -1.25 to 1.25
- skip_gain: float32 [4096], P('chan'), may hold values from 0.5 to 1.5
- cotangent: bfloat16 [2, 1024, 4096], P('dp', 'seq', 'chan'), may hold values from -6 to 6
Outputs:
- hyena_out: bfloat16 [2, 1024, 4096], P('dp', 'seq', 'chan')
- grad_tokens: bfloat16 [2, 1024, 8192], P('dp', None, ('seq', 'chan'))
- grad_weight: bfloat16 [8192, 3, 4096], P('seq', None, 'chan')
- grad_filter: float32 [1024, 4096], P('seq', 'chan')
The draws below stay inside these ranges and needn't reach their ends.
All inputs are finite; a program needn't handle non-finite values.
Results may differ from the reference program's by a relative error of at most 0.02.
Values may be sent and summed in bfloat16 or wider, within the bound.
No kernel may reach another device: no remote copies, remote signals or barrier semaphores. Data moves between devices by JAX's collectives and lax.ppermute only.
A program may use at most 128 MiB of HBM per device.

```python
import jax
import jax.numpy as jnp

D = 8192
C = 4096
KS = 3
L = 1024
BATCH = 2


def draw_long_filter(key, part):
    keys = jax.random.split(key, 5)
    steps = jnp.arange(L, dtype=jnp.float32)[:, None]
    noise = jax.random.truncated_normal(keys[0], -3.5, 3.5, (L, C), jnp.float32)
    log_rate = jax.random.uniform(keys[1], (C,), jnp.float32, jnp.log(0.02 / L), jnp.log(1.0 / 30.0))
    rate = jnp.exp(log_rate)
    cuts = jax.random.randint(keys[4], (2, C), 0, L)
    drops = jnp.where(steps >= cuts[0].astype(jnp.float32), 0.6, 1.0) * jnp.where(steps >= cuts[1].astype(jnp.float32), 0.6, 1.0)
    amplitude = jnp.sqrt(jnp.maximum(2.0 * rate, 1.0 / L))
    return (noise * jnp.exp(-rate * steps) * drops * amplitude).astype(jnp.float32)


def shard_levels(own_key, shape, cuts, low, top_value):
    def one(position, shards_of):
        draws = jax.random.uniform(jax.random.fold_in(jax.random.fold_in(own_key, 6), position), (shards_of,), jnp.float32, low / len(cuts), top_value / len(cuts))
        return jnp.repeat(jnp.exp(draws), shape[position] // shards_of).reshape((-1,) + (1,) * (len(shape) - position - 1))

    factor_of = one(*cuts[0])
    for cut in cuts[1:]:
        factor_of = factor_of * one(*cut)
    return factor_of


def normal_values(own_key, shape, spread, limit, cuts=(), held_as=jnp.bfloat16):
    level = shard_levels(own_key, shape, cuts, -0.22, 0.18) if cuts else 1.0
    result = jax.random.normal(own_key, shape, jnp.float32) * spread * level
    return jnp.minimum(jnp.maximum(result, -limit), limit).astype(held_as)


def setup_inputs(seed: int = 0) -> dict:
    splits = jax.random.split(jax.random.key(seed), 7)
    tokens = normal_values(splits[0], (BATCH, L, D), 1.0, 6.0, ((0, 2), (1, 8)))
    in_weight = normal_values(splits[1], (D, 3, C), D ** -0.5, 0.0625, ((0, 8), (2, 8)))
    short_taps = jnp.clip(jax.random.uniform(splits[2], (3, KS, C), jnp.float32, -1.0, 1.0) * shard_levels(splits[2], (3, KS, C), ((2, 8),), -0.4, 0.0), -1.0, 1.0)
    long_filter = draw_long_filter(jax.random.fold_in(splits[6], 71), 0)
    skip_gain = jnp.clip(0.5 + 1.0 * jax.random.uniform(splits[4], (C,), jnp.float32) ** shard_levels(splits[4], (C,), ((0, 8),), -0.2, 0.2), 0.5, 1.5)
    cotangent = normal_values(splits[5], (BATCH, L, C), 1.0, 6.0, ((0, 2), (1, 8), (2, 8)))
    return dict(tokens=tokens, in_weight=in_weight, short_taps=short_taps, long_filter=long_filter, skip_gain=skip_gain, cotangent=cotangent)


def reference(tokens, in_weight, short_taps, long_filter, skip_gain, cotangent):
    batch_count, seq_len, model_width = tokens.shape
    chan_count = in_weight.shape[2]
    taps_len = short_taps.shape[1]
    fft_len = 2 * seq_len
    grad_scale = (batch_count * seq_len) ** -0.5
    flat_tokens = tokens.reshape(batch_count * seq_len, model_width)
    flat_weight = in_weight.reshape(model_width, 3 * chan_count)
    projected = jnp.dot(flat_tokens, flat_weight, preferred_element_type=jnp.float32)
    projected = projected.reshape(batch_count, seq_len, 3, chan_count)
    padded = jnp.pad(projected, ((0, 0), (taps_len - 1, 0), (0, 0), (0, 0)))
    streams = jnp.zeros_like(projected)
    for tap_pos in range(taps_len):
        begin = taps_len - 1 - tap_pos
        streams = streams + short_taps[:, tap_pos, :] * padded[:, begin:begin + seq_len]
    queries = streams[:, :, 0]
    keys_in = streams[:, :, 1]
    values_in = streams[:, :, 2]
    gated_in = keys_in * values_in
    filter_freq = jnp.fft.rfft(long_filter, n=fft_len, axis=0)[None]
    gated_freq = jnp.fft.rfft(gated_in, n=fft_len, axis=1)
    conv_out = jnp.fft.irfft(gated_freq * filter_freq, n=fft_len, axis=1)[:, :seq_len] + skip_gain * gated_in
    hyena_out = (queries * conv_out).astype(jnp.bfloat16)
    grad_in = cotangent.astype(jnp.float32)
    d_conv = grad_in * queries
    d_query = grad_in * conv_out
    conv_freq = jnp.fft.rfft(d_conv, n=fft_len, axis=1)
    d_gated = jnp.fft.irfft(jnp.conj(filter_freq) * conv_freq, n=fft_len, axis=1)[:, :seq_len] + skip_gain * d_conv
    filter_terms = jnp.fft.irfft(jnp.conj(gated_freq) * conv_freq, n=fft_len, axis=1)[:, :seq_len]
    grad_filter = grad_scale * jnp.sum(filter_terms, axis=0)
    d_streams = jnp.stack([d_query, d_gated * values_in, d_gated * keys_in], axis=2)
    padded_next = jnp.pad(d_streams, ((0, 0), (0, taps_len - 1), (0, 0), (0, 0)))
    d_projected = jnp.zeros_like(d_streams)
    for tap_pos in range(taps_len):
        d_projected = d_projected + short_taps[:, tap_pos, :] * padded_next[:, tap_pos:tap_pos + seq_len]
    d_projected = d_projected.astype(jnp.bfloat16).reshape(batch_count * seq_len, 3 * chan_count)
    grad_tokens = jnp.dot(d_projected, flat_weight.T, preferred_element_type=jnp.float32)
    grad_tokens = grad_tokens.astype(jnp.bfloat16).reshape(batch_count, seq_len, model_width)
    weight_total = jnp.dot(flat_tokens.T, d_projected, preferred_element_type=jnp.float32)
    grad_weight = (grad_scale * weight_total).astype(jnp.bfloat16).reshape(model_width, 3, chan_count)
    return (hyena_out, grad_tokens, grad_weight, grad_filter.astype(jnp.float32))
```

```python
import functools
import math

import jax
import jax.numpy as jnp
from jax import lax
from jax.experimental import pallas as pl
from jax.experimental.pallas import tpu as pltpu
from jax.sharding import PartitionSpec as P

BF = jnp.bfloat16
F32 = jnp.float32
VMEM_BYTES = 48 << 20
NT = (((1,), (1,)), ((), ()))
NN = (((1,), (0,)), ((), ()))


def params():
    return pltpu.CompilerParams(vmem_limit_bytes=VMEM_BYTES)


def cost(flops, bytes_accessed):
    return pl.CostEstimate(flops=flops, bytes_accessed=bytes_accessed, transcendentals=0)


def matmul(left, right, dims):
    return lax.dot_general(left, right, dims, preferred_element_type=F32)


def split(value):
    high = value.astype(BF)
    return high, (value - high.astype(F32)).astype(BF)


def edge_kernel(cot_ref, filter_ref, out_ref):
    slabs, rows, _ = out_ref.shape
    chans = rows // 3
    high, low = split(jnp.transpose(filter_ref[...]))
    cot = jnp.transpose(cot_ref[0].astype(F32)).astype(BF)
    for slab in range(slabs):
        part = slice(slab * chans, (slab + 1) * chans)
        out_ref[slab, :chans] = cot[part]
        out_ref[slab, chans : 2 * chans] = high[part]
        out_ref[slab, 2 * chans :] = low[part]


def edge_rows(cotangent, long_filter, slabs):
    _, tok_rows, chan_cols = cotangent.shape
    return pl.pallas_call(
        edge_kernel,
        out_shape=jax.ShapeDtypeStruct((slabs, 3 * chan_cols // slabs, tok_rows), BF),
        compiler_params=params(),
        cost_estimate=cost(0, 8 * tok_rows * chan_cols),
        name="edge_rows",
    )(cotangent, long_filter)


def flip_kernel(weight_ref, out_ref):
    out_ref[0] = jnp.transpose(weight_ref[0])


def flip_weight(weight):
    streams, slab_rows, chan_cols = weight.shape
    half = chan_cols // 2
    return pl.pallas_call(
        flip_kernel,
        grid=(streams, 2),
        in_specs=[pl.BlockSpec((1, slab_rows, half), lambda i, j: (i, 0, j))],
        out_specs=pl.BlockSpec((1, half, slab_rows), lambda i, j: (i, j, 0)),
        out_shape=jax.ShapeDtypeStruct((streams, chan_cols, slab_rows), BF),
        compiler_params=params(),
        cost_estimate=cost(0, 4 * weight.size),
        name="flip_weight",
    )(weight)


def table_kernel(cos_a_ref, sin_a_ref, cos_b_ref, sin_b_ref, out_ref):
    steps = cos_b_ref.shape[0]
    cos_a = cos_a_ref[0]
    sin_a = sin_a_ref[0]
    cos_b = cos_b_ref[...]
    sin_b = sin_b_ref[...]
    for pos, table in enumerate((cos_a * cos_b - sin_a * sin_b, sin_a * cos_b + cos_a * sin_b)):
        high, low = split(table)
        out_ref[pos] = high
        out_ref[2 + pos] = low


def angle(product, period):
    phases = 2.0 * math.pi / period * (product % period).astype(F32)
    return jnp.cos(phases), jnp.sin(phases)


def tables(count):
    steps = 64
    odd = 2 * jnp.arange(count, dtype=jnp.int32)[None, :] + 1
    period = 8 * count
    base = jnp.arange(count // steps, dtype=jnp.int32)[:, None] * (2 * steps)
    fine = 2 * jnp.arange(steps, dtype=jnp.int32)[:, None] + 1
    cos_a, sin_a = angle(base * odd, period)
    cos_b, sin_b = angle(fine * odd, period)
    return pl.pallas_call(
        table_kernel,
        grid=(count // steps,),
        in_specs=[
            pl.BlockSpec((1, 1, count), lambda i: (i, 0, 0)),
            pl.BlockSpec((1, 1, count), lambda i: (i, 0, 0)),
            pl.BlockSpec((steps, count), lambda i: (0, 0)),
            pl.BlockSpec((steps, count), lambda i: (0, 0)),
        ],
        out_specs=pl.BlockSpec((4, steps, count), lambda i: (0, i, 0)),
        out_shape=jax.ShapeDtypeStruct((4, count, count), BF),
        compiler_params=params(),
        cost_estimate=cost(0, 8 * count * count),
        name="tables",
    )(cos_a[:, None], sin_a[:, None], cos_b, sin_b)


def position_rows(tokens_ref, out_ref):
    _, blocks, rows, width = tokens_ref.shape
    group = tokens_ref.shape[0] * rows
    for block in range(blocks):
        out_ref[block * group : (block + 1) * group] = tokens_ref[:, block].reshape(group, width)


def project_kernel(tokens_ref, weight_ref, out_ref, spread_ref):
    @pl.when(pl.program_id(0) == 0)
    def _():
        position_rows(tokens_ref, spread_ref)

    slabs, _, chans, positions = out_ref.shape
    result = matmul(weight_ref[0], spread_ref[...], NT).astype(BF)
    out_ref[:, 0] = result.reshape(slabs, chans, positions)


def project(tokens, weight, slabs):
    groups, blocks, rows, width = tokens.shape
    streams, chan_cols, _ = weight.shape
    positions = groups * blocks * rows
    chans = chan_cols // slabs
    return pl.pallas_call(
        project_kernel,
        grid=(streams,),
        in_specs=[
            pl.BlockSpec(tokens.shape, lambda i: (0, 0, 0, 0)),
            pl.BlockSpec((1, chan_cols, width), lambda i: (i, 0, 0)),
        ],
        out_specs=pl.BlockSpec((slabs, 1, chans, positions), lambda i: (0, i, 0, 0)),
        out_shape=jax.ShapeDtypeStruct((slabs, streams, chans, positions), BF),
        scratch_shapes=[pltpu.VMEM((positions, width), BF)],
        compiler_params=params(),
        cost_estimate=cost(
            2 * positions * width * streams * chan_cols,
            2 * (tokens.size + weight.size + positions * streams * chan_cols),
        ),
        name="project",
    )(tokens, weight)


def turn_kernel(tokens_ref, out_ref, spread_ref):
    position_rows(tokens_ref, spread_ref)
    out_ref[...] = jnp.transpose(spread_ref[...])


def turn_tokens(tokens):
    groups, blocks, rows, width = tokens.shape
    positions = groups * blocks * rows
    part = width // 4
    return pl.pallas_call(
        turn_kernel,
        grid=(4,),
        in_specs=[pl.BlockSpec((groups, blocks, rows, part), lambda i: (0, 0, 0, i))],
        out_specs=pl.BlockSpec((part, positions), lambda i: (i, 0)),
        out_shape=jax.ShapeDtypeStruct((width, positions), BF),
        scratch_shapes=[pltpu.VMEM((positions, part), BF)],
        compiler_params=params(),
        cost_estimate=cost(0, 4 * tokens.size),
        name="turn_tokens",
    )(tokens)


def delayed(value, steps):
    if steps == 0:
        return value
    lane = lax.broadcasted_iota(jnp.int32, value.shape, 1)
    return jnp.where(lane < steps, 0.0, pltpu.roll(value, steps, 1))


def advanced(value, steps):
    if steps == 0:
        return value
    lanes = value.shape[1]
    lane = lax.broadcasted_iota(jnp.int32, value.shape, 1)
    return jnp.where(lane >= lanes - steps, 0.0, pltpu.roll(value, lanes - steps, 1))


def transform(value, high_table, low_table):
    high, low = split(value)
    return (
        matmul(high, high_table, NN) + matmul(low, high_table, NN) + matmul(high, low_table, NN)
    )


def operator_kernel(grad_scale, parts_ref, edge_ref, taps_ref, phase_ref, table_ref, grads_ref, out_ref):
    sources, streams, chans, positions = parts_ref.shape
    taps_len = (taps_ref.shape[1] - 1) // streams
    blocks, _, block_len = edge_ref.shape

    def tap(stream, pos):
        column = stream * taps_len + pos
        return taps_ref[:, column : column + 1]

    filtered = []
    for stream in range(streams):
        total = parts_ref[0, stream].astype(F32)
        for source in range(1, sources):
            total = total + parts_ref[source, stream].astype(F32)
        acc = tap(stream, 0) * total
        for pos in range(1, taps_len):
            acc = acc + tap(stream, pos) * delayed(total, pos)
        filtered.append(acc)
    query, key, value = filtered
    skip = taps_ref[:, streams * taps_len : streams * taps_len + 1]

    def edge(row):
        return jnp.concatenate(
            [edge_ref[block, row * chans : (row + 1) * chans].astype(F32) for block in range(blocks)],
            axis=1,
        )

    cot = edge(0)
    long_filter = edge(1) + edge(2)
    gated = key * value
    d_conv = cot * query
    stacked = jnp.concatenate([gated, long_filter, d_conv], axis=0)
    cos_all = transform(stacked, table_ref[0], table_ref[2])
    sin_all = transform(stacked, table_ref[1], table_ref[3])
    g_cos, h_cos, d_cos = (cos_all[i * chans : (i + 1) * chans] for i in range(3))
    g_sin, h_sin, d_sin = (sin_all[i * chans : (i + 1) * chans] for i in range(3))
    cos_phase = phase_ref[0:1]
    sin_phase = phase_ref[1:2]
    h_real = h_cos * cos_phase + h_sin * sin_phase
    h_imag = h_cos * sin_phase - h_sin * cos_phase
    conv_real = g_cos * h_real + g_sin * h_imag
    conv_imag = g_cos * h_imag - g_sin * h_real
    back_real = h_real * d_cos - h_imag * d_sin
    back_imag = -(h_real * d_sin + h_imag * d_cos)
    corr_real = g_cos * d_cos + g_sin * d_sin
    corr_imag = g_sin * d_cos - g_cos * d_sin
    lag_real = corr_real * cos_phase + corr_imag * sin_phase
    lag_imag = corr_imag * cos_phase - corr_real * sin_phase
    scale = 1.0 / positions
    real_all = jnp.concatenate([conv_real, back_real, lag_real], axis=0) * scale
    imag_all = jnp.concatenate([conv_imag, back_imag, lag_imag], axis=0) * scale
    result = transform(real_all, table_ref[0], table_ref[2]) - transform(
        imag_all, table_ref[1], table_ref[3]
    )
    conv_out = result[:chans] + skip * gated
    d_gated = result[chans : 2 * chans] + skip * d_conv
    filter_part = (result[2 * chans :] * grad_scale).astype(BF)
    hyena_out = (query * conv_out).astype(BF)
    for block in range(blocks):
        lanes = slice(block * block_len, (block + 1) * block_len)
        out_ref[block, :chans] = hyena_out[:, lanes]
        out_ref[block, chans:] = filter_part[:, lanes]
    for stream, grad in enumerate((cot * conv_out, d_gated * value, d_gated * key)):
        acc = tap(stream, 0) * grad
        for pos in range(1, taps_len):
            acc = acc + tap(stream, pos) * advanced(grad, pos)
        grads_ref[stream * chans : (stream + 1) * chans] = acc.astype(BF)


def operator(parts, edge, taps, phase, table, grad_scale):
    sources, streams, chans, positions = parts.shape
    blocks, _, block_len = edge.shape
    return pl.pallas_call(
        functools.partial(operator_kernel, grad_scale),
        out_shape=(
            jax.ShapeDtypeStruct((streams * chans, positions), BF),
            jax.ShapeDtypeStruct((blocks, 2 * chans, block_len), BF),
        ),
        compiler_params=params(),
        cost_estimate=cost(24 * streams * chans * positions * positions, 2 * (parts.size + table.size)),
        name="operator",
    )(parts, edge, taps, phase, table)


def token_kernel(dp_ref, weight_ref, grads_ref, out_ref):
    streams, _, chan_cols = weight_ref.shape
    positions = grads_ref.shape[-1]
    total = None
    for stream in range(streams):
        grads = grads_ref[:, 0, stream].reshape(chan_cols, positions)
        part = matmul(weight_ref[stream], grads, NN)
        total = part if total is None else total + part
    out_ref[...] = total.astype(BF)


def token_part(dp_pos, weight, grads):
    streams, slab_rows, chan_cols = weight.shape
    slabs, batches, _, chans, positions = grads.shape
    part = slab_rows // 4
    return pl.pallas_call(
        token_kernel,
        grid_spec=pltpu.PrefetchScalarGridSpec(
            num_scalar_prefetch=1,
            grid=(4,),
            in_specs=[
                pl.BlockSpec((streams, part, chan_cols), lambda j, dp: (0, j, 0)),
                pl.BlockSpec((slabs, 1, streams, chans, positions), lambda j, dp: (0, dp[0], 0, 0, 0)),
            ],
            out_specs=pl.BlockSpec((part, positions), lambda j, dp: (j, 0)),
        ),
        out_shape=jax.ShapeDtypeStruct((slab_rows, positions), BF),
        compiler_params=params(),
        cost_estimate=cost(
            2 * streams * slab_rows * chan_cols * positions,
            2 * (weight.size + grads.size // batches + slab_rows * positions),
        ),
        name="token_part",
    )(dp_pos, weight, grads)


def weight_kernel(grad_scale, dp_ref, own_ref, other_ref, own_grads_ref, other_grads_ref, out_ref):
    chan_cols = out_ref.shape[2]
    positions = own_ref.shape[1]
    own = own_grads_ref[...].reshape(chan_cols, positions)
    other = other_grads_ref[...].reshape(chan_cols, positions)
    total = matmul(own_ref[...], own, NT) + matmul(other_ref[...], other, NT)
    out_ref[0] = (total * grad_scale).astype(BF)


def weight_grad(dp_pos, own, other, grads, grad_scale):
    slabs, _, streams, chans, positions = grads.shape
    slab_rows = own.shape[0]
    chan_cols = slabs * chans
    block = (slabs, 1, 1, chans, positions)
    return pl.pallas_call(
        functools.partial(weight_kernel, grad_scale),
        grid_spec=pltpu.PrefetchScalarGridSpec(
            num_scalar_prefetch=1,
            grid=(streams,),
            in_specs=[
                pl.BlockSpec(own.shape, lambda i, dp: (0, 0)),
                pl.BlockSpec(own.shape, lambda i, dp: (0, 0)),
                pl.BlockSpec(block, lambda i, dp: (0, dp[0], i, 0, 0)),
                pl.BlockSpec(block, lambda i, dp: (0, 1 - dp[0], i, 0, 0)),
            ],
            out_specs=pl.BlockSpec((1, slab_rows, chan_cols), lambda i, dp: (i, 0, 0)),
        ),
        out_shape=jax.ShapeDtypeStruct((streams, slab_rows, chan_cols), BF),
        compiler_params=params(),
        cost_estimate=cost(
            4 * streams * slab_rows * chan_cols * positions,
            2 * (2 * own.size + grads.size + streams * slab_rows * chan_cols),
        ),
        name="weight_grad",
    )(dp_pos, own, other, grads, grads)


def total_kernel(parts_ref, out_ref):
    total = parts_ref[0].astype(F32)
    for pos in range(1, parts_ref.shape[0]):
        total = total + parts_ref[pos].astype(F32)
    out_ref[0] = jnp.transpose(total).astype(BF)


def token_total(parts):
    _, rows, positions = parts.shape
    return pl.pallas_call(
        total_kernel,
        out_shape=jax.ShapeDtypeStruct((1, positions, rows), BF),
        compiler_params=params(),
        cost_estimate=cost(0, 2 * parts.size),
        name="token_total",
    )(parts)


def finish_kernel(own_ref, other_ref, out_ref, filter_ref):
    slabs, rows, block_len = own_ref.shape
    chans = rows // 2
    out = own_ref[:, :chans].reshape(slabs * chans, block_len)
    own = own_ref[:, chans:].reshape(slabs * chans, block_len).astype(F32)
    other = other_ref[...].reshape(slabs * chans, block_len).astype(F32)
    out_ref[0] = jnp.transpose(out.astype(F32)).astype(BF)
    filter_ref[...] = jnp.transpose(own + other)


def finish(own, other):
    slabs, rows, block_len = own.shape
    chan_cols = slabs * rows // 2
    return pl.pallas_call(
        finish_kernel,
        out_shape=(
            jax.ShapeDtypeStruct((1, block_len, chan_cols), BF),
            jax.ShapeDtypeStruct((block_len, chan_cols), F32),
        ),
        compiler_params=params(),
        cost_estimate=cost(0, 4 * own.size),
        name="finish",
    )(own, other)


def local(tokens, in_weight, short_taps, long_filter, skip_gain, cotangent):
    seq_count = lax.axis_size("seq")
    seq_pos = lax.axis_index("seq")
    chan_count = lax.axis_size("chan")
    chan_pos = lax.axis_index("chan")
    dp_pos = lax.axis_index("dp").astype(jnp.int32)[None]
    tok_rows = tokens.shape[1]
    slab_rows = in_weight.shape[0]
    chan_cols = in_weight.shape[2]
    streams, taps_len = short_taps.shape[:2]
    positions = seq_count * tok_rows
    chans = chan_cols // seq_count
    share = tok_rows // chan_count
    grad_scale = 1.0 / math.sqrt(lax.axis_size("dp") * positions)
    weight = jnp.transpose(in_weight, (1, 0, 2))

    mine = lax.dynamic_slice_in_dim(tokens[0], chan_pos * share, share, 0)
    mine = jnp.transpose(mine.reshape(share, seq_count, slab_rows), (1, 0, 2))
    mine = lax.all_to_all(mine, "seq", split_axis=0, concat_axis=0, tiled=True)
    swapped = lax.ppermute(mine, "dp", [(0, 1), (1, 0)])
    own_tokens = lax.all_gather(mine, "chan", axis=0)
    other_tokens = lax.all_gather(swapped, "chan", axis=0)

    edge = lax.all_to_all(
        edge_rows(cotangent, long_filter, seq_count), "seq", split_axis=0, concat_axis=0, tiled=True
    )
    taps = jnp.concatenate([short_taps.reshape(streams * taps_len, chan_cols), skip_gain[None]])
    taps = jnp.transpose(lax.dynamic_slice_in_dim(taps, seq_pos * chans, chans, 1))
    table = tables(positions)
    odd = 2 * jnp.arange(positions, dtype=jnp.int32) + 1
    phase = jnp.stack(angle(odd, 8 * positions))

    parts = project(own_tokens, flip_weight(weight), seq_count)
    parts = lax.all_to_all(parts, "seq", split_axis=0, concat_axis=0, tiled=True)
    grads, outs = operator(parts, edge, taps, phase, table, grad_scale)

    all_grads = lax.all_gather(grads, ("seq", "dp"), axis=0)
    all_grads = all_grads.reshape(seq_count, -1, streams, chans, positions)
    outs = lax.all_to_all(outs, "seq", split_axis=0, concat_axis=0, tiled=True)
    other_filter = lax.ppermute(outs[:, chans:], "dp", [(0, 1), (1, 0)])
    hyena_out, grad_filter = finish(outs, other_filter)

    token_block = token_part(dp_pos, weight, all_grads)
    token_block = token_block.reshape(chan_count, -1, positions)
    token_block = lax.all_to_all(token_block, "chan", split_axis=0, concat_axis=0, tiled=True)
    grad_tokens = token_total(token_block)
    grad_weight = weight_grad(
        dp_pos, turn_tokens(own_tokens), turn_tokens(other_tokens), all_grads, grad_scale
    )
    return (hyena_out, grad_tokens, jnp.transpose(grad_weight, (1, 0, 2)), grad_filter)


def solution(mesh):
    placed = (
        P("dp", "seq", None),
        P("seq", None, "chan"),
        P(None, None, "chan"),
        P("seq", "chan"),
        P("chan"),
        P("dp", "seq", "chan"),
    )
    return jax.shard_map(
        local,
        mesh=mesh,
        in_specs=placed,
        out_specs=(
            P("dp", "seq", "chan"),
            P("dp", None, ("seq", "chan")),
            P("seq", None, "chan"),
            P("seq", "chan"),
        ),
        check_vma=False,
    )
```

```python
import functools
import math

import jax
import jax.numpy as jnp
from jax import lax
from jax.experimental import pallas as pl
from jax.experimental.pallas import tpu as pltpu
from jax.sharding import PartitionSpec as P

BF = jnp.bfloat16
F32 = jnp.float32
VMEM_BYTES = 60 << 20
NT = (((1,), (1,)), ((), ()))
NN = (((1,), (0,)), ((), ()))


def params(limit=VMEM_BYTES):
    return pltpu.CompilerParams(vmem_limit_bytes=limit)


def cost(flops, bytes_accessed):
    return pl.CostEstimate(flops=flops, bytes_accessed=bytes_accessed, transcendentals=0)


def kept(shape, dtype=BF):
    return pltpu.HBM(shape, dtype)


def matmul(left, right, dims):
    return lax.dot_general(left, right, dims, preferred_element_type=F32)


def split(value):
    high = value.astype(BF)
    return high, (value - high.astype(F32)).astype(BF)


def edge_kernel(cot_ref, filter_ref, out_ref):
    slabs, rows, lanes = out_ref.shape
    block_len = filter_ref.shape[0]
    chans = filter_ref.shape[1] // slabs
    taps = jnp.transpose(filter_ref[...]).astype(BF)
    cot = jnp.transpose(cot_ref[0].astype(F32)).astype(BF)
    for slab in range(slabs):
        part = slice(slab * chans, (slab + 1) * chans)
        fold(out_ref.at[slab], 0, jnp.concatenate([cot[part], taps[part]], axis=0))


def fold(out_ref, first, value):
    rows, block_len = value.shape
    count = rows * block_len // out_ref.shape[1]
    for pos in range(rows // count):
        out_ref[first : first + count, pos * block_len : (pos + 1) * block_len] = value[
            pos * count : (pos + 1) * count
        ]


def unfold(value, block_len):
    return jnp.concatenate(
        [value[:, at : at + block_len] for at in range(0, value.shape[1], block_len)], axis=0
    )


def edge_rows(cotangent, long_filter, slabs):
    _, tok_rows, chan_cols = cotangent.shape
    lanes = slabs * tok_rows
    return pl.pallas_call(
        edge_kernel,
        out_shape=kept((slabs, 2 * tok_rows * chan_cols // slabs // lanes, lanes)),
        compiler_params=params(),
        cost_estimate=cost(0, 8 * tok_rows * chan_cols),
        name="edge_rows",
    )(cotangent, long_filter)


def arrange_kernel(groups, weight_ref, *out_refs):
    flipped = jnp.transpose(weight_ref[0])
    chans = groups[-1][1]
    slabs = flipped.shape[0] // chans
    for pos, (first, last) in enumerate(groups):
        rows = [flipped[slab * chans + first : slab * chans + last] for slab in range(slabs)]
        rows = jnp.concatenate(rows, axis=0)
        out_refs[2 * pos][0] = rows
        out_refs[2 * pos + 1][0] = jnp.transpose(rows)


def arrange_weight(weight, groups):
    streams, slab_rows, chan_cols = weight.shape
    slabs = chan_cols // groups[-1][1]
    shapes, specs = [], []
    for first, last in groups:
        rows = slabs * (last - first)
        for dims in ((rows, slab_rows), (slab_rows, rows)):
            shapes.append(kept((streams, *dims)))
            specs.append(pl.BlockSpec((1, *dims), lambda i: (i, 0, 0)))
    return pl.pallas_call(
        functools.partial(arrange_kernel, groups),
        grid=(streams,),
        in_specs=[pl.BlockSpec((1, slab_rows, chan_cols), lambda i: (i, 0, 0))],
        out_specs=specs,
        out_shape=shapes,
        compiler_params=params(),
        cost_estimate=cost(0, 6 * weight.size),
        name="arrange_weight",
    )(weight)


def table_kernel(cos_a_ref, sin_a_ref, cos_b_ref, sin_b_ref, out_ref):
    cos_a = cos_a_ref[0]
    sin_a = sin_a_ref[0]
    cos_b = cos_b_ref[...]
    sin_b = sin_b_ref[...]
    out_ref[0] = (cos_a * cos_b - sin_a * sin_b).astype(BF)
    out_ref[1] = (sin_a * cos_b + cos_a * sin_b).astype(BF)


def angle(product, period):
    phases = 2.0 * math.pi / period * (product % period).astype(F32)
    return jnp.cos(phases), jnp.sin(phases)


def tables(count):
    steps = 64
    odd = 2 * jnp.arange(count, dtype=jnp.int32)[None, :] + 1
    period = 8 * count
    base = jnp.arange(count // steps, dtype=jnp.int32)[:, None] * (2 * steps)
    fine = 2 * jnp.arange(steps, dtype=jnp.int32)[:, None] + 1
    cos_a, sin_a = angle(base * odd, period)
    cos_b, sin_b = angle(fine * odd, period)
    return pl.pallas_call(
        table_kernel,
        grid=(count // steps,),
        in_specs=[
            pl.BlockSpec((1, 1, count), lambda i: (i, 0, 0)),
            pl.BlockSpec((1, 1, count), lambda i: (i, 0, 0)),
            pl.BlockSpec((steps, count), lambda i: (0, 0)),
            pl.BlockSpec((steps, count), lambda i: (0, 0)),
        ],
        out_specs=pl.BlockSpec((2, steps, count), lambda i: (0, i, 0)),
        out_shape=jax.ShapeDtypeStruct((2, count, count), BF),
        compiler_params=params(),
        cost_estimate=cost(0, 4 * count * count),
        name="tables",
    )(cos_a[:, None], sin_a[:, None], cos_b, sin_b)


def first_kernel(core_ref, mine_ref, theirs_ref, weight_ref, edge_ref, out_ref, spread_ref):
    blocks, half, _ = mine_ref.shape
    core = core_ref[0]
    step = pl.program_id(0)

    @pl.when(step == 0)
    def _():
        for block in range(blocks):
            base = 2 * block * half
            spread_ref[pl.ds(pl.multiple_of(base + core * half, half), half)] = mine_ref[block]
            spread_ref[pl.ds(pl.multiple_of(base + (1 - core) * half, half), half)] = theirs_ref[block]
        out_ref[:, out_ref.shape[1] - edge_ref.shape[1] :] = edge_ref[...]

    slabs, _, positions = out_ref.shape
    chans = weight_ref.shape[1] // slabs
    result = matmul(weight_ref[0], spread_ref[...], NT).astype(BF).reshape(slabs, chans, positions)
    out_ref[:, pl.ds(pl.multiple_of(step * chans, chans), chans)] = result


def rest_kernel(spread_ref, weight_ref, out_ref):
    slabs, _, chans, positions = out_ref.shape
    result = matmul(weight_ref[0], spread_ref[...], NT).astype(BF)
    out_ref[:, 0] = result.reshape(slabs, chans, positions)


def project_first(core, mine, theirs, weight, edge):
    blocks, half, width = mine.shape
    streams, rows, _ = weight.shape
    slabs, edge_len, positions = edge.shape
    out_dims = (slabs, streams * rows // slabs + edge_len, positions)
    return pl.pallas_call(
        first_kernel,
        grid_spec=pltpu.PrefetchScalarGridSpec(
            num_scalar_prefetch=1,
            grid=(streams,),
            in_specs=[
                pl.BlockSpec(mine.shape, lambda i, core: (0, 0, 0)),
                pl.BlockSpec(mine.shape, lambda i, core: (0, 0, 0)),
                pl.BlockSpec((1, rows, width), lambda i, core: (i, 0, 0)),
                pl.BlockSpec(edge.shape, lambda i, core: (0, 0, 0)),
            ],
            out_specs=[
                pl.BlockSpec(out_dims, lambda i, core: (0, 0, 0)),
                pl.BlockSpec((positions, width), lambda i, core: (0, 0)),
            ],
        ),
        out_shape=(kept(out_dims), kept((positions, width))),
        compiler_params=params(),
        cost_estimate=cost(
            2 * positions * width * streams * rows,
            2 * (2 * positions * width + weight.size + positions * streams * rows),
        ),
        name="project_first",
    )(core, mine, theirs, weight, edge)


def project_rest(spread, weight, slabs):
    positions, width = spread.shape
    streams, rows, _ = weight.shape
    chans = rows // slabs
    return pl.pallas_call(
        rest_kernel,
        grid=(streams,),
        in_specs=[
            pl.BlockSpec((positions, width), lambda i: (0, 0)),
            pl.BlockSpec((1, rows, width), lambda i: (i, 0, 0)),
        ],
        out_specs=pl.BlockSpec((slabs, 1, chans, positions), lambda i: (0, i, 0, 0)),
        out_shape=kept((slabs, streams, chans, positions)),
        compiler_params=params(),
        cost_estimate=cost(
            2 * positions * width * streams * rows,
            2 * (spread.size + weight.size + positions * streams * rows),
        ),
        name="project_rest",
    )(spread, weight)


def turn_kernel(tokens_ref, out_ref):
    out_ref[...] = jnp.transpose(tokens_ref[...])


def turn_tokens(tokens):
    positions, width = tokens.shape
    part = width // 4
    return pl.pallas_call(
        turn_kernel,
        grid=(4,),
        in_specs=[pl.BlockSpec((positions, part), lambda i: (0, i))],
        out_specs=pl.BlockSpec((part, positions), lambda i: (i, 0)),
        out_shape=kept((width, positions)),
        compiler_params=params(),
        cost_estimate=cost(0, 4 * tokens.size),
        name="turn_tokens",
    )(tokens)


def turn_shares_kernel(tokens_ref, out_ref, spread_ref):
    chips, cores, blocks, rows, _ = tokens_ref.shape
    for block in range(blocks):
        for core in range(cores):
            for chip in range(chips):
                base = ((block * cores + core) * chips + chip) * rows
                spread_ref[base : base + rows] = tokens_ref[chip, core, block]
    out_ref[...] = jnp.transpose(spread_ref[...])


def turn_shares(tokens):
    chips, cores, blocks, rows, width = tokens.shape
    positions = chips * cores * blocks * rows
    part = width // 4
    return pl.pallas_call(
        turn_shares_kernel,
        grid=(4,),
        in_specs=[pl.BlockSpec((chips, cores, blocks, rows, part), lambda i: (0, 0, 0, 0, i))],
        out_specs=pl.BlockSpec((part, positions), lambda i: (i, 0)),
        out_shape=kept((width, positions)),
        scratch_shapes=[pltpu.VMEM((positions, part), BF)],
        compiler_params=params(),
        cost_estimate=cost(0, 4 * tokens.size),
        name="turn_shares",
    )(tokens)


def delayed(value, steps):
    if steps == 0:
        return value
    lane = lax.broadcasted_iota(jnp.int32, value.shape, 1)
    return jnp.where(lane < steps, 0.0, pltpu.roll(value, steps, 1))


def advanced(value, steps):
    if steps == 0:
        return value
    lanes = value.shape[1]
    lane = lax.broadcasted_iota(jnp.int32, value.shape, 1)
    return jnp.where(lane >= lanes - steps, 0.0, pltpu.roll(value, lanes - steps, 1))


def transform(value, table):
    rows = value.shape[0]
    result = matmul(jnp.concatenate(split(value), axis=0), table, NN)
    return result[:rows] + result[rows:]


def operator_kernel(first, grad_scale, proj, edge, taps_ref, phase_ref, table):
    chans, positions = proj[0].shape
    streams = len(proj)
    taps_len = (taps_ref.shape[1] - 1) // streams
    own = slice(first, first + chans)

    def tap(stream, pos):
        column = stream * taps_len + pos
        return taps_ref[own, column : column + 1]

    filtered = []
    for stream, total in enumerate(proj):
        acc = tap(stream, 0) * total
        for pos in range(1, taps_len):
            acc = acc + tap(stream, pos) * delayed(total, pos)
        filtered.append(acc)
    query, key, value = filtered
    skip = taps_ref[own, streams * taps_len : streams * taps_len + 1]
    half = edge.shape[0] // 2
    cot = edge[first : first + chans].astype(F32)
    long_filter = edge[half + first : half + first + chans].astype(F32)
    gated = key * value
    d_conv = cot * query
    stacked = jnp.concatenate([gated, long_filter, d_conv], axis=0)
    table_ref = table()
    cos_all = transform(stacked, table_ref[0])
    sin_all = transform(stacked, table_ref[1])
    g_cos, h_cos, d_cos = (cos_all[i * chans : (i + 1) * chans] for i in range(3))
    g_sin, h_sin, d_sin = (sin_all[i * chans : (i + 1) * chans] for i in range(3))
    cos_phase = phase_ref[0:1]
    sin_phase = phase_ref[1:2]
    h_real = h_cos * cos_phase + h_sin * sin_phase
    h_imag = h_cos * sin_phase - h_sin * cos_phase
    conv_real = g_cos * h_real + g_sin * h_imag
    conv_imag = g_cos * h_imag - g_sin * h_real
    back_real = h_real * d_cos - h_imag * d_sin
    back_imag = -(h_real * d_sin + h_imag * d_cos)
    corr_real = g_cos * d_cos + g_sin * d_sin
    corr_imag = g_sin * d_cos - g_cos * d_sin
    lag_real = corr_real * cos_phase + corr_imag * sin_phase
    lag_imag = corr_imag * cos_phase - corr_real * sin_phase
    real_all = jnp.concatenate([conv_real, back_real, lag_real], axis=0)
    imag_all = jnp.concatenate([conv_imag, back_imag, lag_imag], axis=0)
    result = transform(real_all, table_ref[0]) - transform(imag_all, table_ref[1])
    scale = 1.0 / positions
    conv_out = result[:chans] * scale + skip * gated
    d_gated = result[chans : 2 * chans] * scale + skip * d_conv
    filter_part = (result[2 * chans :] * (scale * grad_scale)).astype(BF)
    hyena_out = (query * conv_out).astype(BF)
    grads = []
    for stream, grad in enumerate((cot * conv_out, d_gated * value, d_gated * key)):
        acc = tap(stream, 0) * grad
        for pos in range(1, taps_len):
            acc = acc + tap(stream, pos) * advanced(grad, pos)
        grads.append(acc.astype(BF))
    return grads, hyena_out, filter_part


def summed(parts_ref, row, count):
    total = parts_ref[0, row : row + count].astype(F32)
    for source in range(1, parts_ref.shape[0]):
        total = total + parts_ref[source, row : row + count].astype(F32)
    return total


def load_table(table_ref, held_ref, sem):
    copy = pltpu.make_async_copy(table_ref, held_ref, sem)
    copy.start()

    def ready():
        copy.wait()
        return held_ref

    return ready


def operator_first_kernel(
    group, grad_scale, parts_ref, taps_ref, phase_ref, table_ref, grads_ref, out_ref, edge_ref, held_ref, sem
):
    table = load_table(table_ref, held_ref, sem)
    chans = group[1] - group[0]
    streams = grads_ref.shape[0] // chans
    sources, rows, positions = parts_ref.shape
    edge = jnp.concatenate(
        [
            unfold(parts_ref[source, streams * chans :], positions // sources)
            for source in range(sources)
        ],
        axis=1,
    )
    edge_ref[...] = edge
    proj = [summed(parts_ref, stream * chans, chans) for stream in range(streams)]
    grads, hyena_out, filter_part = operator_kernel(
        group[0], grad_scale, proj, edge, taps_ref, phase_ref, table
    )
    for stream, grad in enumerate(grads):
        grads_ref[stream * chans : (stream + 1) * chans] = grad
    out_ref[:chans] = hyena_out
    out_ref[chans:] = filter_part


def operator_first(group, parts, taps, phase, table, grad_scale, streams):
    sources, rows, positions = parts.shape
    chans = group[1] - group[0]
    full = pl.BlockSpec(memory_space=pltpu.VMEM)
    return pl.pallas_call(
        functools.partial(operator_first_kernel, group, grad_scale),
        in_specs=[full, full, full, pl.BlockSpec(memory_space=pl.ANY)],
        out_shape=(
            kept((streams * chans, positions)),
            jax.ShapeDtypeStruct((2 * chans, positions), BF),
            jax.ShapeDtypeStruct((2 * taps.shape[0], positions), BF),
        ),
        scratch_shapes=[pltpu.VMEM(table.shape, BF), pltpu.SemaphoreType.DMA],
        compiler_params=params(),
        cost_estimate=cost(16 * streams * chans * positions * positions, 2 * (parts.size + table.size)),
        name="operator_first",
    )(parts, taps, phase, table)


def operator_last_kernel(
    group, grad_scale, parts_ref, taps_ref, phase_ref, table_ref, outs_ref, edge_ref, out_ref, held_ref, sem
):
    table = load_table(table_ref, held_ref, sem)
    sources, streams, chans, positions = parts_ref.shape
    proj = []
    for stream in range(streams):
        total = parts_ref[0, stream].astype(F32)
        for source in range(1, sources):
            total = total + parts_ref[source, stream].astype(F32)
        proj.append(total)
    grads, hyena_out, filter_part = operator_kernel(
        group[0], grad_scale, proj, edge_ref[...], taps_ref, phase_ref, table
    )
    before = outs_ref.shape[0] // 2
    columns = jnp.concatenate([outs_ref[:before], hyena_out, outs_ref[before:], filter_part], axis=0)
    devices = out_ref.shape[0]
    block_len = positions // sources
    for device in range(devices):
        for stream, grad in enumerate(grads):
            out_ref[device, stream * chans : (stream + 1) * chans] = grad
        lane = device // (devices // sources) * block_len
        fold(out_ref.at[device], streams * chans, columns[:, lane : lane + block_len])


def operator_last(group, parts, taps, phase, table, outs, edge, grad_scale, devices):
    sources, streams, chans, positions = parts.shape
    full = pl.BlockSpec(memory_space=pltpu.VMEM)
    rows = streams * chans + 2 * taps.shape[0] // sources
    return pl.pallas_call(
        functools.partial(operator_last_kernel, group, grad_scale),
        in_specs=[full, full, full, pl.BlockSpec(memory_space=pl.ANY), full, full],
        out_shape=kept((devices, rows, positions)),
        scratch_shapes=[pltpu.VMEM(table.shape, BF), pltpu.SemaphoreType.DMA],
        compiler_params=params(),
        cost_estimate=cost(16 * streams * chans * positions * positions, 2 * (parts.size + table.size)),
        name="operator_last",
    )(parts, taps, phase, table, outs, edge)


def token_kernel(pos_ref, *refs):
    sent_ref, held_ref = refs[-2:]
    positions = sent_ref.shape[1]
    total = None
    for weight_ref, grads_ref in zip(refs[0:-2:2], refs[1:-2:2]):
        streams, chips, _, rows, cols = weight_ref.shape
        for stream in range(streams):
            weight = weight_ref[stream, :, 0].reshape(chips * rows, cols)
            part = matmul(weight, grads_ref[:, 0, stream].reshape(cols, positions), NN)
            total = part if total is None else total + part
    total = total.astype(BF)

    @pl.when(pl.program_id(0) == 0)
    def _():
        sent_ref[...] = total

    @pl.when(pl.program_id(0) == 1)
    def _():
        held_ref[...] = total


def token_part(pos, weights, grads, chan_count):
    operands, specs = [], []
    flops = 0
    for weight, grad in zip(weights, grads):
        streams, slab_rows, cols = weight.shape
        slabs, _, _, chans, positions = grad.shape
        rows = slab_rows // chan_count
        operands += [weight.reshape(streams, chan_count // 2, 2, rows, cols), grad]
        specs += [
            pl.BlockSpec(
                (streams, chan_count // 2, 1, rows, cols),
                lambda j, pos: (0, 0, jnp.where(j == 0, 1 - pos[1], pos[1]), 0, 0),
            ),
            pl.BlockSpec((slabs, 1, streams, chans, positions), lambda j, pos: (0, pos[0], 0, 0, 0)),
        ]
        flops += 2 * weight.size * positions
    return pl.pallas_call(
        token_kernel,
        grid_spec=pltpu.PrefetchScalarGridSpec(
            num_scalar_prefetch=1,
            grid=(2,),
            in_specs=specs,
            out_specs=[pl.BlockSpec((slab_rows // 2, positions), lambda j, pos: (0, 0))] * 2,
        ),
        out_shape=(kept((slab_rows // 2, positions)), kept((slab_rows // 2, positions))),
        compiler_params=params(),
        cost_estimate=cost(flops, 8 * slab_rows * positions),
        name="token_part",
    )(pos, *operands)


def weight_kernel(grad_scale, pos_ref, own_ref, other_ref, *refs):
    out_ref, rows_ref = refs[-2:]
    slabs = refs[0].shape[0]
    chans = out_ref.shape[2] // slabs
    total = None
    for batch, tokens_ref in enumerate((own_ref, other_ref)):
        first = 0
        for grads_ref in refs[batch:-2:2]:
            count = grads_ref.shape[3]
            for slab in range(slabs):
                base = slab * chans + first
                rows_ref[batch, base : base + count] = grads_ref[slab, 0, 0]
            first += count
        part = matmul(tokens_ref[...], rows_ref[batch], NT)
        total = part if total is None else total + part
    out_ref[0] = (total * grad_scale).astype(BF)


def weight_grad(pos, own, other, grads, grad_scale, streams):
    slabs, _, _, _, positions = grads[0].shape
    slab_rows = own.shape[0]
    chan_cols = slabs * sum(grad.shape[3] for grad in grads)
    operands, specs = [], []
    for grad in grads:
        block = (slabs, 1, 1, grad.shape[3], positions)
        operands += [grad, grad]
        specs += [
            pl.BlockSpec(block, lambda i, pos: (0, pos[0], i, 0, 0)),
            pl.BlockSpec(block, lambda i, pos: (0, 1 - pos[0], i, 0, 0)),
        ]
    return pl.pallas_call(
        functools.partial(weight_kernel, grad_scale),
        grid_spec=pltpu.PrefetchScalarGridSpec(
            num_scalar_prefetch=1,
            grid=(streams,),
            in_specs=[
                pl.BlockSpec(own.shape, lambda i, pos: (0, 0)),
                pl.BlockSpec(own.shape, lambda i, pos: (0, 0)),
                *specs,
            ],
            out_specs=pl.BlockSpec((1, slab_rows, chan_cols), lambda i, pos: (i, 0, 0)),
            scratch_shapes=[pltpu.VMEM((2, chan_cols, positions), BF)],
        ),
        out_shape=jax.ShapeDtypeStruct((streams, slab_rows, chan_cols), BF),
        compiler_params=params(),
        cost_estimate=cost(
            4 * streams * slab_rows * chan_cols * positions,
            2 * (2 * own.size + 2 * streams * chan_cols * positions + streams * slab_rows * chan_cols),
        ),
        name="weight_grad",
    )(pos, own, other, *operands)


def total_kernel(parts_ref, out_ref):
    total = parts_ref[0].astype(F32)
    for pos in range(1, parts_ref.shape[0]):
        total = total + parts_ref[pos].astype(F32)
    out_ref[0] = jnp.transpose(total).astype(BF)


def token_total(parts):
    _, rows, positions = parts.shape
    return pl.pallas_call(
        total_kernel,
        out_shape=jax.ShapeDtypeStruct((1, positions, rows), BF),
        compiler_params=params(24 << 20),
        cost_estimate=cost(0, 2 * parts.size),
        name="token_total",
    )(parts)


def finish_kernel(block_len, pos_ref, own_ref, other_ref, out_ref, filter_ref):
    slabs = own_ref.shape[0]
    hyena, filters = [], []
    for slab in range(slabs):
        own = unfold(own_ref[slab, 0, 0], block_len)
        other = unfold(other_ref[slab, 0, 0], block_len)
        chans = own.shape[0] // 2
        hyena.append(own[:chans].astype(F32))
        filters.append(own[chans:].astype(F32) + other[chans:].astype(F32))
    out_ref[0] = jnp.transpose(jnp.concatenate(hyena, axis=0)).astype(BF)
    filter_ref[...] = jnp.transpose(jnp.concatenate(filters, axis=0))


def finish(pos, received, chan_cols):
    slabs, batches, parts, rows, positions = received.shape
    block_len = positions // slabs
    block = (slabs, 1, 1, rows, positions)
    return pl.pallas_call(
        functools.partial(finish_kernel, block_len),
        grid_spec=pltpu.PrefetchScalarGridSpec(
            num_scalar_prefetch=1,
            grid=(1,),
            in_specs=[
                pl.BlockSpec(block, lambda i, pos: (0, pos[0], parts - 1, 0, 0)),
                pl.BlockSpec(block, lambda i, pos: (0, 1 - pos[0], parts - 1, 0, 0)),
            ],
            out_specs=[
                pl.BlockSpec((1, block_len, chan_cols), lambda i, pos: (0, 0, 0)),
                pl.BlockSpec((block_len, chan_cols), lambda i, pos: (0, 0)),
            ],
        ),
        out_shape=(
            jax.ShapeDtypeStruct((1, block_len, chan_cols), BF),
            jax.ShapeDtypeStruct((block_len, chan_cols), F32),
        ),
        compiler_params=params(),
        cost_estimate=cost(0, 8 * slabs * rows * positions),
        name="finish",
    )(pos, received, received)


def exchange(value, axis, groups=None):
    return lax.all_to_all(
        value, axis, split_axis=0, concat_axis=0, tiled=True, axis_index_groups=groups
    )


def local(tokens, in_weight, short_taps, long_filter, skip_gain, cotangent):
    seq_count = lax.axis_size("seq")
    seq_pos = lax.axis_index("seq")
    dp_count = lax.axis_size("dp")
    chan_count = lax.axis_size("chan")
    chan_pos = lax.axis_index("chan").astype(jnp.int32)
    core = chan_pos % 2
    pos = jnp.stack([lax.axis_index("dp").astype(jnp.int32), core])
    tok_rows = tokens.shape[1]
    slab_rows = in_weight.shape[0]
    chan_cols = in_weight.shape[2]
    streams, taps_len = short_taps.shape[:2]
    positions = seq_count * tok_rows
    chans = chan_cols // seq_count
    half = tok_rows // 2
    share = tok_rows // chan_count
    chips = chan_count // 2
    grad_scale = 1.0 / math.sqrt(dp_count * positions)
    groups = ((0, chans * 3 // 4), (chans * 3 // 4, chans))
    cores = [(i, i ^ 1) for i in range(chan_count)]
    batches = [(0, 1), (1, 0)]
    weight = jnp.transpose(in_weight, (1, 0, 2))

    mine = lax.dynamic_slice_in_dim(tokens[0], core * half, half, 0)
    mine = jnp.transpose(mine.reshape(half, seq_count, slab_rows), (1, 0, 2))
    taps = jnp.concatenate([short_taps.reshape(streams * taps_len, chan_cols), skip_gain[None]])
    taps = jnp.transpose(lax.dynamic_slice_in_dim(taps, seq_pos * chans, chans, 1))
    odd = 2 * jnp.arange(positions, dtype=jnp.int32) + 1
    phase = jnp.stack(angle(odd, 8 * positions))
    mine, edge, arranged, table, taps, phase = lax.optimization_barrier(
        (
            exchange(mine, "seq"),
            edge_rows(cotangent, long_filter, seq_count),
            arrange_weight(weight, groups),
            tables(positions),
            taps,
            phase,
        )
    )
    flipped_a, weight_a, flipped_b, weight_b = arranged
    theirs = lax.ppermute(mine, "chan", cores)
    parts_a, spread = project_first(core[None], mine, theirs, flipped_a, edge)
    shares = lax.dynamic_slice_in_dim(mine, chan_pos // 2 * share, share, 1)
    shares = lax.ppermute(shares, "dp", batches)
    parts_a, shares = lax.optimization_barrier((parts_a, shares))
    shares = lax.all_gather(shares, "chan", axis=0)
    shares = shares.reshape(chips, 2, seq_count, share, slab_rows)
    parts_a, parts_b = lax.optimization_barrier(
        (exchange(parts_a, "seq"), project_rest(spread, flipped_b, seq_count))
    )
    parts_b = exchange(parts_b, "seq")

    grads_a, outs, edge = operator_first(groups[0], parts_a, taps, phase, table, grad_scale, streams)
    grads_a, shares = lax.optimization_barrier((grads_a, shares))
    grads_a = lax.all_gather(grads_a, ("seq", "dp"), axis=0)
    grads_b = operator_last(
        groups[1], parts_b, taps, phase, table, outs, edge, grad_scale, seq_count * dp_count
    )
    grads_b = exchange(grads_b, ("seq", "dp"))
    grads_a = grads_a.reshape(seq_count, dp_count, streams, -1, positions)
    grads_b = grads_b.reshape(seq_count, dp_count, streams + 1, -1, positions)
    finished = finish(pos, grads_b, chan_cols)
    own, other = turn_tokens(spread), turn_shares(shares)
    grads_a, finished, own, other = lax.optimization_barrier((grads_a, finished, own, other))
    hyena_out, grad_filter = finished

    grads = (grads_a, grads_b)
    sent, held = token_part(pos, (weight_a, weight_b), grads, chan_count)
    received = lax.ppermute(sent, "chan", cores)
    token_block = (held.astype(F32) + received.astype(F32)).astype(BF)
    token_block = exchange(
        token_block.reshape(chips, -1, positions),
        "chan",
        [[chip * 2 + side for chip in range(chips)] for side in range(2)],
    )
    grad_tokens = token_total(token_block)
    grad_weight = weight_grad(pos, own, other, grads, grad_scale, streams)
    return (hyena_out, grad_tokens, jnp.transpose(grad_weight, (1, 0, 2)), grad_filter)


def solution(mesh):
    placed = (
        P("dp", "seq", None),
        P("seq", None, "chan"),
        P(None, None, "chan"),
        P("seq", "chan"),
        P("chan"),
        P("dp", "seq", "chan"),
    )
    return jax.shard_map(
        local,
        mesh=mesh,
        in_specs=placed,
        out_specs=(
            P("dp", "seq", "chan"),
            P("dp", None, ("seq", "chan")),
            P("seq", None, "chan"),
            P("seq", "chan"),
        ),
        check_vma=False,
    )
```

```python
import functools
import math

import jax
import jax.numpy as jnp
from jax import lax
from jax.experimental import pallas as pl
from jax.experimental.pallas import tpu as pltpu
from jax.sharding import PartitionSpec as P

BF = jnp.bfloat16
F32 = jnp.float32
VMEM_BYTES = 60 << 20
NT = (((1,), (1,)), ((), ()))
NN = (((1,), (0,)), ((), ()))


def params(limit=VMEM_BYTES):
    return pltpu.CompilerParams(vmem_limit_bytes=limit)


def cost(flops, bytes_accessed):
    return pl.CostEstimate(flops=flops, bytes_accessed=bytes_accessed, transcendentals=0)


def kept(shape, dtype=BF):
    return pltpu.HBM(shape, dtype)


def matmul(left, right, dims):
    return lax.dot_general(left, right, dims, preferred_element_type=F32)


def split(value):
    high = value.astype(BF)
    return high, (value - high.astype(F32)).astype(BF)


def edge_kernel(pos_ref, cot_ref, filter_ref, out_ref):
    slabs = out_ref.shape[0]
    chans = filter_ref.shape[1] // slabs
    high, low = split(jnp.transpose(filter_ref[...]))
    taps = jnp.where(pos_ref[0] == 0, high.astype(F32), low.astype(F32)).astype(BF)
    cot = jnp.transpose(cot_ref[0].astype(F32)).astype(BF)
    for slab in range(slabs):
        part = slice(slab * chans, (slab + 1) * chans)
        fold(out_ref.at[slab], 0, jnp.concatenate([cot[part], taps[part]], axis=0))


def fold(out_ref, first, value):
    rows, block_len = value.shape
    count = rows * block_len // out_ref.shape[1]
    for pos in range(rows // count):
        out_ref[first : first + count, pos * block_len : (pos + 1) * block_len] = value[
            pos * count : (pos + 1) * count
        ]


def unfold(value, block_len):
    return jnp.concatenate(
        [value[:, at : at + block_len] for at in range(0, value.shape[1], block_len)], axis=0
    )


def edge_rows(pos, cotangent, long_filter, slabs, lanes):
    _, tok_rows, chan_cols = cotangent.shape
    full = pl.BlockSpec(memory_space=pltpu.VMEM)
    return pl.pallas_call(
        edge_kernel,
        in_specs=[pl.BlockSpec(memory_space=pltpu.SMEM), full, full],
        out_shape=kept((slabs, 2 * tok_rows * chan_cols // slabs // lanes, lanes)),
        compiler_params=params(),
        cost_estimate=cost(0, 8 * tok_rows * chan_cols),
        name="edge_rows",
    )(pos, cotangent, long_filter)


def flip_kernel(weight_ref, out_ref):
    out_ref[0] = jnp.transpose(weight_ref[0])


def flip_weight(weight):
    streams, slab_rows, chan_cols = weight.shape
    half = chan_cols // 2
    return pl.pallas_call(
        flip_kernel,
        grid=(streams, 2),
        in_specs=[pl.BlockSpec((1, slab_rows, half), lambda i, j: (i, 0, j))],
        out_specs=pl.BlockSpec((1, half, slab_rows), lambda i, j: (i, j, 0)),
        out_shape=kept((streams, chan_cols, slab_rows)),
        compiler_params=params(),
        cost_estimate=cost(0, 4 * weight.size),
        name="flip_weight",
    )(weight)


def table_kernel(cos_a_ref, sin_a_ref, cos_b_ref, sin_b_ref, out_ref):
    cos_a = cos_a_ref[0]
    sin_a = sin_a_ref[0]
    cos_b = cos_b_ref[...]
    sin_b = sin_b_ref[...]
    out_ref[0] = (cos_a * cos_b - sin_a * sin_b).astype(BF)
    out_ref[1] = (sin_a * cos_b + cos_a * sin_b).astype(BF)


def angle(product, period):
    phases = 2.0 * math.pi / period * (product % period).astype(F32)
    return jnp.cos(phases), jnp.sin(phases)


def tables(odd):
    steps = 64
    count = odd.shape[1]
    period = 8 * count
    base = jnp.arange(count // steps, dtype=jnp.int32)[:, None] * (2 * steps)
    fine = 2 * jnp.arange(steps, dtype=jnp.int32)[:, None] + 1
    cos_a, sin_a = angle(base * odd, period)
    cos_b, sin_b = angle(fine * odd, period)
    return pl.pallas_call(
        table_kernel,
        grid=(count // steps,),
        in_specs=[
            pl.BlockSpec((1, 1, count), lambda i: (i, 0, 0)),
            pl.BlockSpec((1, 1, count), lambda i: (i, 0, 0)),
            pl.BlockSpec((steps, count), lambda i: (0, 0)),
            pl.BlockSpec((steps, count), lambda i: (0, 0)),
        ],
        out_specs=pl.BlockSpec((2, steps, count), lambda i: (0, i, 0)),
        out_shape=jax.ShapeDtypeStruct((2, count, count), BF),
        compiler_params=params(),
        cost_estimate=cost(0, 4 * count * count),
        name="tables",
    )(cos_a[:, None], sin_a[:, None], cos_b, sin_b)


def project_kernel(core_ref, mine_ref, theirs_ref, weight_ref, edge_ref, out_ref, spread_ref):
    blocks, half, _ = mine_ref.shape
    core = core_ref[0]
    step = pl.program_id(0)

    @pl.when(step == 0)
    def _():
        for block in range(blocks):
            base = 2 * block * half
            spread_ref[pl.ds(pl.multiple_of(base + core * half, half), half)] = mine_ref[block]
            spread_ref[pl.ds(pl.multiple_of(base + (1 - core) * half, half), half)] = theirs_ref[block]
        out_ref[:, out_ref.shape[1] - edge_ref.shape[1] :] = edge_ref[...]

    slabs, _, positions = out_ref.shape
    chans = weight_ref.shape[1] // slabs
    result = matmul(weight_ref[0], spread_ref[...], NT).astype(BF).reshape(slabs, chans, positions)
    out_ref[:, pl.ds(pl.multiple_of(step * chans, chans), chans)] = result


def project(core, mine, theirs, weight, edge):
    blocks, half, width = mine.shape
    streams, rows, _ = weight.shape
    slabs, edge_len, positions = edge.shape
    out_dims = (slabs, streams * rows // slabs + edge_len, positions)
    return pl.pallas_call(
        project_kernel,
        grid_spec=pltpu.PrefetchScalarGridSpec(
            num_scalar_prefetch=1,
            grid=(streams,),
            in_specs=[
                pl.BlockSpec(mine.shape, lambda i, core: (0, 0, 0)),
                pl.BlockSpec(mine.shape, lambda i, core: (0, 0, 0)),
                pl.BlockSpec((1, rows, width), lambda i, core: (i, 0, 0)),
                pl.BlockSpec(edge.shape, lambda i, core: (0, 0, 0)),
            ],
            out_specs=[
                pl.BlockSpec(out_dims, lambda i, core: (0, 0, 0)),
                pl.BlockSpec((positions, width), lambda i, core: (0, 0)),
            ],
        ),
        out_shape=(kept(out_dims), kept((positions, width))),
        compiler_params=params(),
        cost_estimate=cost(
            2 * positions * width * streams * rows,
            2 * (2 * positions * width + weight.size + positions * streams * rows),
        ),
        name="project",
    )(core, mine, theirs, weight, edge)


def turn_kernel(tokens_ref, out_ref):
    out_ref[...] = jnp.transpose(tokens_ref[...])


def turn_tokens(tokens):
    positions, width = tokens.shape
    part = width // 4
    return pl.pallas_call(
        turn_kernel,
        grid=(4,),
        in_specs=[pl.BlockSpec((positions, part), lambda i: (0, i))],
        out_specs=pl.BlockSpec((part, positions), lambda i: (i, 0)),
        out_shape=kept((width, positions)),
        compiler_params=params(),
        cost_estimate=cost(0, 4 * tokens.size),
        name="turn_tokens",
    )(tokens)


def turn_shares_kernel(tokens_ref, out_ref, spread_ref):
    chips, cores, blocks, rows, _ = tokens_ref.shape
    for block in range(blocks):
        for core in range(cores):
            for chip in range(chips):
                base = ((block * cores + core) * chips + chip) * rows
                spread_ref[base : base + rows] = tokens_ref[chip, core, block]
    out_ref[...] = jnp.transpose(spread_ref[...])


def turn_shares(tokens):
    chips, cores, blocks, rows, width = tokens.shape
    positions = chips * cores * blocks * rows
    part = width // 4
    return pl.pallas_call(
        turn_shares_kernel,
        grid=(4,),
        in_specs=[pl.BlockSpec((chips, cores, blocks, rows, part), lambda i: (0, 0, 0, 0, i))],
        out_specs=pl.BlockSpec((part, positions), lambda i: (i, 0)),
        out_shape=kept((width, positions)),
        scratch_shapes=[pltpu.VMEM((positions, part), BF)],
        compiler_params=params(),
        cost_estimate=cost(0, 4 * tokens.size),
        name="turn_shares",
    )(tokens)


def delayed(value, steps):
    if steps == 0:
        return value
    lane = lax.broadcasted_iota(jnp.int32, value.shape, 1)
    return jnp.where(lane < steps, 0.0, pltpu.roll(value, steps, 1))


def advanced(value, steps):
    if steps == 0:
        return value
    lanes = value.shape[1]
    lane = lax.broadcasted_iota(jnp.int32, value.shape, 1)
    return jnp.where(lane >= lanes - steps, 0.0, pltpu.roll(value, lanes - steps, 1))


def transform(value, table):
    rows = value.shape[0]
    result = matmul(jnp.concatenate(split(value), axis=0), table, NN)
    return result[:rows] + result[rows:]


def operator_kernel(grad_scale, parts_ref, taps_ref, phase_ref, table_ref, grads_ref, out_ref, held_ref, sem):
    copy = pltpu.make_async_copy(table_ref, held_ref, sem)
    copy.start()
    devices, _, positions = parts_ref.shape
    block_len = out_ref.shape[2]
    batches = 2
    chans = taps_ref.shape[0]
    streams = grads_ref.shape[0] // (batches * chans)
    taps_len = (taps_ref.shape[1] - 1) // streams
    sources = devices // batches
    all_taps = jnp.concatenate([taps_ref[...]] * batches, axis=0)

    def tap(stream, pos):
        column = stream * taps_len + pos
        return all_taps[:, column : column + 1]

    def summed(batch, row):
        total = parts_ref[batch, row : row + chans].astype(F32)
        for source in range(1, sources):
            total = total + parts_ref[source * batches + batch, row : row + chans].astype(F32)
        return total

    def edge(batch):
        return jnp.concatenate(
            [
                unfold(parts_ref[source * batches + batch, streams * chans :], block_len).astype(F32)
                for source in range(sources)
            ],
            axis=1,
        )

    filtered = []
    for stream in range(streams):
        total = jnp.concatenate([summed(batch, stream * chans) for batch in range(batches)], axis=0)
        acc = tap(stream, 0) * total
        for pos in range(1, taps_len):
            acc = acc + tap(stream, pos) * delayed(total, pos)
        filtered.append(acc)
    query, key, value = filtered
    skip = all_taps[:, streams * taps_len : streams * taps_len + 1]
    edges = [edge(batch) for batch in range(batches)]
    cot = jnp.concatenate([rows[:chans] for rows in edges], axis=0)
    long_filter = edges[0][chans:] + edges[1][chans:]
    gated = key * value
    d_conv = cot * query
    stacked = jnp.concatenate([gated, d_conv, long_filter], axis=0)
    copy.wait()
    cos_all = transform(stacked, held_ref[0])
    sin_all = transform(stacked, held_ref[1])
    rows = batches * chans
    g_cos, d_cos, h_cos = cos_all[:rows], cos_all[rows : 2 * rows], cos_all[2 * rows :]
    g_sin, d_sin, h_sin = sin_all[:rows], sin_all[rows : 2 * rows], sin_all[2 * rows :]
    cos_phase = phase_ref[0:1]
    sin_phase = phase_ref[1:2]
    h_real = jnp.concatenate([h_cos * cos_phase + h_sin * sin_phase] * batches, axis=0)
    h_imag = jnp.concatenate([h_cos * sin_phase - h_sin * cos_phase] * batches, axis=0)
    conv_real = g_cos * h_real + g_sin * h_imag
    conv_imag = g_cos * h_imag - g_sin * h_real
    back_real = h_real * d_cos - h_imag * d_sin
    back_imag = -(h_real * d_sin + h_imag * d_cos)
    corr_real = g_cos * d_cos + g_sin * d_sin
    corr_imag = g_sin * d_cos - g_cos * d_sin
    corr_real = corr_real[:chans] + corr_real[chans:]
    corr_imag = corr_imag[:chans] + corr_imag[chans:]
    lag_real = corr_real * cos_phase + corr_imag * sin_phase
    lag_imag = corr_imag * cos_phase - corr_real * sin_phase
    real_all = jnp.concatenate([conv_real, back_real, lag_real], axis=0)
    imag_all = jnp.concatenate([conv_imag, back_imag, lag_imag], axis=0)
    result = transform(real_all, held_ref[0]) - transform(imag_all, held_ref[1])
    scale = 1.0 / positions
    conv_out = result[:rows] * scale + skip * gated
    d_gated = result[rows : 2 * rows] * scale + skip * d_conv
    filter_part = (result[2 * rows :] * (scale * grad_scale)).astype(BF)
    hyena_out = (query * conv_out).astype(BF)
    for device in range(devices):
        batch = device % batches
        lanes = slice(device // batches * block_len, (device // batches + 1) * block_len)
        out_ref[device, :chans] = hyena_out[batch * chans : (batch + 1) * chans, lanes]
        out_ref[device, chans:] = filter_part[:, lanes]
    for stream, grad in enumerate((cot * conv_out, d_gated * value, d_gated * key)):
        acc = tap(stream, 0) * grad
        for pos in range(1, taps_len):
            acc = acc + tap(stream, pos) * advanced(grad, pos)
        acc = acc.astype(BF)
        for batch in range(batches):
            row = (batch * streams + stream) * chans
            grads_ref[row : row + chans] = acc[batch * chans : (batch + 1) * chans]


def operator(parts, taps, phase, table, grad_scale, streams, block_len):
    devices, _, positions = parts.shape
    chans = taps.shape[0]
    rows = devices * block_len // positions * streams * chans
    full = pl.BlockSpec(memory_space=pltpu.VMEM)
    return pl.pallas_call(
        functools.partial(operator_kernel, grad_scale),
        in_specs=[full, full, full, pl.BlockSpec(memory_space=pl.ANY)],
        out_shape=(kept((rows, positions)), kept((devices, 2 * chans, block_len))),
        scratch_shapes=[pltpu.VMEM(table.shape, BF), pltpu.SemaphoreType.DMA],
        compiler_params=params(),
        cost_estimate=cost(8 * rows * positions * positions, 2 * (parts.size + table.size)),
        name="operator",
    )(parts, taps, phase, table)


def token_kernel(pos_ref, weight_ref, grads_ref, sent_ref, held_ref):
    streams, chips, _, rows, cols = weight_ref.shape
    positions = sent_ref.shape[1]
    weight = jnp.concatenate(
        [weight_ref[stream, :, 0].reshape(chips * rows, cols) for stream in range(streams)], axis=1
    )
    grads = jnp.concatenate(
        [grads_ref[:, 0, stream].reshape(cols, positions) for stream in range(streams)], axis=0
    )
    total = matmul(weight, grads, NN).astype(BF)

    @pl.when(pl.program_id(0) == 0)
    def _():
        sent_ref[...] = total

    @pl.when(pl.program_id(0) == 1)
    def _():
        held_ref[...] = total


def token_part(pos, weight, grads, chan_count):
    streams, slab_rows, cols = weight.shape
    slabs, _, _, chans, positions = grads.shape
    rows = slab_rows // chan_count
    return pl.pallas_call(
        token_kernel,
        grid_spec=pltpu.PrefetchScalarGridSpec(
            num_scalar_prefetch=1,
            grid=(2,),
            in_specs=[
                pl.BlockSpec(
                    (streams, chan_count // 2, 1, rows, cols),
                    lambda j, pos: (0, 0, jnp.where(j == 0, 1 - pos[1], pos[1]), 0, 0),
                ),
                pl.BlockSpec((slabs, 1, streams, chans, positions), lambda j, pos: (0, pos[0], 0, 0, 0)),
            ],
            out_specs=[pl.BlockSpec((slab_rows // 2, positions), lambda j, pos: (0, 0))] * 2,
        ),
        out_shape=(kept((slab_rows // 2, positions)), kept((slab_rows // 2, positions))),
        compiler_params=params(),
        cost_estimate=cost(2 * weight.size * positions, 8 * slab_rows * positions),
        name="token_part",
    )(pos, weight.reshape(streams, chan_count // 2, 2, rows, cols), grads)


def pair_kernel(held_ref, received_ref, out_ref):
    out_ref[...] = (held_ref[...].astype(F32) + received_ref[...].astype(F32)).astype(BF)


def pair_sum(held, received):
    rows, positions = held.shape
    block = pl.BlockSpec((rows // 4, positions), lambda i: (i, 0))
    return pl.pallas_call(
        pair_kernel,
        grid=(4,),
        in_specs=[block, block],
        out_specs=block,
        out_shape=kept((rows, positions)),
        compiler_params=params(24 << 20),
        cost_estimate=cost(0, 6 * held.size),
        name="pair_sum",
    )(held, received)


def weight_kernel(grad_scale, pos_ref, own_ref, other_ref, own_grads_ref, other_grads_ref, out_ref):
    chan_cols = out_ref.shape[2]
    positions = own_ref.shape[1]
    own = own_grads_ref[...].reshape(chan_cols, positions)
    other = other_grads_ref[...].reshape(chan_cols, positions)
    total = matmul(own_ref[...], own, NT) + matmul(other_ref[...], other, NT)
    out_ref[0] = (total * grad_scale).astype(BF)


def weight_grad(pos, own, other, grads, grad_scale):
    slabs, _, streams, chans, positions = grads.shape
    slab_rows = own.shape[0]
    chan_cols = slabs * chans
    block = (slabs, 1, 1, chans, positions)
    return pl.pallas_call(
        functools.partial(weight_kernel, grad_scale),
        grid_spec=pltpu.PrefetchScalarGridSpec(
            num_scalar_prefetch=1,
            grid=(streams,),
            in_specs=[
                pl.BlockSpec(own.shape, lambda i, pos: (0, 0)),
                pl.BlockSpec(own.shape, lambda i, pos: (0, 0)),
                pl.BlockSpec(block, lambda i, pos: (0, pos[0], i, 0, 0)),
                pl.BlockSpec(block, lambda i, pos: (0, 1 - pos[0], i, 0, 0)),
            ],
            out_specs=pl.BlockSpec((1, slab_rows, chan_cols), lambda i, pos: (i, 0, 0)),
        ),
        out_shape=jax.ShapeDtypeStruct((streams, slab_rows, chan_cols), BF),
        compiler_params=params(),
        cost_estimate=cost(
            4 * streams * slab_rows * chan_cols * positions,
            2 * (2 * own.size + grads.size + streams * slab_rows * chan_cols),
        ),
        name="weight_grad",
    )(pos, own, other, grads, grads)


def total_kernel(parts_ref, out_ref):
    total = parts_ref[0].astype(F32)
    for pos in range(1, parts_ref.shape[0]):
        total = total + parts_ref[pos].astype(F32)
    out_ref[0] = jnp.transpose(total).astype(BF)


def token_total(parts):
    _, rows, positions = parts.shape
    return pl.pallas_call(
        total_kernel,
        out_shape=jax.ShapeDtypeStruct((1, positions, rows), BF),
        compiler_params=params(24 << 20),
        cost_estimate=cost(0, 2 * parts.size),
        name="token_total",
    )(parts)


def finish_kernel(parts_ref, out_ref, filter_ref):
    slabs, rows, block_len = parts_ref.shape
    chans = rows // 2
    hyena = parts_ref[:, :chans].astype(F32).reshape(slabs * chans, block_len)
    filters = parts_ref[:, chans:].astype(F32).reshape(slabs * chans, block_len)
    out_ref[0] = jnp.transpose(hyena).astype(BF)
    filter_ref[...] = jnp.transpose(filters)


def finish(parts):
    slabs, rows, block_len = parts.shape
    chan_cols = slabs * rows // 2
    return pl.pallas_call(
        finish_kernel,
        out_shape=(
            jax.ShapeDtypeStruct((1, block_len, chan_cols), BF),
            jax.ShapeDtypeStruct((block_len, chan_cols), F32),
        ),
        compiler_params=params(24 << 20),
        cost_estimate=cost(0, 4 * parts.size),
        name="finish",
    )(parts)


def exchange(value, axis, groups=None):
    return lax.all_to_all(
        value, axis, split_axis=0, concat_axis=0, tiled=True, axis_index_groups=groups
    )


def local(tokens, in_weight, short_taps, long_filter, skip_gain, cotangent):
    seq_count = lax.axis_size("seq")
    dp_count = lax.axis_size("dp")
    dp_pos = lax.axis_index("dp").astype(jnp.int32)
    slab_pos = lax.axis_index("seq").astype(jnp.int32) * dp_count + dp_pos
    chan_count = lax.axis_size("chan")
    chan_pos = lax.axis_index("chan").astype(jnp.int32)
    core = chan_pos % 2
    pos = jnp.stack([dp_pos, core])
    tok_rows = tokens.shape[1]
    slab_rows = in_weight.shape[0]
    chan_cols = in_weight.shape[2]
    streams, taps_len = short_taps.shape[:2]
    positions = seq_count * tok_rows
    slabs = seq_count * dp_count
    chans = chan_cols // slabs
    half = tok_rows // 2
    share = tok_rows // chan_count
    chips = chan_count // 2
    grad_scale = 1.0 / math.sqrt(dp_count * positions)
    cores = [(i, i ^ 1) for i in range(chan_count)]
    weight = jnp.transpose(in_weight, (1, 0, 2))

    mine = lax.dynamic_slice_in_dim(tokens[0], core * half, half, 0)
    mine = jnp.transpose(mine.reshape(half, seq_count, slab_rows), (1, 0, 2))
    mine, edge, flipped = lax.optimization_barrier(
        (
            exchange(mine, "seq"),
            edge_rows(pos, cotangent, long_filter, slabs, positions),
            flip_weight(weight),
        )
    )
    theirs = lax.ppermute(mine, "chan", cores)
    parts, spread = project(core[None], mine, theirs, flipped, edge)

    shares = lax.dynamic_slice_in_dim(mine, chan_pos // 2 * share, share, 1)
    shares = lax.ppermute(shares, "dp", [(0, 1), (1, 0)])
    odd = 2 * jnp.arange(positions, dtype=jnp.int32)[None] + 1
    parts, shares, odd, short_taps = lax.optimization_barrier((parts, shares, odd, short_taps))
    shares = lax.all_gather(shares, "chan", axis=0)
    shares = shares.reshape(chips, 2, seq_count, share, slab_rows)
    taps = jnp.concatenate([short_taps.reshape(streams * taps_len, chan_cols), skip_gain[None]])
    taps = jnp.transpose(lax.dynamic_slice_in_dim(taps, slab_pos * chans, chans, 1))
    parts, table, taps, phase, own = lax.optimization_barrier(
        (
            exchange(parts, ("seq", "dp")),
            tables(odd),
            taps,
            jnp.concatenate(angle(odd, 8 * positions)),
            turn_tokens(spread),
        )
    )

    grads, outs = operator(parts, taps, phase, table, grad_scale, streams, tok_rows)
    grads, shares = lax.optimization_barrier((grads, shares))
    grads = lax.all_gather(grads, ("seq", "dp"), axis=0)
    finished = finish(exchange(outs, ("seq", "dp")))
    grads, finished, other = lax.optimization_barrier((grads, finished, turn_shares(shares)))
    hyena_out, grad_filter = finished

    grads = grads.reshape(slabs, dp_count, streams, chans, positions)
    sent, held = token_part(pos, weight, grads, chan_count)
    token_block = pair_sum(held, lax.ppermute(sent, "chan", cores))
    token_block = exchange(
        token_block.reshape(chips, -1, positions),
        "chan",
        [[chip * 2 + side for chip in range(chips)] for side in range(2)],
    )
    grad_tokens = token_total(token_block)
    grad_weight = weight_grad(pos, own, other, grads, grad_scale)
    return (hyena_out, grad_tokens, jnp.transpose(grad_weight, (1, 0, 2)), grad_filter)


def solution(mesh):
    placed = (
        P("dp", "seq", None),
        P("seq", None, "chan"),
        P(None, None, "chan"),
        P("seq", "chan"),
        P("chan"),
        P("dp", "seq", "chan"),
    )
    return jax.shard_map(
        local,
        mesh=mesh,
        in_specs=placed,
        out_specs=(
            P("dp", "seq", "chan"),
            P("dp", None, ("seq", "chan")),
            P("seq", None, "chan"),
            P("seq", "chan"),
        ),
        check_vma=False,
    )
```

```python
import functools
import math

import jax
import jax.numpy as jnp
import numpy as np
from jax import lax
from jax.experimental import pallas as pl
from jax.experimental.pallas import tpu as pltpu
from jax.sharding import PartitionSpec as P

BF = jnp.bfloat16
F32 = jnp.float32
VMEM_BYTES = 60 << 20
NT = (((1,), (1,)), ((), ()))
NN = (((1,), (0,)), ((), ()))


def params(limit=VMEM_BYTES):
    return pltpu.CompilerParams(vmem_limit_bytes=limit)


def cost(flops, bytes_accessed):
    return pl.CostEstimate(flops=flops, bytes_accessed=bytes_accessed, transcendentals=0)


def kept(shape, dtype=BF):
    return pltpu.HBM(shape, dtype)


def stay(value):
    return pltpu.with_memory_space_constraint(value, pltpu.HBM)


def matmul(left, right, dims):
    return lax.dot_general(left, right, dims, preferred_element_type=F32)


def split(value):
    high = value.astype(BF)
    return high, (value - high.astype(F32)).astype(BF)


def edge_kernel(pos_ref, cot_ref, filter_ref, out_ref):
    slabs = out_ref.shape[0]
    chans = filter_ref.shape[1] // slabs
    high, low = split(jnp.transpose(filter_ref[...]))
    taps = jnp.where(pos_ref[0] == 0, high.astype(F32), low.astype(F32)).astype(BF)
    cot = jnp.transpose(cot_ref[0].astype(F32)).astype(BF)
    for slab in range(slabs):
        part = slice(slab * chans, (slab + 1) * chans)
        fold(out_ref.at[slab], 0, jnp.concatenate([cot[part], taps[part]], axis=0))


def fold(out_ref, first, value):
    rows, block_len = value.shape
    count = rows * block_len // out_ref.shape[1]
    for pos in range(rows // count):
        out_ref[first : first + count, pos * block_len : (pos + 1) * block_len] = value[
            pos * count : (pos + 1) * count
        ]


def unfold(value, block_len):
    return jnp.concatenate(
        [value[:, at : at + block_len] for at in range(0, value.shape[1], block_len)], axis=0
    )


def edge_rows(pos, cotangent, long_filter, slabs, lanes):
    _, tok_rows, chan_cols = cotangent.shape
    full = pl.BlockSpec(memory_space=pltpu.VMEM)
    return pl.pallas_call(
        edge_kernel,
        in_specs=[pl.BlockSpec(memory_space=pltpu.SMEM), full, full],
        out_shape=kept((slabs, 2 * tok_rows * chan_cols // slabs // lanes, lanes)),
        compiler_params=params(),
        cost_estimate=cost(0, 8 * tok_rows * chan_cols),
        name="edge_rows",
    )(pos, cotangent, long_filter)


def flip_kernel(weight_ref, out_ref):
    out_ref[0] = jnp.transpose(weight_ref[0])


def flip_weight(weight):
    streams, slab_rows, chan_cols = weight.shape
    half = chan_cols // 2
    return pl.pallas_call(
        flip_kernel,
        grid=(streams, 2),
        in_specs=[pl.BlockSpec((1, slab_rows, half), lambda i, j: (i, 0, j))],
        out_specs=pl.BlockSpec((1, half, slab_rows), lambda i, j: (i, j, 0)),
        out_shape=kept((streams, chan_cols, slab_rows)),
        compiler_params=params(),
        cost_estimate=cost(0, 4 * weight.size),
        name="flip_weight",
    )(weight)


BLOCKS = 4


def block_angle(residue, block):
    return math.pi * (2 * residue + 1) * block / (2 * BLOCKS)


def frequencies(count, residue):
    steps = 2 * BLOCKS * np.arange(count // (2 * BLOCKS))
    return steps + residue, steps + 2 * BLOCKS - 1 - residue


def transform_tables(count):
    width = count // BLOCKS
    tables, phases = [], []
    for residue in range(BLOCKS):
        columns, rows = [], []
        for side, freq in zip((1.0, -1.0), frequencies(count, residue)):
            angles = math.pi / (4 * count) * (2 * np.arange(width)[:, None] + 1) * (2 * freq[None] + 1)
            cos, sin = np.cos(angles), np.sin(angles)
            columns += [np.concatenate([cos, side * sin]), np.concatenate([-sin, side * cos])]
            rows.append(math.pi / (4 * count) * (2 * freq + 1))
        tables.append(np.concatenate(columns, axis=1))
        rows = np.concatenate(rows)
        phases += [np.cos(rows), np.sin(rows)]
    return jnp.asarray(np.stack(tables), BF), jnp.asarray(np.stack(phases), F32)


def cut_kernel(pos_ref, tokens_ref, out_ref, sems):
    slabs, half, width = out_ref.shape
    start = pl.multiple_of(pos_ref[1] * half, half)
    copies = [
        pltpu.make_async_copy(
            tokens_ref.at[0, pl.ds(start, half), slice(slab * width, (slab + 1) * width)],
            out_ref.at[slab],
            sems.at[slab],
        )
        for slab in range(slabs)
    ]
    for copy in copies:
        copy.start()
    for copy in copies:
        copy.wait()


def cut_tokens(pos, tokens, slabs):
    _, rows, width = tokens.shape
    return pl.pallas_call(
        cut_kernel,
        in_specs=[pl.BlockSpec(memory_space=pltpu.SMEM), pl.BlockSpec(memory_space=pl.ANY)],
        out_specs=pl.BlockSpec(memory_space=pl.ANY),
        out_shape=kept((slabs, rows // 2, width // slabs)),
        scratch_shapes=[pltpu.SemaphoreType.DMA((slabs,))],
        compiler_params=params(),
        cost_estimate=cost(0, 2 * tokens.size),
        name="cut_tokens",
    )(pos, tokens)


def in_order(core, mine_ref, theirs_ref, spread_ref):
    blocks, half, _ = mine_ref.shape
    for block in range(blocks):
        base = 2 * block * half
        spread_ref[pl.ds(pl.multiple_of(base + core * half, half), half)] = mine_ref[block]
        spread_ref[pl.ds(pl.multiple_of(base + (1 - core) * half, half), half)] = theirs_ref[block]


def project_kernel(pos_ref, mine_ref, theirs_ref, weight_ref, edge_ref, out_ref, spread_ref):
    step = pl.program_id(0)
    last = pl.num_programs(0) - 1

    @pl.when(step == 0)
    def _():
        in_order(pos_ref[1], mine_ref, theirs_ref, spread_ref)

    @pl.when(step < last)
    def _():
        result = matmul(weight_ref[0], spread_ref[...], NT).astype(BF)
        out_ref[...] = result.reshape(out_ref.shape)

    @pl.when(step == last)
    def _():
        out_ref[:, : edge_ref.shape[1]] = edge_ref[...]


def project(pos, mine, theirs, weight, edge):
    blocks, half, width = mine.shape
    streams, rows, _ = weight.shape
    slabs, edge_len, positions = edge.shape
    chans = rows // slabs
    return pl.pallas_call(
        project_kernel,
        grid_spec=pltpu.PrefetchScalarGridSpec(
            num_scalar_prefetch=1,
            grid=(streams + 1,),
            in_specs=[
                pl.BlockSpec(memory_space=pltpu.VMEM),
                pl.BlockSpec(memory_space=pltpu.VMEM),
                pl.BlockSpec((1, rows, width), lambda i, pos: (jnp.minimum(i, streams - 1), 0, 0)),
                pl.BlockSpec(edge.shape, lambda i, pos: (0, 0, 0)),
            ],
            out_specs=pl.BlockSpec((slabs, chans, positions), lambda i, pos: (0, i, 0)),
            scratch_shapes=[pltpu.VMEM((positions, width), BF)],
        ),
        out_shape=kept((slabs, streams * chans + edge_len, positions)),
        compiler_params=params(36 << 20),
        cost_estimate=cost(
            2 * positions * width * streams * rows,
            2 * (positions * width + weight.size + positions * streams * rows),
        ),
        name="project",
    )(pos, mine, theirs, stay(weight), stay(edge))


def turn_kernel(pos_ref, mine_ref, theirs_ref, out_ref, spread_ref):
    in_order(pos_ref[1], mine_ref, theirs_ref, spread_ref)
    out_ref[...] = jnp.transpose(spread_ref[...])


def turn_tokens(pos, mine, theirs):
    blocks, half, width = mine.shape
    positions = 2 * blocks * half
    part = width // 4
    block = pl.BlockSpec((blocks, half, part), lambda i, pos: (0, 0, i))
    return pl.pallas_call(
        turn_kernel,
        grid_spec=pltpu.PrefetchScalarGridSpec(
            num_scalar_prefetch=1,
            grid=(4,),
            in_specs=[block, block],
            out_specs=pl.BlockSpec((part, positions), lambda i, pos: (i, 0)),
            scratch_shapes=[pltpu.VMEM((positions, part), BF)],
        ),
        out_shape=kept((width, positions)),
        compiler_params=params(),
        cost_estimate=cost(0, 4 * positions * width),
        name="turn_tokens",
    )(pos, mine, theirs)


def turn_shares_kernel(tokens_ref, out_ref, spread_ref):
    chips, cores, blocks, rows, _ = tokens_ref.shape
    for block in range(blocks):
        for core in range(cores):
            for chip in range(chips):
                base = ((block * cores + core) * chips + chip) * rows
                spread_ref[base : base + rows] = tokens_ref[chip, core, block]
    out_ref[...] = jnp.transpose(spread_ref[...])


def turn_shares(tokens):
    chips, cores, blocks, rows, width = tokens.shape
    positions = chips * cores * blocks * rows
    part = width // 4
    return pl.pallas_call(
        turn_shares_kernel,
        grid=(4,),
        in_specs=[pl.BlockSpec((chips, cores, blocks, rows, part), lambda i: (0, 0, 0, 0, i))],
        out_specs=pl.BlockSpec((part, positions), lambda i: (i, 0)),
        out_shape=kept((width, positions)),
        scratch_shapes=[pltpu.VMEM((positions, part), BF)],
        compiler_params=params(),
        cost_estimate=cost(0, 4 * tokens.size),
        name="turn_shares",
    )(tokens)


def delayed(value, steps):
    if steps == 0:
        return value
    lane = lax.broadcasted_iota(jnp.int32, value.shape, 1)
    return jnp.where(lane < steps, 0.0, pltpu.roll(value, steps, 1))


def advanced(value, steps):
    if steps == 0:
        return value
    lanes = value.shape[1]
    lane = lax.broadcasted_iota(jnp.int32, value.shape, 1)
    return jnp.where(lane >= lanes - steps, 0.0, pltpu.roll(value, lanes - steps, 1))


def two_part(value, table, dims):
    rows = value.shape[0]
    result = matmul(jnp.concatenate(split(value), axis=0), table, dims)
    return result[:rows] + result[rows:]


def spectrum(value, residue, table):
    width = value.shape[1] // BLOCKS
    parts = [value[:, block * width : (block + 1) * width] for block in range(BLOCKS)]
    real = parts[0]
    imag = None
    for block in range(1, BLOCKS):
        angle = block_angle(residue, block)
        real = real + parts[block] * math.cos(angle)
        term = parts[block] * -math.sin(angle)
        imag = term if imag is None else imag + term
    result = two_part(jnp.concatenate([real, imag], axis=1), table, NN)
    steps = result.shape[1] // 4
    quarter = [result[:, i * steps : (i + 1) * steps] for i in range(4)]
    return jnp.concatenate([quarter[0], quarter[2]], axis=1), jnp.concatenate(
        [quarter[1], quarter[3]], axis=1
    )


def from_spectrum(real, imag, residue, table, totals):
    steps = real.shape[1] // 2
    value = jnp.concatenate(
        [real[:, :steps], imag[:, :steps], real[:, steps:], imag[:, steps:]], axis=1
    )
    result = two_part(value, table, NT)
    width = result.shape[1] // 2
    even, odd = result[:, :width], result[:, width:]
    for block in range(BLOCKS):
        angle = block_angle(residue, block)
        term = even if block == 0 else even * math.cos(angle) - odd * math.sin(angle)
        totals[block] = term if totals[block] is None else totals[block] + term


def operator_kernel(grad_scale, parts_ref, taps_ref, phase_ref, table_ref, grads_ref, out_ref, held_ref, sem):
    copy = pltpu.make_async_copy(table_ref, held_ref, sem)
    copy.start()
    devices, _, positions = parts_ref.shape
    block_len = out_ref.shape[2]
    batches = 2
    chans = taps_ref.shape[0]
    streams = grads_ref.shape[0] // (batches * chans)
    taps_len = (taps_ref.shape[1] - 1) // streams
    sources = devices // batches
    all_taps = jnp.concatenate([taps_ref[...]] * batches, axis=0)

    def tap(stream, pos):
        column = stream * taps_len + pos
        return all_taps[:, column : column + 1]

    def summed(batch, row):
        total = parts_ref[batch, row : row + chans].astype(F32)
        for source in range(1, sources):
            total = total + parts_ref[source * batches + batch, row : row + chans].astype(F32)
        return total

    def edge(batch):
        return jnp.concatenate(
            [
                unfold(parts_ref[source * batches + batch, streams * chans :], block_len).astype(F32)
                for source in range(sources)
            ],
            axis=1,
        )

    filtered = []
    for stream in range(streams):
        total = jnp.concatenate([summed(batch, stream * chans) for batch in range(batches)], axis=0)
        acc = tap(stream, 0) * total
        for pos in range(1, taps_len):
            acc = acc + tap(stream, pos) * delayed(total, pos)
        filtered.append(acc)
    query, key, value = filtered
    skip = all_taps[:, streams * taps_len : streams * taps_len + 1]
    edges = [edge(batch) for batch in range(batches)]
    cot = jnp.concatenate([rows[:chans] for rows in edges], axis=0)
    long_filter = edges[0][chans:] + edges[1][chans:]
    gated = key * value
    d_conv = cot * query
    stacked = jnp.concatenate([gated, d_conv, long_filter], axis=0)
    rows = batches * chans
    totals = [None] * BLOCKS
    copy.wait()
    for residue in range(BLOCKS):
        cos_all, sin_all = spectrum(stacked, residue, held_ref[residue])
        g_real, d_real, h_real = cos_all[:rows], cos_all[rows : 2 * rows], cos_all[2 * rows :]
        g_imag, d_imag, h_imag = sin_all[:rows], sin_all[rows : 2 * rows], sin_all[2 * rows :]
        cos_phase = phase_ref[2 * residue : 2 * residue + 1]
        sin_phase = phase_ref[2 * residue + 1 : 2 * residue + 2]
        f_real = jnp.concatenate([h_real * cos_phase - h_imag * sin_phase] * batches, axis=0)
        f_imag = jnp.concatenate([h_real * sin_phase + h_imag * cos_phase] * batches, axis=0)
        conv_real = g_real * f_real - g_imag * f_imag
        conv_imag = g_real * f_imag + g_imag * f_real
        back_real = f_real * d_real + f_imag * d_imag
        back_imag = f_real * d_imag - f_imag * d_real
        corr_real = g_real * d_real + g_imag * d_imag
        corr_imag = g_real * d_imag - g_imag * d_real
        corr_real = corr_real[:chans] + corr_real[chans:]
        corr_imag = corr_imag[:chans] + corr_imag[chans:]
        lag_real = corr_real * cos_phase + corr_imag * sin_phase
        lag_imag = corr_imag * cos_phase - corr_real * sin_phase
        from_spectrum(
            jnp.concatenate([conv_real, back_real, lag_real], axis=0),
            jnp.concatenate([conv_imag, back_imag, lag_imag], axis=0),
            residue,
            held_ref[residue],
            totals,
        )
    result = jnp.concatenate(totals, axis=1)
    scale = 1.0 / positions
    conv_out = result[:rows] * scale + skip * gated
    d_gated = result[rows : 2 * rows] * scale + skip * d_conv
    filter_part = (result[2 * rows :] * (scale * grad_scale)).astype(BF)
    hyena_out = (query * conv_out).astype(BF)
    for device in range(devices):
        batch = device % batches
        lanes = slice(device // batches * block_len, (device // batches + 1) * block_len)
        out_ref[device, :chans] = hyena_out[batch * chans : (batch + 1) * chans, lanes]
        out_ref[device, chans:] = filter_part[:, lanes]
    for stream, grad in enumerate((cot * conv_out, d_gated * value, d_gated * key)):
        acc = tap(stream, 0) * grad
        for pos in range(1, taps_len):
            acc = acc + tap(stream, pos) * advanced(grad, pos)
        acc = acc.astype(BF)
        for batch in range(batches):
            row = (batch * streams + stream) * chans
            grads_ref[row : row + chans] = acc[batch * chans : (batch + 1) * chans]


def operator(parts, taps, phase, table, grad_scale, streams, block_len):
    devices, _, positions = parts.shape
    chans = taps.shape[0]
    rows = devices * block_len // positions * streams * chans
    full = pl.BlockSpec(memory_space=pltpu.VMEM)
    return pl.pallas_call(
        functools.partial(operator_kernel, grad_scale),
        in_specs=[full, full, full, pl.BlockSpec(memory_space=pl.ANY)],
        out_shape=(kept((rows, positions)), kept((devices, 2 * chans, block_len))),
        scratch_shapes=[pltpu.VMEM(table.shape, BF), pltpu.SemaphoreType.DMA],
        compiler_params=params(40 << 20),
        cost_estimate=cost(8 * rows * positions * positions, 2 * (parts.size + table.size)),
        name="operator",
    )(parts, taps, phase, stay(table))


def token_kernel(pos_ref, weight_ref, grads_ref, sent_ref, held_ref):
    streams, chips, _, rows, cols = weight_ref.shape
    positions = sent_ref.shape[1]
    grads = [grads_ref[:, 0, stream].reshape(cols, positions) for stream in range(streams)]
    for side, out_ref in ((1 - pos_ref[1], sent_ref), (pos_ref[1], held_ref)):
        total = None
        for stream in range(streams):
            weight = weight_ref[stream, :, pl.ds(side, 1)].reshape(chips * rows, cols)
            part = matmul(weight, grads[stream], NN)
            total = part if total is None else total + part
        out_ref[...] = total.astype(BF)


def token_part(pos, weight, grads, chan_count):
    streams, slab_rows, cols = weight.shape
    slabs, _, _, chans, positions = grads.shape
    rows = slab_rows // chan_count
    part = positions // 4
    dims = (streams, chan_count // 2, 2, rows, cols)
    return pl.pallas_call(
        token_kernel,
        grid_spec=pltpu.PrefetchScalarGridSpec(
            num_scalar_prefetch=1,
            grid=(4,),
            in_specs=[
                pl.BlockSpec(dims, lambda j, pos: (0, 0, 0, 0, 0)),
                pl.BlockSpec((slabs, 1, streams, chans, part), lambda j, pos: (0, pos[0], 0, 0, j)),
            ],
            out_specs=[pl.BlockSpec((slab_rows // 2, part), lambda j, pos: (0, j))] * 2,
        ),
        out_shape=(kept((slab_rows // 2, positions)), kept((slab_rows // 2, positions))),
        compiler_params=params(),
        cost_estimate=cost(2 * weight.size * positions, 8 * slab_rows * positions),
        name="token_part",
    )(pos, weight.reshape(dims), grads)


def pair_kernel(held_ref, received_ref, out_ref):
    out_ref[...] = (held_ref[...].astype(F32) + received_ref[...].astype(F32)).astype(BF)


def pair_sum(held, received):
    return pl.pallas_call(
        pair_kernel,
        in_specs=[pl.BlockSpec(memory_space=pltpu.VMEM)] * 2,
        out_shape=kept(held.shape),
        compiler_params=params(24 << 20),
        cost_estimate=cost(0, 6 * held.size),
        name="pair_sum",
    )(stay(held), received)


def weight_kernel(grad_scale, pos_ref, own_ref, other_ref, own_grads_ref, other_grads_ref, out_ref):
    chan_cols = out_ref.shape[2]
    positions = own_ref.shape[1]
    own = own_grads_ref[...].reshape(chan_cols, positions)
    other = other_grads_ref[...].reshape(chan_cols, positions)
    total = matmul(own_ref[...], own, NT) + matmul(other_ref[...], other, NT)
    out_ref[0] = (total * grad_scale).astype(BF)


def weight_grad(pos, own, other, grads, grad_scale):
    slabs, _, streams, chans, positions = grads.shape
    slab_rows = own.shape[0]
    chan_cols = slabs * chans
    block = (slabs, 1, 1, chans, positions)
    return pl.pallas_call(
        functools.partial(weight_kernel, grad_scale),
        grid_spec=pltpu.PrefetchScalarGridSpec(
            num_scalar_prefetch=1,
            grid=(streams,),
            in_specs=[
                pl.BlockSpec(own.shape, lambda i, pos: (0, 0)),
                pl.BlockSpec(own.shape, lambda i, pos: (0, 0)),
                pl.BlockSpec(block, lambda i, pos: (0, pos[0], i, 0, 0)),
                pl.BlockSpec(block, lambda i, pos: (0, 1 - pos[0], i, 0, 0)),
            ],
            out_specs=pl.BlockSpec((1, slab_rows, chan_cols), lambda i, pos: (i, 0, 0)),
        ),
        out_shape=jax.ShapeDtypeStruct((streams, slab_rows, chan_cols), BF),
        compiler_params=params(),
        cost_estimate=cost(
            4 * streams * slab_rows * chan_cols * positions,
            2 * (2 * own.size + grads.size + streams * slab_rows * chan_cols),
        ),
        name="weight_grad",
    )(pos, own, other, grads, grads)


def total_kernel(parts_ref, out_ref):
    total = parts_ref[0].astype(F32)
    for pos in range(1, parts_ref.shape[0]):
        total = total + parts_ref[pos].astype(F32)
    out_ref[0] = jnp.transpose(total).astype(BF)


def token_total(parts):
    _, rows, positions = parts.shape
    return pl.pallas_call(
        total_kernel,
        out_shape=jax.ShapeDtypeStruct((1, positions, rows), BF),
        compiler_params=params(24 << 20),
        cost_estimate=cost(0, 2 * parts.size),
        name="token_total",
    )(parts)


def finish_kernel(parts_ref, out_ref, filter_ref):
    slabs, rows, block_len = parts_ref.shape
    chans = rows // 2
    hyena = parts_ref[:, :chans].astype(F32).reshape(slabs * chans, block_len)
    filters = parts_ref[:, chans:].astype(F32).reshape(slabs * chans, block_len)
    out_ref[0] = jnp.transpose(hyena).astype(BF)
    filter_ref[...] = jnp.transpose(filters)


def finish(parts):
    slabs, rows, block_len = parts.shape
    chan_cols = slabs * rows // 2
    return pl.pallas_call(
        finish_kernel,
        out_shape=(
            jax.ShapeDtypeStruct((1, block_len, chan_cols), BF),
            jax.ShapeDtypeStruct((block_len, chan_cols), F32),
        ),
        compiler_params=params(24 << 20),
        cost_estimate=cost(0, 4 * parts.size),
        name="finish",
    )(parts)


def exchange(value, axis, groups=None):
    return lax.all_to_all(
        value, axis, split_axis=0, concat_axis=0, tiled=True, axis_index_groups=groups
    )


def local(tokens, in_weight, short_taps, long_filter, skip_gain, cotangent):
    seq_count = lax.axis_size("seq")
    dp_count = lax.axis_size("dp")
    dp_pos = lax.axis_index("dp").astype(jnp.int32)
    slab_pos = lax.axis_index("seq").astype(jnp.int32) * dp_count + dp_pos
    chan_count = lax.axis_size("chan")
    chan_pos = lax.axis_index("chan").astype(jnp.int32)
    core = chan_pos % 2
    pos = jnp.stack([dp_pos, core])
    tok_rows = tokens.shape[1]
    slab_rows = in_weight.shape[0]
    chan_cols = in_weight.shape[2]
    streams, taps_len = short_taps.shape[:2]
    positions = seq_count * tok_rows
    slabs = seq_count * dp_count
    chans = chan_cols // slabs
    half = tok_rows // 2
    share = tok_rows // chan_count
    chips = chan_count // 2
    grad_scale = 1.0 / math.sqrt(dp_count * positions)
    cores = [(i, i ^ 1) for i in range(chan_count)]
    weight = jnp.transpose(in_weight, (1, 0, 2))

    mine, edge, flipped = lax.optimization_barrier(
        (
            exchange(cut_tokens(pos, tokens, seq_count), "seq"),
            edge_rows(pos, cotangent, long_filter, slabs, positions),
            flip_weight(weight),
        )
    )
    theirs = lax.ppermute(mine, "chan", cores)
    parts = project(pos, mine, theirs, flipped, edge)

    shares = lax.dynamic_slice_in_dim(mine, chan_pos // 2 * share, share, 1)
    shares = lax.ppermute(shares, "dp", [(0, 1), (1, 0)])
    parts, shares, short_taps = lax.optimization_barrier((parts, shares, short_taps))
    shares = lax.all_gather(shares, "chan", axis=0)
    shares = shares.reshape(chips, 2, seq_count, share, slab_rows)
    taps = jnp.concatenate([short_taps.reshape(streams * taps_len, chan_cols), skip_gain[None]])
    taps = jnp.transpose(lax.dynamic_slice_in_dim(taps, slab_pos * chans, chans, 1))
    table, phase = transform_tables(positions)
    parts, taps = lax.optimization_barrier((exchange(parts, ("seq", "dp")), taps))

    grads, outs = operator(parts, taps, phase, table, grad_scale, streams, tok_rows)
    grads, shares, mine, theirs = lax.optimization_barrier((grads, shares, mine, theirs))
    grads = lax.all_gather(grads, ("seq", "dp"), axis=0)
    finished = finish(exchange(outs, ("seq", "dp")))
    grads, finished, own, other = lax.optimization_barrier(
        (grads, finished, turn_tokens(pos, mine, theirs), turn_shares(shares))
    )
    hyena_out, grad_filter = finished

    grads = grads.reshape(slabs, dp_count, streams, chans, positions)
    sent, held = token_part(pos, weight, grads, chan_count)
    token_block = pair_sum(held, lax.ppermute(sent, "chan", cores))
    token_block = exchange(
        token_block.reshape(chips, -1, positions),
        "chan",
        [[chip * 2 + side for chip in range(chips)] for side in range(2)],
    )
    grad_tokens = token_total(token_block)
    grad_weight = weight_grad(pos, own, other, grads, grad_scale)
    return (hyena_out, grad_tokens, jnp.transpose(grad_weight, (1, 0, 2)), grad_filter)


def solution(mesh):
    placed = (
        P("dp", "seq", None),
        P("seq", None, "chan"),
        P(None, None, "chan"),
        P("seq", "chan"),
        P("chan"),
        P("dp", "seq", "chan"),
    )
    return jax.shard_map(
        local,
        mesh=mesh,
        in_specs=placed,
        out_specs=(
            P("dp", "seq", "chan"),
            P("dp", None, ("seq", "chan")),
            P("seq", None, "chan"),
            P("seq", "chan"),
        ),
        check_vma=False,
    )
```

```python
import functools
import math

import jax
import jax.numpy as jnp
import numpy as np
from jax import lax
from jax.experimental import pallas as pl
from jax.experimental.pallas import tpu as pltpu
from jax.sharding import PartitionSpec as P

BF = jnp.bfloat16
F32 = jnp.float32
VMEM_BYTES = 60 << 20
NT = (((1,), (1,)), ((), ()))
NN = (((1,), (0,)), ((), ()))


def params(limit=VMEM_BYTES):
    return pltpu.CompilerParams(vmem_limit_bytes=limit)


def cost(flops, bytes_accessed):
    return pl.CostEstimate(flops=flops, bytes_accessed=bytes_accessed, transcendentals=0)


def kept(shape, dtype=BF):
    return pltpu.HBM(shape, dtype)


def stay(value):
    return pltpu.with_memory_space_constraint(value, pltpu.HBM)


def matmul(left, right, dims):
    return lax.dot_general(left, right, dims, preferred_element_type=F32)


def split(value):
    high = value.astype(BF)
    return high, (value - high.astype(F32)).astype(BF)


def edge_kernel(cot_ref, filter_ref, out_ref):
    slabs = out_ref.shape[0]
    chans = filter_ref.shape[1] // slabs
    taps = jnp.transpose(filter_ref[...]).astype(BF)
    cot = jnp.transpose(cot_ref[0].astype(F32)).astype(BF)
    for slab in range(slabs):
        part = slice(slab * chans, (slab + 1) * chans)
        fold(out_ref.at[slab], 0, jnp.concatenate([cot[part], taps[part]], axis=0))


def fold(out_ref, first, value):
    rows, block_len = value.shape
    count = rows * block_len // out_ref.shape[1]
    for pos in range(rows // count):
        out_ref[first : first + count, pos * block_len : (pos + 1) * block_len] = value[
            pos * count : (pos + 1) * count
        ]


def unfold(value, block_len):
    return jnp.concatenate(
        [value[:, at : at + block_len] for at in range(0, value.shape[1], block_len)], axis=0
    )


def edge_rows(cotangent, long_filter, slabs, lanes):
    _, tok_rows, chan_cols = cotangent.shape
    full = pl.BlockSpec(memory_space=pltpu.VMEM)
    return pl.pallas_call(
        edge_kernel,
        in_specs=[full, full],
        out_shape=kept((slabs, 2 * tok_rows * chan_cols // slabs // lanes, lanes)),
        compiler_params=params(),
        cost_estimate=cost(0, 8 * tok_rows * chan_cols),
        name="edge_rows",
    )(cotangent, long_filter)


def flip_kernel(weight_ref, out_ref):
    out_ref[0] = jnp.transpose(weight_ref[0])


def flip_weight(weight):
    streams, slab_rows, chan_cols = weight.shape
    half = chan_cols // 2
    return pl.pallas_call(
        flip_kernel,
        grid=(streams, 2),
        in_specs=[pl.BlockSpec((1, slab_rows, half), lambda i, j: (i, 0, j))],
        out_specs=pl.BlockSpec((1, half, slab_rows), lambda i, j: (i, j, 0)),
        out_shape=kept((streams, chan_cols, slab_rows)),
        compiler_params=params(),
        cost_estimate=cost(0, 4 * weight.size),
        name="flip_weight",
    )(weight)


BLOCKS = 4


def block_angle(residue, block):
    return math.pi * (2 * residue + 1) * block / (2 * BLOCKS)


def frequencies(count, residue):
    steps = 2 * BLOCKS * np.arange(count // (2 * BLOCKS))
    return steps + residue, steps + 2 * BLOCKS - 1 - residue


def transform_tables(count):
    width = count // BLOCKS
    tables, phases = [], []
    for residue in range(BLOCKS):
        columns, rows = [], []
        for side, freq in zip((1.0, -1.0), frequencies(count, residue)):
            angles = math.pi / (4 * count) * (2 * np.arange(width)[:, None] + 1) * (2 * freq[None] + 1)
            cos, sin = np.cos(angles), np.sin(angles)
            columns += [np.concatenate([cos, side * sin]), np.concatenate([-sin, side * cos])]
            rows.append(math.pi / (4 * count) * (2 * freq + 1))
        tables.append(np.concatenate(columns, axis=1))
        rows = np.concatenate(rows)
        phases += [np.cos(rows), np.sin(rows)]
    return jnp.asarray(np.stack(tables), BF), jnp.asarray(np.stack(phases), F32)


def cut_kernel(pos_ref, tokens_ref, out_ref):
    slabs, _, width = out_ref.shape
    for slab in range(slabs):
        out_ref[slab] = tokens_ref[0, :, slab * width : (slab + 1) * width]


def cut_tokens(pos, tokens, slabs):
    _, rows, width = tokens.shape
    dims = (slabs, rows // 2, width // slabs)
    return pl.pallas_call(
        cut_kernel,
        grid_spec=pltpu.PrefetchScalarGridSpec(
            num_scalar_prefetch=1,
            grid=(1,),
            in_specs=[pl.BlockSpec((1, rows // 2, width), lambda i, pos: (0, pos[1], 0))],
            out_specs=pl.BlockSpec(dims, lambda i, pos: (0, 0, 0)),
        ),
        out_shape=kept(dims),
        compiler_params=params(),
        cost_estimate=cost(0, 2 * tokens.size),
        name="cut_tokens",
    )(pos, tokens)


def in_order(core, mine_ref, theirs_ref, spread_ref):
    blocks, half, _ = mine_ref.shape
    for block in range(blocks):
        base = 2 * block * half
        spread_ref[pl.ds(pl.multiple_of(base + core * half, half), half)] = mine_ref[block]
        spread_ref[pl.ds(pl.multiple_of(base + (1 - core) * half, half), half)] = theirs_ref[block]


def project_kernel(pos_ref, mine_ref, theirs_ref, weight_ref, edge_ref, out_ref, spread_ref):
    step = pl.program_id(0)
    last = pl.num_programs(0) - 1

    @pl.when(step == 0)
    def _():
        in_order(pos_ref[1], mine_ref, theirs_ref, spread_ref)

    @pl.when(step < last)
    def _():
        result = matmul(weight_ref[0], spread_ref[...], NT).astype(BF)
        out_ref[...] = result.reshape(out_ref.shape)

    @pl.when(step == last)
    def _():
        out_ref[:, : edge_ref.shape[1]] = edge_ref[...]


def project(pos, mine, theirs, weight, edge):
    blocks, half, width = mine.shape
    streams, rows, _ = weight.shape
    slabs, edge_len, positions = edge.shape
    chans = rows // slabs
    return pl.pallas_call(
        project_kernel,
        grid_spec=pltpu.PrefetchScalarGridSpec(
            num_scalar_prefetch=1,
            grid=(streams + 1,),
            in_specs=[
                pl.BlockSpec(memory_space=pltpu.VMEM),
                pl.BlockSpec(memory_space=pltpu.VMEM),
                pl.BlockSpec((1, rows, width), lambda i, pos: (jnp.minimum(i, streams - 1), 0, 0)),
                pl.BlockSpec(edge.shape, lambda i, pos: (0, 0, 0)),
            ],
            out_specs=pl.BlockSpec((slabs, chans, positions), lambda i, pos: (0, i, 0)),
            scratch_shapes=[pltpu.VMEM((positions, width), BF)],
        ),
        out_shape=kept((slabs, streams * chans + edge_len, positions)),
        compiler_params=params(36 << 20),
        cost_estimate=cost(
            2 * positions * width * streams * rows,
            2 * (positions * width + weight.size + positions * streams * rows),
        ),
        name="project",
    )(pos, mine, theirs, stay(weight), stay(edge))


def turn_kernel(pos_ref, mine_ref, theirs_ref, out_ref, spread_ref):
    in_order(pos_ref[1], mine_ref, theirs_ref, spread_ref)
    out_ref[...] = jnp.transpose(spread_ref[...])


def turn_tokens(pos, mine, theirs):
    blocks, half, width = mine.shape
    positions = 2 * blocks * half
    part = width // 4
    block = pl.BlockSpec((blocks, half, part), lambda i, pos: (0, 0, i))
    return pl.pallas_call(
        turn_kernel,
        grid_spec=pltpu.PrefetchScalarGridSpec(
            num_scalar_prefetch=1,
            grid=(4,),
            in_specs=[block, block],
            out_specs=pl.BlockSpec((part, positions), lambda i, pos: (i, 0)),
            scratch_shapes=[pltpu.VMEM((positions, part), BF)],
        ),
        out_shape=kept((width, positions)),
        compiler_params=params(),
        cost_estimate=cost(0, 4 * positions * width),
        name="turn_tokens",
    )(pos, mine, theirs)


def turn_shares_kernel(tokens_ref, out_ref, spread_ref):
    chips, cores, blocks, rows, _ = tokens_ref.shape
    for block in range(blocks):
        for core in range(cores):
            for chip in range(chips):
                base = ((block * cores + core) * chips + chip) * rows
                spread_ref[base : base + rows] = tokens_ref[chip, core, block]
    out_ref[...] = jnp.transpose(spread_ref[...])


def turn_shares(tokens):
    chips, cores, blocks, rows, width = tokens.shape
    positions = chips * cores * blocks * rows
    part = width // 4
    return pl.pallas_call(
        turn_shares_kernel,
        grid=(4,),
        in_specs=[pl.BlockSpec((chips, cores, blocks, rows, part), lambda i: (0, 0, 0, 0, i))],
        out_specs=pl.BlockSpec((part, positions), lambda i: (i, 0)),
        out_shape=kept((width, positions)),
        scratch_shapes=[pltpu.VMEM((positions, part), BF)],
        compiler_params=params(),
        cost_estimate=cost(0, 4 * tokens.size),
        name="turn_shares",
    )(tokens)


def delayed(value, steps):
    if steps == 0:
        return value
    lane = lax.broadcasted_iota(jnp.int32, value.shape, 1)
    return jnp.where(lane < steps, 0.0, pltpu.roll(value, steps, 1))


def advanced(value, steps):
    if steps == 0:
        return value
    lanes = value.shape[1]
    lane = lax.broadcasted_iota(jnp.int32, value.shape, 1)
    return jnp.where(lane >= lanes - steps, 0.0, pltpu.roll(value, lanes - steps, 1))


def two_part(value, table, dims):
    rows = value.shape[0]
    result = matmul(jnp.concatenate(split(value), axis=0), table, dims)
    return result[:rows] + result[rows:]


def spectrum(value, residue, table):
    width = value.shape[1] // BLOCKS
    parts = [value[:, block * width : (block + 1) * width] for block in range(BLOCKS)]
    real = parts[0]
    imag = None
    for block in range(1, BLOCKS):
        angle = block_angle(residue, block)
        real = real + parts[block] * math.cos(angle)
        term = parts[block] * -math.sin(angle)
        imag = term if imag is None else imag + term
    result = two_part(jnp.concatenate([real, imag], axis=1), table, NN)
    steps = result.shape[1] // 4
    quarter = [result[:, i * steps : (i + 1) * steps] for i in range(4)]
    return jnp.concatenate([quarter[0], quarter[2]], axis=1), jnp.concatenate(
        [quarter[1], quarter[3]], axis=1
    )


def from_spectrum(real, imag, residue, table, totals):
    steps = real.shape[1] // 2
    value = jnp.concatenate(
        [real[:, :steps], imag[:, :steps], real[:, steps:], imag[:, steps:]], axis=1
    )
    result = two_part(value, table, NT)
    width = result.shape[1] // 2
    even, odd = result[:, :width], result[:, width:]
    for block in range(BLOCKS):
        angle = block_angle(residue, block)
        term = even if block == 0 else even * math.cos(angle) - odd * math.sin(angle)
        totals[block] = term if totals[block] is None else totals[block] + term


def operator_kernel(grad_scale, parts_ref, taps_ref, phase_ref, table_ref, grads_ref, out_ref, held_ref, sem):
    copy = pltpu.make_async_copy(table_ref, held_ref, sem)
    copy.start()
    sources, _, positions = parts_ref.shape
    block_len = out_ref.shape[2]
    chans = taps_ref.shape[0]
    streams = grads_ref.shape[0] // chans
    taps_len = (taps_ref.shape[1] - 1) // streams

    def tap(stream, pos):
        column = stream * taps_len + pos
        return taps_ref[:, column : column + 1]

    def summed(row):
        total = parts_ref[0, row : row + chans].astype(F32)
        for source in range(1, sources):
            total = total + parts_ref[source, row : row + chans].astype(F32)
        return total

    filtered = []
    for stream in range(streams):
        total = summed(stream * chans)
        acc = tap(stream, 0) * total
        for pos in range(1, taps_len):
            acc = acc + tap(stream, pos) * delayed(total, pos)
        filtered.append(acc)
    query, key, value = filtered
    skip = taps_ref[:, streams * taps_len : streams * taps_len + 1]
    edge = jnp.concatenate(
        [
            unfold(parts_ref[source, streams * chans :], block_len).astype(F32)
            for source in range(sources)
        ],
        axis=1,
    )
    cot, long_filter = edge[:chans], edge[chans:]
    gated = key * value
    d_conv = cot * query
    stacked = jnp.concatenate([gated, d_conv, long_filter], axis=0)
    rows = chans
    totals = [None] * BLOCKS
    copy.wait()
    for residue in range(BLOCKS):
        cos_all, sin_all = spectrum(stacked, residue, held_ref[residue])
        g_real, d_real, h_real = cos_all[:rows], cos_all[rows : 2 * rows], cos_all[2 * rows :]
        g_imag, d_imag, h_imag = sin_all[:rows], sin_all[rows : 2 * rows], sin_all[2 * rows :]
        cos_phase = phase_ref[2 * residue : 2 * residue + 1]
        sin_phase = phase_ref[2 * residue + 1 : 2 * residue + 2]
        f_real = h_real * cos_phase - h_imag * sin_phase
        f_imag = h_real * sin_phase + h_imag * cos_phase
        conv_real = g_real * f_real - g_imag * f_imag
        conv_imag = g_real * f_imag + g_imag * f_real
        back_real = f_real * d_real + f_imag * d_imag
        back_imag = f_real * d_imag - f_imag * d_real
        corr_real = g_real * d_real + g_imag * d_imag
        corr_imag = g_real * d_imag - g_imag * d_real
        lag_real = corr_real * cos_phase + corr_imag * sin_phase
        lag_imag = corr_imag * cos_phase - corr_real * sin_phase
        from_spectrum(
            jnp.concatenate([conv_real, back_real, lag_real], axis=0),
            jnp.concatenate([conv_imag, back_imag, lag_imag], axis=0),
            residue,
            held_ref[residue],
            totals,
        )
    result = jnp.concatenate(totals, axis=1)
    scale = 1.0 / positions
    conv_out = result[:rows] * scale + skip * gated
    d_gated = result[rows : 2 * rows] * scale + skip * d_conv
    filter_part = (result[2 * rows :] * (scale * grad_scale)).astype(BF)
    hyena_out = (query * conv_out).astype(BF)
    for block in range(sources):
        lanes = slice(block * block_len, (block + 1) * block_len)
        out_ref[block, :chans] = hyena_out[:, lanes]
        out_ref[block, chans:] = filter_part[:, lanes]
    for stream, grad in enumerate((cot * conv_out, d_gated * value, d_gated * key)):
        acc = tap(stream, 0) * grad
        for pos in range(1, taps_len):
            acc = acc + tap(stream, pos) * advanced(grad, pos)
        grads_ref[stream * chans : (stream + 1) * chans] = acc.astype(BF)


def operator(parts, taps, phase, table, grad_scale, streams, block_len):
    sources, _, positions = parts.shape
    chans = taps.shape[0]
    rows = streams * chans
    full = pl.BlockSpec(memory_space=pltpu.VMEM)
    return pl.pallas_call(
        functools.partial(operator_kernel, grad_scale),
        in_specs=[full, full, full, pl.BlockSpec(memory_space=pl.ANY)],
        out_shape=(kept((rows, positions)), kept((sources, 2 * chans, block_len))),
        scratch_shapes=[pltpu.VMEM(table.shape, BF), pltpu.SemaphoreType.DMA],
        compiler_params=params(40 << 20),
        cost_estimate=cost(8 * rows * positions * positions, 2 * (parts.size + table.size)),
        name="operator",
    )(parts, taps, phase, stay(table))


def token_kernel(pos_ref, weight_ref, grads_ref, sent_ref, held_ref):
    streams, chips, _, rows, cols = weight_ref.shape
    positions = sent_ref.shape[1]
    grads = [grads_ref[:, 0, stream].reshape(cols, positions) for stream in range(streams)]
    for side, out_ref in ((1 - pos_ref[1], sent_ref), (pos_ref[1], held_ref)):
        total = None
        for stream in range(streams):
            weight = weight_ref[stream, :, pl.ds(side, 1)].reshape(chips * rows, cols)
            part = matmul(weight, grads[stream], NN)
            total = part if total is None else total + part
        out_ref[...] = total.astype(BF)


def token_part(pos, weight, grads, chan_count):
    streams, slab_rows, cols = weight.shape
    slabs, _, _, chans, positions = grads.shape
    rows = slab_rows // chan_count
    part = positions // 4
    dims = (streams, chan_count // 2, 2, rows, cols)
    return pl.pallas_call(
        token_kernel,
        grid_spec=pltpu.PrefetchScalarGridSpec(
            num_scalar_prefetch=1,
            grid=(4,),
            in_specs=[
                pl.BlockSpec(dims, lambda j, pos: (0, 0, 0, 0, 0)),
                pl.BlockSpec((slabs, 1, streams, chans, part), lambda j, pos: (0, pos[0], 0, 0, j)),
            ],
            out_specs=[pl.BlockSpec((slab_rows // 2, part), lambda j, pos: (0, j))] * 2,
        ),
        out_shape=(kept((slab_rows // 2, positions)), kept((slab_rows // 2, positions))),
        compiler_params=params(),
        cost_estimate=cost(2 * weight.size * positions, 8 * slab_rows * positions),
        name="token_part",
    )(pos, weight.reshape(dims), grads)


def pair_kernel(held_ref, received_ref, out_ref):
    out_ref[...] = (held_ref[...].astype(F32) + received_ref[...].astype(F32)).astype(BF)


def pair_sum(held, received):
    return pl.pallas_call(
        pair_kernel,
        in_specs=[pl.BlockSpec(memory_space=pltpu.VMEM)] * 2,
        out_shape=kept(held.shape),
        compiler_params=params(24 << 20),
        cost_estimate=cost(0, 6 * held.size),
        name="pair_sum",
    )(stay(held), received)


def weight_kernel(grad_scale, pos_ref, own_ref, other_ref, own_grads_ref, other_grads_ref, out_ref):
    chan_cols = out_ref.shape[2]
    positions = own_ref.shape[1]
    own = own_grads_ref[...].reshape(chan_cols, positions)
    other = other_grads_ref[...].reshape(chan_cols, positions)
    total = matmul(own_ref[...], own, NT) + matmul(other_ref[...], other, NT)
    out_ref[0] = (total * grad_scale).astype(BF)


def weight_grad(pos, own, other, grads, grad_scale):
    slabs, _, streams, chans, positions = grads.shape
    slab_rows = own.shape[0]
    chan_cols = slabs * chans
    block = (slabs, 1, 1, chans, positions)
    return pl.pallas_call(
        functools.partial(weight_kernel, grad_scale),
        grid_spec=pltpu.PrefetchScalarGridSpec(
            num_scalar_prefetch=1,
            grid=(streams,),
            in_specs=[
                pl.BlockSpec(own.shape, lambda i, pos: (0, 0)),
                pl.BlockSpec(own.shape, lambda i, pos: (0, 0)),
                pl.BlockSpec(block, lambda i, pos: (0, pos[0], i, 0, 0)),
                pl.BlockSpec(block, lambda i, pos: (0, 1 - pos[0], i, 0, 0)),
            ],
            out_specs=pl.BlockSpec((1, slab_rows, chan_cols), lambda i, pos: (i, 0, 0)),
        ),
        out_shape=jax.ShapeDtypeStruct((streams, slab_rows, chan_cols), BF),
        compiler_params=params(),
        cost_estimate=cost(
            4 * streams * slab_rows * chan_cols * positions,
            2 * (2 * own.size + grads.size + streams * slab_rows * chan_cols),
        ),
        name="weight_grad",
    )(pos, own, other, grads, grads)


def total_kernel(parts_ref, out_ref):
    total = parts_ref[0].astype(F32)
    for pos in range(1, parts_ref.shape[0]):
        total = total + parts_ref[pos].astype(F32)
    out_ref[0] = jnp.transpose(total).astype(BF)


def token_total(parts):
    _, rows, positions = parts.shape
    return pl.pallas_call(
        total_kernel,
        out_shape=jax.ShapeDtypeStruct((1, positions, rows), BF),
        compiler_params=params(24 << 20),
        cost_estimate=cost(0, 2 * parts.size),
        name="token_total",
    )(parts)


def finish_kernel(own_ref, other_ref, out_ref, filter_ref):
    slabs, rows, block_len = own_ref.shape
    chans = rows // 2
    hyena = own_ref[:, :chans].astype(F32).reshape(slabs * chans, block_len)
    filters = own_ref[:, chans:].astype(F32) + other_ref[...].astype(F32)
    out_ref[0] = jnp.transpose(hyena).astype(BF)
    filter_ref[...] = jnp.transpose(filters.reshape(slabs * chans, block_len))


def finish(own, other):
    slabs, rows, block_len = own.shape
    chan_cols = slabs * rows // 2
    return pl.pallas_call(
        finish_kernel,
        out_shape=(
            jax.ShapeDtypeStruct((1, block_len, chan_cols), BF),
            jax.ShapeDtypeStruct((block_len, chan_cols), F32),
        ),
        compiler_params=params(24 << 20),
        cost_estimate=cost(0, 4 * own.size),
        name="finish",
    )(own, other)


def exchange(value, axis, groups=None):
    return lax.all_to_all(
        value, axis, split_axis=0, concat_axis=0, tiled=True, axis_index_groups=groups
    )


def local(tokens, in_weight, short_taps, long_filter, skip_gain, cotangent):
    seq_count = lax.axis_size("seq")
    dp_count = lax.axis_size("dp")
    dp_pos = lax.axis_index("dp").astype(jnp.int32)
    seq_pos = lax.axis_index("seq").astype(jnp.int32)
    chan_count = lax.axis_size("chan")
    chan_pos = lax.axis_index("chan").astype(jnp.int32)
    core = chan_pos % 2
    pos = jnp.stack([dp_pos, core])
    tok_rows = tokens.shape[1]
    slab_rows = in_weight.shape[0]
    chan_cols = in_weight.shape[2]
    streams, taps_len = short_taps.shape[:2]
    positions = seq_count * tok_rows
    chans = chan_cols // seq_count
    half = tok_rows // 2
    share = tok_rows // chan_count
    chips = chan_count // 2
    grad_scale = 1.0 / math.sqrt(dp_count * positions)
    batches = [(0, 1), (1, 0)]
    cores = [(i, i ^ 1) for i in range(chan_count)]
    weight = jnp.transpose(in_weight, (1, 0, 2))

    mine, edge, flipped = lax.optimization_barrier(
        (
            exchange(cut_tokens(pos, tokens, seq_count), "seq"),
            edge_rows(cotangent, long_filter, seq_count, positions),
            flip_weight(weight),
        )
    )
    theirs = lax.ppermute(mine, "chan", cores)
    parts = project(pos, mine, theirs, flipped, edge)

    shares = lax.dynamic_slice_in_dim(mine, chan_pos // 2 * share, share, 1)
    shares = lax.ppermute(shares, "dp", batches)
    parts, shares, short_taps = lax.optimization_barrier((parts, shares, short_taps))
    shares = lax.all_gather(shares, "chan", axis=0)
    shares = shares.reshape(chips, 2, seq_count, share, slab_rows)
    taps = jnp.concatenate([short_taps.reshape(streams * taps_len, chan_cols), skip_gain[None]])
    taps = jnp.transpose(lax.dynamic_slice_in_dim(taps, seq_pos * chans, chans, 1))
    table, phase = transform_tables(positions)
    parts, taps = lax.optimization_barrier((exchange(parts, "seq"), taps))

    grads, outs = operator(parts, taps, phase, table, grad_scale, streams, tok_rows)
    grads, shares, mine, theirs = lax.optimization_barrier((grads, shares, mine, theirs))
    grads = lax.all_gather(grads, ("seq", "dp"), axis=0)
    outs = exchange(outs, "seq")
    finished = finish(outs, lax.ppermute(outs[:, chans:], "dp", batches))
    grads, finished, own, other = lax.optimization_barrier(
        (grads, finished, turn_tokens(pos, mine, theirs), turn_shares(shares))
    )
    hyena_out, grad_filter = finished

    grads = grads.reshape(seq_count, dp_count, streams, chans, positions)
    sent, held = token_part(pos, weight, grads, chan_count)
    token_block = pair_sum(held, lax.ppermute(sent, "chan", cores))
    token_block = exchange(
        token_block.reshape(chips, -1, positions),
        "chan",
        [[chip * 2 + side for chip in range(chips)] for side in range(2)],
    )
    grad_tokens = token_total(token_block)
    grad_weight = weight_grad(pos, own, other, grads, grad_scale)
    return (hyena_out, grad_tokens, jnp.transpose(grad_weight, (1, 0, 2)), grad_filter)


def solution(mesh):
    placed = (
        P("dp", "seq", None),
        P("seq", None, "chan"),
        P(None, None, "chan"),
        P("seq", "chan"),
        P("chan"),
        P("dp", "seq", "chan"),
    )
    return jax.shard_map(
        local,
        mesh=mesh,
        in_specs=placed,
        out_specs=(
            P("dp", "seq", "chan"),
            P("dp", None, ("seq", "chan")),
            P("seq", None, "chan"),
            P("seq", "chan"),
        ),
        check_vma=False,
    )
```

```python
import functools
import math

import jax
import jax.numpy as jnp
import numpy as np
from jax import lax
from jax.experimental import pallas as pl
from jax.experimental.pallas import tpu as pltpu
from jax.sharding import PartitionSpec as P

BF = jnp.bfloat16
F32 = jnp.float32
VMEM_BYTES = 60 << 20
NT = (((1,), (1,)), ((), ()))
NN = (((1,), (0,)), ((), ()))


def params(limit=VMEM_BYTES):
    return pltpu.CompilerParams(vmem_limit_bytes=limit)


def cost(flops, bytes_accessed):
    return pl.CostEstimate(flops=flops, bytes_accessed=bytes_accessed, transcendentals=0)


def kept(shape, dtype=BF):
    return pltpu.HBM(shape, dtype)


def stay(value):
    return pltpu.with_memory_space_constraint(value, pltpu.HBM)


def matmul(left, right, dims):
    return lax.dot_general(left, right, dims, preferred_element_type=F32)


def split(value):
    high = value.astype(BF)
    return high, (value - high.astype(F32)).astype(BF)


def edge_kernel(cot_ref, filter_ref, out_ref):
    slabs = out_ref.shape[0]
    chans = filter_ref.shape[1] // slabs
    taps = jnp.transpose(filter_ref[...]).astype(BF)
    cot = jnp.transpose(cot_ref[0].astype(F32)).astype(BF)
    for slab in range(slabs):
        part = slice(slab * chans, (slab + 1) * chans)
        fold(out_ref.at[slab], 0, jnp.concatenate([cot[part], taps[part]], axis=0))


def fold(out_ref, first, value):
    rows, block_len = value.shape
    count = rows * block_len // out_ref.shape[1]
    for pos in range(rows // count):
        out_ref[first : first + count, pos * block_len : (pos + 1) * block_len] = value[
            pos * count : (pos + 1) * count
        ]


def unfold(value, block_len):
    return jnp.concatenate(
        [value[:, at : at + block_len] for at in range(0, value.shape[1], block_len)], axis=0
    )


def edge_rows(cotangent, long_filter, slabs, lanes):
    _, tok_rows, chan_cols = cotangent.shape
    full = pl.BlockSpec(memory_space=pltpu.VMEM)
    return pl.pallas_call(
        edge_kernel,
        in_specs=[full, full],
        out_shape=kept((slabs, 2 * tok_rows * chan_cols // slabs // lanes, lanes)),
        compiler_params=params(),
        cost_estimate=cost(0, 8 * tok_rows * chan_cols),
        name="edge_rows",
    )(cotangent, long_filter)


def flip_kernel(weight_ref, out_ref):
    out_ref[0] = jnp.transpose(weight_ref[0])


def flip_weight(weight):
    streams, slab_rows, chan_cols = weight.shape
    half = chan_cols // 2
    return pl.pallas_call(
        flip_kernel,
        grid=(streams, 2),
        in_specs=[pl.BlockSpec((1, slab_rows, half), lambda i, j: (i, 0, j))],
        out_specs=pl.BlockSpec((1, half, slab_rows), lambda i, j: (i, j, 0)),
        out_shape=kept((streams, chan_cols, slab_rows)),
        compiler_params=params(),
        cost_estimate=cost(0, 4 * weight.size),
        name="flip_weight",
    )(weight)


BLOCKS = 4


def block_angle(residue, block):
    return math.pi * (2 * residue + 1) * block / (2 * BLOCKS)


def frequencies(count, residue):
    steps = 2 * BLOCKS * np.arange(count // (2 * BLOCKS))
    return steps + residue, steps + 2 * BLOCKS - 1 - residue


def transform_tables(count):
    width = count // BLOCKS
    tables, phases = [], []
    for residue in range(BLOCKS):
        columns, rows = [], []
        for side, freq in zip((1.0, -1.0), frequencies(count, residue)):
            angles = math.pi / (4 * count) * (2 * np.arange(width)[:, None] + 1) * (2 * freq[None] + 1)
            cos, sin = np.cos(angles), np.sin(angles)
            columns += [np.concatenate([cos, side * sin]), np.concatenate([-sin, side * cos])]
            rows.append(math.pi / (4 * count) * (2 * freq + 1))
        tables.append(np.concatenate(columns, axis=1))
        rows = np.concatenate(rows)
        phases += [np.cos(rows), np.sin(rows)]
    return jnp.asarray(np.stack(tables), BF), jnp.asarray(np.stack(phases), F32)


def cut_kernel(core_ref, tokens_ref, out_ref):
    slabs, _, width = out_ref.shape
    for slab in range(slabs):
        out_ref[slab] = tokens_ref[0, :, slab * width : (slab + 1) * width]


def cut_tokens(core, tokens, slabs):
    _, rows, width = tokens.shape
    dims = (slabs, rows // 2, width // slabs)
    return pl.pallas_call(
        cut_kernel,
        grid_spec=pltpu.PrefetchScalarGridSpec(
            num_scalar_prefetch=1,
            grid=(1,),
            in_specs=[pl.BlockSpec((1, rows // 2, width), lambda i, core: (0, core[0], 0))],
            out_specs=pl.BlockSpec(dims, lambda i, core: (0, 0, 0)),
        ),
        out_shape=kept(dims),
        compiler_params=params(),
        cost_estimate=cost(0, 2 * tokens.size),
        name="cut_tokens",
    )(core, tokens)


def in_order(core, mine_ref, theirs_ref, spread_ref):
    blocks, half, _ = mine_ref.shape
    for block in range(blocks):
        base = 2 * block * half
        spread_ref[pl.ds(pl.multiple_of(base + core * half, half), half)] = mine_ref[block]
        spread_ref[pl.ds(pl.multiple_of(base + (1 - core) * half, half), half)] = theirs_ref[block]


def project_kernel(pos_ref, mine_ref, theirs_ref, weight_ref, edge_ref, out_ref, spread_ref):
    step = pl.program_id(0)
    last = pl.num_programs(0) - 1

    @pl.when(step == 0)
    def _():
        in_order(pos_ref[1], mine_ref, theirs_ref, spread_ref)

    @pl.when(step < last)
    def _():
        result = matmul(weight_ref[0], spread_ref[...], NT).astype(BF)
        out_ref[...] = result.reshape(out_ref.shape)

    @pl.when(step == last)
    def _():
        out_ref[:, : edge_ref.shape[1]] = edge_ref[...]


def project(pos, mine, theirs, weight, edge):
    blocks, half, width = mine.shape
    streams, rows, _ = weight.shape
    slabs, edge_len, positions = edge.shape
    chans = rows // slabs
    return pl.pallas_call(
        project_kernel,
        grid_spec=pltpu.PrefetchScalarGridSpec(
            num_scalar_prefetch=1,
            grid=(streams + 1,),
            in_specs=[
                pl.BlockSpec(memory_space=pltpu.VMEM),
                pl.BlockSpec(memory_space=pltpu.VMEM),
                pl.BlockSpec((1, rows, width), lambda i, pos: (jnp.minimum(i, streams - 1), 0, 0)),
                pl.BlockSpec(edge.shape, lambda i, pos: (0, 0, 0)),
            ],
            out_specs=pl.BlockSpec((slabs, chans, positions), lambda i, pos: (0, i, 0)),
            scratch_shapes=[pltpu.VMEM((positions, width), BF)],
        ),
        out_shape=kept((slabs, streams * chans + edge_len, positions)),
        compiler_params=params(36 << 20),
        cost_estimate=cost(
            2 * positions * width * streams * rows,
            2 * (positions * width + weight.size + positions * streams * rows),
        ),
        name="project",
    )(pos, mine, theirs, stay(weight), stay(edge))


def turn_kernel(pos_ref, mine_ref, theirs_ref, out_ref, spread_ref):
    in_order(pos_ref[1], mine_ref, theirs_ref, spread_ref)
    out_ref[...] = jnp.transpose(spread_ref[...])


def turn_tokens(pos, mine, theirs):
    blocks, half, width = mine.shape
    positions = 2 * blocks * half
    part = width // 4
    block = pl.BlockSpec((blocks, half, part), lambda i, pos: (0, 0, i))
    return pl.pallas_call(
        turn_kernel,
        grid_spec=pltpu.PrefetchScalarGridSpec(
            num_scalar_prefetch=1,
            grid=(4,),
            in_specs=[block, block],
            out_specs=pl.BlockSpec((part, positions), lambda i, pos: (i, 0)),
            scratch_shapes=[pltpu.VMEM((positions, part), BF)],
        ),
        out_shape=kept((width, positions)),
        compiler_params=params(),
        cost_estimate=cost(0, 4 * positions * width),
        name="turn_tokens",
    )(pos, mine, theirs)


def turn_shares_kernel(tokens_ref, out_ref, spread_ref):
    chips, cores, blocks, rows, _ = tokens_ref.shape
    for block in range(blocks):
        for core in range(cores):
            for chip in range(chips):
                base = ((block * cores + core) * chips + chip) * rows
                spread_ref[base : base + rows] = tokens_ref[chip, core, block]
    out_ref[...] = jnp.transpose(spread_ref[...])


def turn_shares(tokens):
    chips, cores, blocks, rows, width = tokens.shape
    positions = chips * cores * blocks * rows
    part = width // 4
    return pl.pallas_call(
        turn_shares_kernel,
        grid=(4,),
        in_specs=[pl.BlockSpec((chips, cores, blocks, rows, part), lambda i: (0, 0, 0, 0, i))],
        out_specs=pl.BlockSpec((part, positions), lambda i: (i, 0)),
        out_shape=kept((width, positions)),
        scratch_shapes=[pltpu.VMEM((positions, part), BF)],
        compiler_params=params(),
        cost_estimate=cost(0, 4 * tokens.size),
        name="turn_shares",
    )(tokens)


def delayed(value, steps):
    if steps == 0:
        return value
    lane = lax.broadcasted_iota(jnp.int32, value.shape, 1)
    return jnp.where(lane < steps, 0.0, pltpu.roll(value, steps, 1))


def advanced(value, steps):
    if steps == 0:
        return value
    lanes = value.shape[1]
    lane = lax.broadcasted_iota(jnp.int32, value.shape, 1)
    return jnp.where(lane >= lanes - steps, 0.0, pltpu.roll(value, lanes - steps, 1))


def two_part(value, table, dims):
    rows = value.shape[0]
    result = matmul(jnp.concatenate(split(value), axis=0), table, dims)
    return result[:rows] + result[rows:]


def spectrum(value, residue, table):
    width = value.shape[1] // BLOCKS
    parts = [value[:, block * width : (block + 1) * width] for block in range(BLOCKS)]
    real = parts[0]
    imag = None
    for block in range(1, BLOCKS):
        angle = block_angle(residue, block)
        real = real + parts[block] * math.cos(angle)
        term = parts[block] * -math.sin(angle)
        imag = term if imag is None else imag + term
    result = two_part(jnp.concatenate([real, imag], axis=1), table, NN)
    steps = result.shape[1] // 4
    quarter = [result[:, i * steps : (i + 1) * steps] for i in range(4)]
    return jnp.concatenate([quarter[0], quarter[2]], axis=1), jnp.concatenate(
        [quarter[1], quarter[3]], axis=1
    )


def from_spectrum(real, imag, residue, table, totals):
    steps = real.shape[1] // 2
    value = jnp.concatenate(
        [real[:, :steps], imag[:, :steps], real[:, steps:], imag[:, steps:]], axis=1
    )
    result = two_part(value, table, NT)
    width = result.shape[1] // 2
    even, odd = result[:, :width], result[:, width:]
    for block in range(BLOCKS):
        angle = block_angle(residue, block)
        term = even if block == 0 else even * math.cos(angle) - odd * math.sin(angle)
        totals[block] = term if totals[block] is None else totals[block] + term


def operator_kernel(grad_scale, parts_ref, taps_ref, phase_ref, table_ref, grads_ref, out_ref, held_ref, sem):
    copy = pltpu.make_async_copy(table_ref, held_ref, sem)
    copy.start()
    sources, _, positions = parts_ref.shape
    block_len = out_ref.shape[2]
    chans = taps_ref.shape[0]
    streams = grads_ref.shape[0] // chans
    taps_len = (taps_ref.shape[1] - 1) // streams

    def tap(stream, pos):
        column = stream * taps_len + pos
        return taps_ref[:, column : column + 1]

    def summed(row):
        total = parts_ref[0, row : row + chans].astype(F32)
        for source in range(1, sources):
            total = total + parts_ref[source, row : row + chans].astype(F32)
        return total

    filtered = []
    for stream in range(streams):
        total = summed(stream * chans)
        acc = tap(stream, 0) * total
        for pos in range(1, taps_len):
            acc = acc + tap(stream, pos) * delayed(total, pos)
        filtered.append(acc)
    query, key, value = filtered
    skip = taps_ref[:, streams * taps_len : streams * taps_len + 1]
    edge = jnp.concatenate(
        [
            unfold(parts_ref[source, streams * chans :], block_len).astype(F32)
            for source in range(sources)
        ],
        axis=1,
    )
    cot, long_filter = edge[:chans], edge[chans:]
    gated = key * value
    d_conv = cot * query
    stacked = jnp.concatenate([gated, d_conv, long_filter], axis=0)
    rows = chans
    totals = [None] * BLOCKS
    copy.wait()
    for residue in range(BLOCKS):
        cos_all, sin_all = spectrum(stacked, residue, held_ref[residue])
        g_real, d_real, h_real = cos_all[:rows], cos_all[rows : 2 * rows], cos_all[2 * rows :]
        g_imag, d_imag, h_imag = sin_all[:rows], sin_all[rows : 2 * rows], sin_all[2 * rows :]
        cos_phase = phase_ref[2 * residue : 2 * residue + 1]
        sin_phase = phase_ref[2 * residue + 1 : 2 * residue + 2]
        f_real = h_real * cos_phase - h_imag * sin_phase
        f_imag = h_real * sin_phase + h_imag * cos_phase
        conv_real = g_real * f_real - g_imag * f_imag
        conv_imag = g_real * f_imag + g_imag * f_real
        back_real = f_real * d_real + f_imag * d_imag
        back_imag = f_real * d_imag - f_imag * d_real
        corr_real = g_real * d_real + g_imag * d_imag
        corr_imag = g_real * d_imag - g_imag * d_real
        lag_real = corr_real * cos_phase + corr_imag * sin_phase
        lag_imag = corr_imag * cos_phase - corr_real * sin_phase
        from_spectrum(
            jnp.concatenate([conv_real, back_real, lag_real], axis=0),
            jnp.concatenate([conv_imag, back_imag, lag_imag], axis=0),
            residue,
            held_ref[residue],
            totals,
        )
    result = jnp.concatenate(totals, axis=1)
    scale = 1.0 / positions
    conv_out = result[:rows] * scale + skip * gated
    d_gated = result[rows : 2 * rows] * scale + skip * d_conv
    filter_part = (result[2 * rows :] * (scale * grad_scale)).astype(BF)
    hyena_out = (query * conv_out).astype(BF)
    for block in range(sources):
        lanes = slice(block * block_len, (block + 1) * block_len)
        out_ref[block, :chans] = hyena_out[:, lanes]
        out_ref[block, chans:] = filter_part[:, lanes]
    for stream, grad in enumerate((cot * conv_out, d_gated * value, d_gated * key)):
        acc = tap(stream, 0) * grad
        for pos in range(1, taps_len):
            acc = acc + tap(stream, pos) * advanced(grad, pos)
        grads_ref[stream * chans : (stream + 1) * chans] = acc.astype(BF)


def operator(parts, taps, phase, table, grad_scale, streams, block_len):
    sources, _, positions = parts.shape
    chans = taps.shape[0]
    rows = streams * chans
    full = pl.BlockSpec(memory_space=pltpu.VMEM)
    return pl.pallas_call(
        functools.partial(operator_kernel, grad_scale),
        in_specs=[full, full, full, pl.BlockSpec(memory_space=pl.ANY)],
        out_shape=(kept((rows, positions)), kept((sources, 2 * chans, block_len))),
        scratch_shapes=[pltpu.VMEM(table.shape, BF), pltpu.SemaphoreType.DMA],
        compiler_params=params(40 << 20),
        cost_estimate=cost(8 * rows * positions * positions, 2 * (parts.size + table.size)),
        name="operator",
    )(parts, taps, phase, stay(table))


def near_kernel(weight_ref, out_ref, sem):
    copy = pltpu.make_async_copy(weight_ref, out_ref, sem)
    copy.start()
    copy.wait()


def near_weight(weight):
    return pl.pallas_call(
        near_kernel,
        in_specs=[pl.BlockSpec(memory_space=pltpu.HBM)],
        out_specs=pl.BlockSpec(memory_space=pltpu.VMEM),
        out_shape=pltpu.VMEM(weight.shape, weight.dtype),
        scratch_shapes=[pltpu.SemaphoreType.DMA],
        compiler_params=params(16 << 20),
        cost_estimate=cost(0, 4 * weight.size),
        name="near_weight",
    )(stay(weight))


def token_kernel(pos_ref, weight_ref, grads_ref, sent_ref, held_ref):
    streams, chips, _, rows, cols = weight_ref.shape
    part = sent_ref.shape[1]
    grads = [grads_ref[:, 0, stream].reshape(cols, part) for stream in range(streams)]
    lanes = pl.ds(pl.multiple_of(pl.program_id(0) * part, part), part)
    for own in (False, True):
        total = None
        side = pos_ref[1] if own else 1 - pos_ref[1]
        for stream in range(streams):
            weight = weight_ref[stream, :, pl.ds(side, 1)].reshape(chips * rows, cols)
            term = matmul(weight, grads[stream], NN)
            total = term if total is None else total + term
        if own:
            held_ref[:, lanes] = total.astype(BF)
        else:
            sent_ref[...] = total.astype(BF)


def token_part(pos, weight, grads):
    streams, chips, cores, rows, cols = weight.shape
    slabs, _, _, chans, positions = grads.shape
    part = positions // 4
    return pl.pallas_call(
        token_kernel,
        grid_spec=pltpu.PrefetchScalarGridSpec(
            num_scalar_prefetch=1,
            grid=(4,),
            in_specs=[
                pl.BlockSpec(memory_space=pltpu.VMEM),
                pl.BlockSpec((slabs, 1, streams, chans, part), lambda j, pos: (0, pos[0], 0, 0, j)),
            ],
            out_specs=[
                pl.BlockSpec((chips * rows, part), lambda j, pos: (0, j)),
                pl.BlockSpec(memory_space=pltpu.VMEM),
            ],
        ),
        out_shape=(kept((chips * rows, positions)), pltpu.VMEM((chips * rows, positions), BF)),
        compiler_params=params(40 << 20),
        cost_estimate=cost(2 * weight.size * positions, 8 * chips * rows * positions),
        name="token_part",
    )(pos, weight, stay(grads))


def pair_kernel(held_ref, received_ref, out_ref):
    out_ref[...] = (held_ref[...].astype(F32) + received_ref[...].astype(F32)).astype(BF)


def pair_sum(held, received):
    return pl.pallas_call(
        pair_kernel,
        in_specs=[pl.BlockSpec(memory_space=pltpu.VMEM)] * 2,
        out_shape=kept(held.shape),
        compiler_params=params(24 << 20),
        cost_estimate=cost(0, 6 * held.size),
        name="pair_sum",
    )(held, received)


def weight_kernel(grad_scale, pos_ref, own_ref, other_ref, own_grads_ref, other_grads_ref, out_ref):
    chan_cols = out_ref.shape[2]
    positions = own_ref.shape[1]
    own = own_grads_ref[...].reshape(chan_cols, positions)
    other = other_grads_ref[...].reshape(chan_cols, positions)
    total = matmul(own_ref[...], own, NT) + matmul(other_ref[...], other, NT)
    out_ref[0] = (total * grad_scale).astype(BF)


def weight_grad(pos, own, other, grads, grad_scale):
    slabs, _, streams, chans, positions = grads.shape
    slab_rows = own.shape[0]
    chan_cols = slabs * chans
    block = (slabs, 1, 1, chans, positions)
    return pl.pallas_call(
        functools.partial(weight_kernel, grad_scale),
        grid_spec=pltpu.PrefetchScalarGridSpec(
            num_scalar_prefetch=1,
            grid=(streams,),
            in_specs=[
                pl.BlockSpec(own.shape, lambda i, pos: (0, 0)),
                pl.BlockSpec(own.shape, lambda i, pos: (0, 0)),
                pl.BlockSpec(block, lambda i, pos: (0, pos[0], i, 0, 0)),
                pl.BlockSpec(block, lambda i, pos: (0, 1 - pos[0], i, 0, 0)),
            ],
            out_specs=pl.BlockSpec((1, slab_rows, chan_cols), lambda i, pos: (i, 0, 0)),
        ),
        out_shape=jax.ShapeDtypeStruct((streams, slab_rows, chan_cols), BF),
        compiler_params=params(),
        cost_estimate=cost(
            4 * streams * slab_rows * chan_cols * positions,
            2 * (2 * own.size + grads.size + streams * slab_rows * chan_cols),
        ),
        name="weight_grad",
    )(pos, own, other, grads, grads)


def total_kernel(parts_ref, out_ref):
    total = parts_ref[0].astype(F32)
    for pos in range(1, parts_ref.shape[0]):
        total = total + parts_ref[pos].astype(F32)
    out_ref[0] = jnp.transpose(total).astype(BF)


def token_total(parts):
    _, rows, positions = parts.shape
    return pl.pallas_call(
        total_kernel,
        out_shape=jax.ShapeDtypeStruct((1, positions, rows), BF),
        compiler_params=params(24 << 20),
        cost_estimate=cost(0, 2 * parts.size),
        name="token_total",
    )(parts)


def finish_kernel(own_ref, other_ref, out_ref, filter_ref):
    slabs, rows, block_len = own_ref.shape
    chans = rows // 2
    hyena = own_ref[:, :chans].astype(F32).reshape(slabs * chans, block_len)
    filters = own_ref[:, chans:].astype(F32) + other_ref[...].astype(F32)
    out_ref[0] = jnp.transpose(hyena).astype(BF)
    filter_ref[...] = jnp.transpose(filters.reshape(slabs * chans, block_len))


def finish(own, other):
    slabs, rows, block_len = own.shape
    chan_cols = slabs * rows // 2
    return pl.pallas_call(
        finish_kernel,
        out_shape=(
            jax.ShapeDtypeStruct((1, block_len, chan_cols), BF),
            jax.ShapeDtypeStruct((block_len, chan_cols), F32),
        ),
        compiler_params=params(24 << 20),
        cost_estimate=cost(0, 4 * own.size),
        name="finish",
    )(own, other)


def exchange(value, axis, groups=None):
    return lax.all_to_all(
        value, axis, split_axis=0, concat_axis=0, tiled=True, axis_index_groups=groups
    )


def local(tokens, in_weight, short_taps, long_filter, skip_gain, cotangent):
    seq_count = lax.axis_size("seq")
    dp_count = lax.axis_size("dp")
    dp_pos = lax.axis_index("dp").astype(jnp.int32)
    seq_pos = lax.axis_index("seq").astype(jnp.int32)
    chan_count = lax.axis_size("chan")
    chan_pos = lax.axis_index("chan").astype(jnp.int32)
    core = chan_pos % 2
    pos = jnp.stack([dp_pos, core])
    tok_rows = tokens.shape[1]
    slab_rows = in_weight.shape[0]
    chan_cols = in_weight.shape[2]
    streams, taps_len = short_taps.shape[:2]
    positions = seq_count * tok_rows
    chans = chan_cols // seq_count
    half = tok_rows // 2
    share = tok_rows // chan_count
    chips = chan_count // 2
    grad_scale = 1.0 / math.sqrt(dp_count * positions)
    batches = [(0, 1), (1, 0)]
    cores = [(i, i ^ 1) for i in range(chan_count)]
    weight = jnp.transpose(in_weight, (1, 0, 2))

    mine, edge, flipped = lax.optimization_barrier(
        (
            exchange(cut_tokens(core[None], tokens, seq_count), "seq"),
            edge_rows(cotangent, long_filter, seq_count, positions),
            flip_weight(weight),
        )
    )
    theirs = lax.ppermute(mine, "chan", cores)
    parts = project(pos, mine, theirs, flipped, edge)

    shares = lax.dynamic_slice_in_dim(mine, chan_pos // 2 * share, share, 1)
    shares = lax.ppermute(shares, "dp", batches)
    parts, shares, short_taps = lax.optimization_barrier((parts, shares, short_taps))
    shares = lax.all_gather(shares, "chan", axis=0)
    shares = shares.reshape(chips, 2, seq_count, share, slab_rows)
    taps = jnp.concatenate([short_taps.reshape(streams * taps_len, chan_cols), skip_gain[None]])
    taps = jnp.transpose(lax.dynamic_slice_in_dim(taps, seq_pos * chans, chans, 1))
    table, phase = transform_tables(positions)
    parts, taps = lax.optimization_barrier((exchange(parts, "seq"), taps))

    grads, outs = operator(parts, taps, phase, table, grad_scale, streams, tok_rows)
    grads, shares, mine, theirs = lax.optimization_barrier((grads, shares, mine, theirs))
    grads = lax.all_gather(grads, ("seq", "dp"), axis=0)
    outs = exchange(outs, "seq")
    finished = finish(outs, lax.ppermute(outs[:, chans:], "dp", batches))
    own, other, near, finished = lax.optimization_barrier(
        (
            turn_tokens(pos, mine, theirs),
            turn_shares(shares),
            weight.reshape(streams, chips, 2, slab_rows // chan_count, chan_cols),
            finished,
        )
    )
    near = near_weight(near)
    grads, finished, own, other = lax.optimization_barrier((grads, finished, own, other))
    hyena_out, grad_filter = finished

    grads = grads.reshape(seq_count, dp_count, streams, chans, positions)
    sent, held = token_part(pos, near, grads)
    token_block = pair_sum(held, lax.ppermute(sent, "chan", cores))
    token_block = exchange(
        token_block.reshape(chips, -1, positions),
        "chan",
        [[chip * 2 + side for chip in range(chips)] for side in range(2)],
    )
    grad_tokens = token_total(token_block)
    grad_weight = weight_grad(pos, own, other, grads, grad_scale)
    return (hyena_out, grad_tokens, jnp.transpose(grad_weight, (1, 0, 2)), grad_filter)


def solution(mesh):
    placed = (
        P("dp", "seq", None),
        P("seq", None, "chan"),
        P(None, None, "chan"),
        P("seq", "chan"),
        P("chan"),
        P("dp", "seq", "chan"),
    )
    return jax.shard_map(
        local,
        mesh=mesh,
        in_specs=placed,
        out_specs=(
            P("dp", "seq", "chan"),
            P("dp", None, ("seq", "chan")),
            P("seq", None, "chan"),
            P("seq", "chan"),
        ),
        check_vma=False,
    )
```

```python
import functools
import math

import jax
import jax.numpy as jnp
import numpy as np
from jax import lax
from jax.experimental import pallas as pl
from jax.experimental.pallas import tpu as pltpu
from jax.sharding import PartitionSpec as P

BF = jnp.bfloat16
F32 = jnp.float32
VMEM_BYTES = 60 << 20
NT = (((1,), (1,)), ((), ()))
NN = (((1,), (0,)), ((), ()))


def params(limit=VMEM_BYTES):
    return pltpu.CompilerParams(vmem_limit_bytes=limit)


def cost(flops, bytes_accessed):
    return pl.CostEstimate(flops=flops, bytes_accessed=bytes_accessed, transcendentals=0)


def kept(shape, dtype=BF):
    return pltpu.HBM(shape, dtype)


def stay(value):
    return pltpu.with_memory_space_constraint(value, pltpu.HBM)


def matmul(left, right, dims):
    return lax.dot_general(left, right, dims, preferred_element_type=F32)


def edge_kernel(cot_ref, filter_ref, out_ref):
    slabs = out_ref.shape[0]
    chans = filter_ref.shape[1] // slabs
    taps = jnp.transpose(filter_ref[...]).astype(BF)
    cot = jnp.transpose(cot_ref[0].astype(F32)).astype(BF)
    for slab in range(slabs):
        part = slice(slab * chans, (slab + 1) * chans)
        fold(out_ref.at[slab], 0, jnp.concatenate([cot[part], taps[part]], axis=0))


def fold(out_ref, first, value):
    rows, block_len = value.shape
    count = rows * block_len // out_ref.shape[1]
    for pos in range(rows // count):
        out_ref[first : first + count, pos * block_len : (pos + 1) * block_len] = value[
            pos * count : (pos + 1) * count
        ]


def unfold(value, block_len):
    return jnp.concatenate(
        [value[:, at : at + block_len] for at in range(0, value.shape[1], block_len)], axis=0
    )


def edge_rows(cotangent, long_filter, slabs, lanes):
    _, tok_rows, chan_cols = cotangent.shape
    full = pl.BlockSpec(memory_space=pltpu.VMEM)
    return pl.pallas_call(
        edge_kernel,
        in_specs=[full, full],
        out_shape=kept((slabs, 2 * tok_rows * chan_cols // slabs // lanes, lanes)),
        compiler_params=params(),
        cost_estimate=cost(0, 8 * tok_rows * chan_cols),
        name="edge_rows",
    )(cotangent, long_filter)


def flip_kernel(weight_ref, out_ref):
    out_ref[0] = jnp.transpose(weight_ref[0])


def flip_weight(weight):
    streams, slab_rows, chan_cols = weight.shape
    half = chan_cols // 2
    return pl.pallas_call(
        flip_kernel,
        grid=(streams, 2),
        in_specs=[pl.BlockSpec((1, slab_rows, half), lambda i, j: (i, 0, j))],
        out_specs=pl.BlockSpec((1, half, slab_rows), lambda i, j: (i, j, 0)),
        out_shape=kept((streams, chan_cols, slab_rows)),
        compiler_params=params(),
        cost_estimate=cost(0, 4 * weight.size),
        name="flip_weight",
    )(weight)


BLOCKS = 4


def block_angle(residue, block):
    return math.pi * (2 * residue + 1) * block / (2 * BLOCKS)


def frequencies(count, residue):
    steps = 2 * BLOCKS * np.arange(count // (2 * BLOCKS))
    return steps + residue, steps + 2 * BLOCKS - 1 - residue


def transform_tables(count):
    width = count // BLOCKS
    tables, phases = [], []
    for residue in range(BLOCKS):
        columns, rows = [], []
        for side, freq in zip((1.0, -1.0), frequencies(count, residue)):
            angles = math.pi / (4 * count) * (2 * np.arange(width)[:, None] + 1) * (2 * freq[None] + 1)
            cos, sin = np.cos(angles), np.sin(angles)
            columns += [np.concatenate([cos, side * sin]), np.concatenate([-sin, side * cos])]
            rows.append(math.pi / (4 * count) * (2 * freq + 1))
        tables.append(np.concatenate(columns, axis=1))
        rows = np.concatenate(rows)
        phases += [np.cos(rows), np.sin(rows)]
    return jnp.asarray(np.stack(tables), BF), jnp.asarray(np.stack(phases), F32)


def cut_kernel(core_ref, tokens_ref, out_ref, held_ref, in_sems, out_sems):
    slabs, half, width = held_ref.shape
    start = pl.multiple_of(core_ref[0] * half, half)
    inward = [
        pltpu.make_async_copy(
            tokens_ref.at[0, pl.ds(start, half), slice(slab * width, (slab + 1) * width)],
            held_ref.at[slab],
            in_sems.at[slab],
        )
        for slab in range(slabs)
    ]
    outward = [
        pltpu.make_async_copy(held_ref.at[slab], out_ref.at[slab], out_sems.at[slab])
        for slab in range(slabs)
    ]
    for copy in inward:
        copy.start()
    for slab in range(slabs):
        inward[slab].wait()
        outward[slab].start()
    for copy in outward:
        copy.wait()


def cut_tokens(core, tokens, slabs):
    _, rows, width = tokens.shape
    dims = (slabs, rows // 2, width // slabs)
    return pl.pallas_call(
        cut_kernel,
        in_specs=[pl.BlockSpec(memory_space=pltpu.SMEM), pl.BlockSpec(memory_space=pltpu.HBM)],
        out_specs=pl.BlockSpec(memory_space=pltpu.HBM),
        out_shape=kept(dims),
        scratch_shapes=[
            pltpu.VMEM(dims, BF),
            pltpu.SemaphoreType.DMA((slabs,)),
            pltpu.SemaphoreType.DMA((slabs,)),
        ],
        compiler_params=params(),
        cost_estimate=cost(0, 2 * tokens.size),
        name="cut_tokens",
    )(core, stay(tokens))


def in_order(core, mine_ref, theirs_ref, spread_ref):
    blocks, half, _ = mine_ref.shape
    for block in range(blocks):
        base = 2 * block * half
        spread_ref[pl.ds(pl.multiple_of(base + core * half, half), half)] = mine_ref[block]
        spread_ref[pl.ds(pl.multiple_of(base + (1 - core) * half, half), half)] = theirs_ref[block]


def project_kernel(pos_ref, mine_ref, theirs_ref, weight_ref, edge_ref, out_ref, spread_ref):
    step = pl.program_id(0)
    last = pl.num_programs(0) - 1

    @pl.when(step == 0)
    def _():
        in_order(pos_ref[1], mine_ref, theirs_ref, spread_ref)

    @pl.when(step < last)
    def _():
        result = matmul(weight_ref[0], spread_ref[...], NT).astype(BF)
        out_ref[...] = result.reshape(out_ref.shape)

    @pl.when(step == last)
    def _():
        out_ref[:, : edge_ref.shape[1]] = edge_ref[...]


def project(pos, mine, theirs, weight, edge):
    blocks, half, width = mine.shape
    streams, rows, _ = weight.shape
    slabs, edge_len, positions = edge.shape
    chans = rows // slabs
    return pl.pallas_call(
        project_kernel,
        grid_spec=pltpu.PrefetchScalarGridSpec(
            num_scalar_prefetch=1,
            grid=(streams + 1,),
            in_specs=[
                pl.BlockSpec(memory_space=pltpu.VMEM),
                pl.BlockSpec(memory_space=pltpu.VMEM),
                pl.BlockSpec((1, rows, width), lambda i, pos: (jnp.minimum(i, streams - 1), 0, 0)),
                pl.BlockSpec(edge.shape, lambda i, pos: (0, 0, 0)),
            ],
            out_specs=pl.BlockSpec((slabs, chans, positions), lambda i, pos: (0, i, 0)),
            scratch_shapes=[pltpu.VMEM((positions, width), BF)],
        ),
        out_shape=kept((slabs, streams * chans + edge_len, positions)),
        compiler_params=params(36 << 20),
        cost_estimate=cost(
            2 * positions * width * streams * rows,
            2 * (positions * width + weight.size + positions * streams * rows),
        ),
        name="project",
    )(pos, mine, theirs, stay(weight), stay(edge))


def turn_kernel(pos_ref, mine_ref, theirs_ref, out_ref, spread_ref):
    in_order(pos_ref[1], mine_ref, theirs_ref, spread_ref)
    out_ref[...] = jnp.transpose(spread_ref[...])


def turn_tokens(pos, mine, theirs):
    blocks, half, width = mine.shape
    positions = 2 * blocks * half
    part = width // 4
    block = pl.BlockSpec((blocks, half, part), lambda i, pos: (0, 0, i))
    return pl.pallas_call(
        turn_kernel,
        grid_spec=pltpu.PrefetchScalarGridSpec(
            num_scalar_prefetch=1,
            grid=(4,),
            in_specs=[block, block],
            out_specs=pl.BlockSpec((part, positions), lambda i, pos: (i, 0)),
            scratch_shapes=[pltpu.VMEM((positions, part), BF)],
        ),
        out_shape=kept((width, positions)),
        compiler_params=params(),
        cost_estimate=cost(0, 4 * positions * width),
        name="turn_tokens",
    )(pos, mine, theirs)


def turn_shares_kernel(tokens_ref, out_ref, spread_ref):
    chips, cores, blocks, rows, _ = tokens_ref.shape
    for block in range(blocks):
        for core in range(cores):
            for chip in range(chips):
                base = ((block * cores + core) * chips + chip) * rows
                spread_ref[base : base + rows] = tokens_ref[chip, core, block]
    out_ref[...] = jnp.transpose(spread_ref[...])


def turn_shares(tokens):
    chips, cores, blocks, rows, width = tokens.shape
    positions = chips * cores * blocks * rows
    part = width // 4
    return pl.pallas_call(
        turn_shares_kernel,
        grid=(4,),
        in_specs=[pl.BlockSpec((chips, cores, blocks, rows, part), lambda i: (0, 0, 0, 0, i))],
        out_specs=pl.BlockSpec((part, positions), lambda i: (i, 0)),
        out_shape=kept((width, positions)),
        scratch_shapes=[pltpu.VMEM((positions, part), BF)],
        compiler_params=params(),
        cost_estimate=cost(0, 4 * tokens.size),
        name="turn_shares",
    )(tokens)


def delayed(value, steps):
    if steps == 0:
        return value
    lane = lax.broadcasted_iota(jnp.int32, value.shape, 1)
    return jnp.where(lane < steps, 0.0, pltpu.roll(value, steps, 1))


def advanced(value, steps):
    if steps == 0:
        return value
    lanes = value.shape[1]
    lane = lax.broadcasted_iota(jnp.int32, value.shape, 1)
    return jnp.where(lane >= lanes - steps, 0.0, pltpu.roll(value, lanes - steps, 1))


def spectrum(value, residue, table):
    width = value.shape[1] // BLOCKS
    parts = [value[:, block * width : (block + 1) * width] for block in range(BLOCKS)]
    real = parts[0]
    imag = None
    for block in range(1, BLOCKS):
        angle = block_angle(residue, block)
        real = real + parts[block] * math.cos(angle)
        term = parts[block] * -math.sin(angle)
        imag = term if imag is None else imag + term
    result = matmul(jnp.concatenate([real, imag], axis=1).astype(BF), table, NN)
    steps = result.shape[1] // 4
    quarter = [result[:, i * steps : (i + 1) * steps] for i in range(4)]
    return jnp.concatenate([quarter[0], quarter[2]], axis=1), jnp.concatenate(
        [quarter[1], quarter[3]], axis=1
    )


def from_spectrum(real, imag, residue, table, totals):
    steps = real.shape[1] // 2
    value = jnp.concatenate(
        [real[:, :steps], imag[:, :steps], real[:, steps:], imag[:, steps:]], axis=1
    )
    result = matmul(value.astype(BF), table, NT)
    width = result.shape[1] // 2
    even, odd = result[:, :width], result[:, width:]
    for block in range(BLOCKS):
        angle = block_angle(residue, block)
        term = even if block == 0 else even * math.cos(angle) - odd * math.sin(angle)
        totals[block] = term if totals[block] is None else totals[block] + term


def operator_kernel(grad_scale, parts_ref, taps_ref, phase_ref, table_ref, grads_ref, out_ref, held_ref, sem):
    copy = pltpu.make_async_copy(table_ref, held_ref, sem)
    copy.start()
    sources, _, positions = parts_ref.shape
    block_len = out_ref.shape[2]
    chans = taps_ref.shape[0]
    streams = grads_ref.shape[0] // chans
    taps_len = (taps_ref.shape[1] - 1) // streams

    def tap(stream, pos):
        column = stream * taps_len + pos
        return taps_ref[:, column : column + 1]

    def summed(row):
        total = parts_ref[0, row : row + chans].astype(F32)
        for source in range(1, sources):
            total = total + parts_ref[source, row : row + chans].astype(F32)
        return total

    filtered = []
    for stream in range(streams):
        total = summed(stream * chans)
        acc = tap(stream, 0) * total
        for pos in range(1, taps_len):
            acc = acc + tap(stream, pos) * delayed(total, pos)
        filtered.append(acc)
    query, key, value = filtered
    skip = taps_ref[:, streams * taps_len : streams * taps_len + 1]
    edge = jnp.concatenate(
        [
            unfold(parts_ref[source, streams * chans :], block_len).astype(F32)
            for source in range(sources)
        ],
        axis=1,
    )
    cot, long_filter = edge[:chans], edge[chans:]
    gated = key * value
    d_conv = cot * query
    stacked = jnp.concatenate([gated, d_conv, long_filter], axis=0)
    rows = chans
    totals = [None] * BLOCKS
    copy.wait()
    for residue in range(BLOCKS):
        cos_all, sin_all = spectrum(stacked, residue, held_ref[residue])
        g_real, d_real, h_real = cos_all[:rows], cos_all[rows : 2 * rows], cos_all[2 * rows :]
        g_imag, d_imag, h_imag = sin_all[:rows], sin_all[rows : 2 * rows], sin_all[2 * rows :]
        cos_phase = phase_ref[2 * residue : 2 * residue + 1]
        sin_phase = phase_ref[2 * residue + 1 : 2 * residue + 2]
        f_real = h_real * cos_phase - h_imag * sin_phase
        f_imag = h_real * sin_phase + h_imag * cos_phase
        conv_real = g_real * f_real - g_imag * f_imag
        conv_imag = g_real * f_imag + g_imag * f_real
        back_real = f_real * d_real + f_imag * d_imag
        back_imag = f_real * d_imag - f_imag * d_real
        corr_real = g_real * d_real + g_imag * d_imag
        corr_imag = g_real * d_imag - g_imag * d_real
        lag_real = corr_real * cos_phase + corr_imag * sin_phase
        lag_imag = corr_imag * cos_phase - corr_real * sin_phase
        from_spectrum(
            jnp.concatenate([conv_real, back_real, lag_real], axis=0),
            jnp.concatenate([conv_imag, back_imag, lag_imag], axis=0),
            residue,
            held_ref[residue],
            totals,
        )
    result = jnp.concatenate(totals, axis=1)
    scale = 1.0 / positions
    conv_out = result[:rows] * scale + skip * gated
    d_gated = result[rows : 2 * rows] * scale + skip * d_conv
    filter_part = (result[2 * rows :] * (scale * grad_scale)).astype(BF)
    hyena_out = (query * conv_out).astype(BF)
    for block in range(sources):
        lanes = slice(block * block_len, (block + 1) * block_len)
        out_ref[block, :chans] = hyena_out[:, lanes]
        out_ref[block, chans:] = filter_part[:, lanes]
    for stream, grad in enumerate((cot * conv_out, d_gated * value, d_gated * key)):
        acc = tap(stream, 0) * grad
        for pos in range(1, taps_len):
            acc = acc + tap(stream, pos) * advanced(grad, pos)
        grads_ref[stream * chans : (stream + 1) * chans] = acc.astype(BF)


def operator(parts, taps, phase, table, grad_scale, streams, block_len):
    sources, _, positions = parts.shape
    chans = taps.shape[0]
    rows = streams * chans
    full = pl.BlockSpec(memory_space=pltpu.VMEM)
    return pl.pallas_call(
        functools.partial(operator_kernel, grad_scale),
        in_specs=[full, full, full, pl.BlockSpec(memory_space=pl.ANY)],
        out_shape=(kept((rows, positions)), kept((sources, 2 * chans, block_len))),
        scratch_shapes=[pltpu.VMEM(table.shape, BF), pltpu.SemaphoreType.DMA],
        compiler_params=params(40 << 20),
        cost_estimate=cost(8 * rows * positions * positions, 2 * (parts.size + table.size)),
        name="operator",
    )(parts, taps, phase, stay(table))


def near_kernel(weight_ref, out_ref, sem):
    copy = pltpu.make_async_copy(weight_ref, out_ref, sem)
    copy.start()
    copy.wait()


def near_weight(weight):
    return pl.pallas_call(
        near_kernel,
        in_specs=[pl.BlockSpec(memory_space=pltpu.HBM)],
        out_specs=pl.BlockSpec(memory_space=pltpu.VMEM),
        out_shape=pltpu.VMEM(weight.shape, weight.dtype),
        scratch_shapes=[pltpu.SemaphoreType.DMA],
        compiler_params=params(16 << 20),
        cost_estimate=cost(0, 4 * weight.size),
        name="near_weight",
    )(stay(weight))


def token_kernel(pos_ref, weight_ref, grads_ref, sent_ref, held_ref):
    streams, chips, _, rows, cols = weight_ref.shape
    part = sent_ref.shape[1]
    grads = [grads_ref[:, 0, stream].reshape(cols, part) for stream in range(streams)]
    lanes = pl.ds(pl.multiple_of(pl.program_id(0) * part, part), part)
    for own in (False, True):
        total = None
        side = pos_ref[1] if own else 1 - pos_ref[1]
        for stream in range(streams):
            weight = weight_ref[stream, :, pl.ds(side, 1)].reshape(chips * rows, cols)
            term = matmul(weight, grads[stream], NN)
            total = term if total is None else total + term
        if own:
            held_ref[:, lanes] = total.astype(BF)
        else:
            sent_ref[...] = total.astype(BF)


def token_part(pos, weight, grads):
    streams, chips, cores, rows, cols = weight.shape
    slabs, _, _, chans, positions = grads.shape
    part = positions // 4
    return pl.pallas_call(
        token_kernel,
        grid_spec=pltpu.PrefetchScalarGridSpec(
            num_scalar_prefetch=1,
            grid=(4,),
            in_specs=[
                pl.BlockSpec(memory_space=pltpu.VMEM),
                pl.BlockSpec((slabs, 1, streams, chans, part), lambda j, pos: (0, pos[0], 0, 0, j)),
            ],
            out_specs=[
                pl.BlockSpec((chips * rows, part), lambda j, pos: (0, j)),
                pl.BlockSpec(memory_space=pltpu.VMEM),
            ],
        ),
        out_shape=(kept((chips * rows, positions)), pltpu.VMEM((chips * rows, positions), BF)),
        compiler_params=params(40 << 20),
        cost_estimate=cost(2 * weight.size * positions, 8 * chips * rows * positions),
        name="token_part",
    )(pos, weight, stay(grads))


def pair_kernel(held_ref, received_ref, out_ref):
    out_ref[...] = (held_ref[...].astype(F32) + received_ref[...].astype(F32)).astype(BF)


def pair_sum(held, received):
    return pl.pallas_call(
        pair_kernel,
        in_specs=[pl.BlockSpec(memory_space=pltpu.VMEM)] * 2,
        out_shape=kept(held.shape),
        compiler_params=params(24 << 20),
        cost_estimate=cost(0, 6 * held.size),
        name="pair_sum",
    )(held, received)


def weight_kernel(grad_scale, pos_ref, own_ref, other_ref, own_grads_ref, other_grads_ref, out_ref):
    chan_cols = out_ref.shape[2]
    positions = own_ref.shape[1]
    own = own_grads_ref[...].reshape(chan_cols, positions)
    other = other_grads_ref[...].reshape(chan_cols, positions)
    total = matmul(own_ref[...], own, NT) + matmul(other_ref[...], other, NT)
    out_ref[0] = (total * grad_scale).astype(BF)


def weight_grad(pos, own, other, grads, grad_scale):
    slabs, _, streams, chans, positions = grads.shape
    slab_rows = own.shape[0]
    chan_cols = slabs * chans
    block = (slabs, 1, 1, chans, positions)
    return pl.pallas_call(
        functools.partial(weight_kernel, grad_scale),
        grid_spec=pltpu.PrefetchScalarGridSpec(
            num_scalar_prefetch=1,
            grid=(streams,),
            in_specs=[
                pl.BlockSpec(own.shape, lambda i, pos: (0, 0)),
                pl.BlockSpec(own.shape, lambda i, pos: (0, 0)),
                pl.BlockSpec(block, lambda i, pos: (0, pos[0], i, 0, 0)),
                pl.BlockSpec(block, lambda i, pos: (0, 1 - pos[0], i, 0, 0)),
            ],
            out_specs=pl.BlockSpec((1, slab_rows, chan_cols), lambda i, pos: (i, 0, 0)),
        ),
        out_shape=jax.ShapeDtypeStruct((streams, slab_rows, chan_cols), BF),
        compiler_params=params(),
        cost_estimate=cost(
            4 * streams * slab_rows * chan_cols * positions,
            2 * (2 * own.size + grads.size + streams * slab_rows * chan_cols),
        ),
        name="weight_grad",
    )(pos, own, other, grads, grads)


def total_kernel(parts_ref, out_ref):
    total = parts_ref[0].astype(F32)
    for pos in range(1, parts_ref.shape[0]):
        total = total + parts_ref[pos].astype(F32)
    out_ref[0] = jnp.transpose(total).astype(BF)


def token_total(parts):
    _, rows, positions = parts.shape
    return pl.pallas_call(
        total_kernel,
        out_shape=jax.ShapeDtypeStruct((1, positions, rows), BF),
        compiler_params=params(24 << 20),
        cost_estimate=cost(0, 2 * parts.size),
        name="token_total",
    )(parts)


def finish_kernel(own_ref, other_ref, out_ref, filter_ref):
    slabs, rows, block_len = own_ref.shape
    chans = rows // 2
    hyena = own_ref[:, :chans].astype(F32).reshape(slabs * chans, block_len)
    filters = own_ref[:, chans:].astype(F32) + other_ref[...].astype(F32)
    out_ref[0] = jnp.transpose(hyena).astype(BF)
    filter_ref[...] = jnp.transpose(filters.reshape(slabs * chans, block_len))


def finish(own, other):
    slabs, rows, block_len = own.shape
    chan_cols = slabs * rows // 2
    return pl.pallas_call(
        finish_kernel,
        out_shape=(
            jax.ShapeDtypeStruct((1, block_len, chan_cols), BF),
            jax.ShapeDtypeStruct((block_len, chan_cols), F32),
        ),
        compiler_params=params(24 << 20),
        cost_estimate=cost(0, 4 * own.size),
        name="finish",
    )(own, other)


def exchange(value, axis, groups=None):
    return lax.all_to_all(
        value, axis, split_axis=0, concat_axis=0, tiled=True, axis_index_groups=groups
    )


def local(tokens, in_weight, short_taps, long_filter, skip_gain, cotangent):
    seq_count = lax.axis_size("seq")
    dp_count = lax.axis_size("dp")
    dp_pos = lax.axis_index("dp").astype(jnp.int32)
    seq_pos = lax.axis_index("seq").astype(jnp.int32)
    chan_count = lax.axis_size("chan")
    chan_pos = lax.axis_index("chan").astype(jnp.int32)
    core = chan_pos % 2
    pos = jnp.stack([dp_pos, core])
    tok_rows = tokens.shape[1]
    slab_rows = in_weight.shape[0]
    chan_cols = in_weight.shape[2]
    streams, taps_len = short_taps.shape[:2]
    positions = seq_count * tok_rows
    chans = chan_cols // seq_count
    half = tok_rows // 2
    share = tok_rows // chan_count
    chips = chan_count // 2
    grad_scale = 1.0 / math.sqrt(dp_count * positions)
    batches = [(0, 1), (1, 0)]
    cores = [(i, i ^ 1) for i in range(chan_count)]
    weight = jnp.transpose(in_weight, (1, 0, 2))

    mine, edge, flipped = lax.optimization_barrier(
        (
            exchange(cut_tokens(core[None], tokens, seq_count), "seq"),
            edge_rows(cotangent, long_filter, seq_count, positions),
            flip_weight(weight),
        )
    )
    theirs = lax.ppermute(mine, "chan", cores)
    parts = project(pos, mine, theirs, flipped, edge)

    shares = lax.dynamic_slice_in_dim(mine, chan_pos // 2 * share, share, 1)
    shares = lax.ppermute(shares, "dp", batches)
    parts, shares, short_taps = lax.optimization_barrier((parts, shares, short_taps))
    shares = lax.all_gather(shares, "chan", axis=0)
    shares = shares.reshape(chips, 2, seq_count, share, slab_rows)
    taps = jnp.concatenate([short_taps.reshape(streams * taps_len, chan_cols), skip_gain[None]])
    taps = jnp.transpose(lax.dynamic_slice_in_dim(taps, seq_pos * chans, chans, 1))
    table, phase = transform_tables(positions)
    parts, taps = lax.optimization_barrier((exchange(parts, "seq"), taps))

    grads, outs = operator(parts, taps, phase, table, grad_scale, streams, tok_rows)
    grads, shares, mine, theirs = lax.optimization_barrier((grads, shares, mine, theirs))
    grads = lax.all_gather(grads, ("seq", "dp"), axis=0)
    outs = exchange(outs, "seq")
    finished = finish(outs, lax.ppermute(outs[:, chans:], "dp", batches))
    own, other, near, finished = lax.optimization_barrier(
        (
            turn_tokens(pos, mine, theirs),
            turn_shares(shares),
            weight.reshape(streams, chips, 2, slab_rows // chan_count, chan_cols),
            finished,
        )
    )
    near = near_weight(near)
    grads, finished, own, other = lax.optimization_barrier((grads, finished, own, other))
    hyena_out, grad_filter = finished

    grads = grads.reshape(seq_count, dp_count, streams, chans, positions)
    sent, held = token_part(pos, near, grads)
    token_block = pair_sum(held, lax.ppermute(sent, "chan", cores))
    token_block = exchange(
        token_block.reshape(chips, -1, positions),
        "chan",
        [[chip * 2 + side for chip in range(chips)] for side in range(2)],
    )
    grad_tokens = token_total(token_block)
    grad_weight = weight_grad(pos, own, other, grads, grad_scale)
    return (hyena_out, grad_tokens, jnp.transpose(grad_weight, (1, 0, 2)), grad_filter)


def solution(mesh):
    placed = (
        P("dp", "seq", None),
        P("seq", None, "chan"),
        P(None, None, "chan"),
        P("seq", "chan"),
        P("chan"),
        P("dp", "seq", "chan"),
    )
    return jax.shard_map(
        local,
        mesh=mesh,
        in_specs=placed,
        out_specs=(
            P("dp", "seq", "chan"),
            P("dp", None, ("seq", "chan")),
            P("seq", None, "chan"),
            P("seq", "chan"),
        ),
        check_vma=False,
    )
```

```python
import functools
import math

import jax
import jax.numpy as jnp
import numpy as np
from jax import lax
from jax.experimental import pallas as pl
from jax.experimental.pallas import tpu as pltpu
from jax.sharding import PartitionSpec as P

BF = jnp.bfloat16
F32 = jnp.float32
VMEM_BYTES = 60 << 20
NT = (((1,), (1,)), ((), ()))
NN = (((1,), (0,)), ((), ()))


def params(limit=VMEM_BYTES):
    return pltpu.CompilerParams(vmem_limit_bytes=limit)


def cost(flops, bytes_accessed):
    return pl.CostEstimate(flops=flops, bytes_accessed=bytes_accessed, transcendentals=0)


def kept(shape, dtype=BF):
    return pltpu.HBM(shape, dtype)


def stay(value):
    return pltpu.with_memory_space_constraint(value, pltpu.HBM)


def matmul(left, right, dims):
    return lax.dot_general(left, right, dims, preferred_element_type=F32)


def split(value):
    high = value.astype(BF)
    return high, (value - high.astype(F32)).astype(BF)


def edge_kernel(cot_ref, filter_ref, out_ref):
    slabs = out_ref.shape[0]
    chans = filter_ref.shape[1] // slabs
    taps = jnp.transpose(filter_ref[...]).astype(BF)
    cot = jnp.transpose(cot_ref[0].astype(F32)).astype(BF)
    for slab in range(slabs):
        part = slice(slab * chans, (slab + 1) * chans)
        fold(out_ref.at[slab], 0, jnp.concatenate([cot[part], taps[part]], axis=0))


def fold(out_ref, first, value):
    rows, block_len = value.shape
    count = rows * block_len // out_ref.shape[1]
    for pos in range(rows // count):
        out_ref[first : first + count, pos * block_len : (pos + 1) * block_len] = value[
            pos * count : (pos + 1) * count
        ]


def unfold(value, block_len):
    return jnp.concatenate(
        [value[:, at : at + block_len] for at in range(0, value.shape[1], block_len)], axis=0
    )


def edge_rows(cotangent, long_filter, slabs, lanes):
    _, tok_rows, chan_cols = cotangent.shape
    full = pl.BlockSpec(memory_space=pltpu.VMEM)
    return pl.pallas_call(
        edge_kernel,
        in_specs=[full, full],
        out_shape=kept((slabs, 2 * tok_rows * chan_cols // slabs // lanes, lanes)),
        compiler_params=params(),
        cost_estimate=cost(0, 8 * tok_rows * chan_cols),
        name="edge_rows",
    )(cotangent, long_filter)


def flip_kernel(weight_ref, out_ref):
    out_ref[0] = jnp.transpose(weight_ref[0])


def flip_weight(weight):
    streams, slab_rows, chan_cols = weight.shape
    half = chan_cols // 2
    return pl.pallas_call(
        flip_kernel,
        grid=(streams, 2),
        in_specs=[pl.BlockSpec((1, slab_rows, half), lambda i, j: (i, 0, j))],
        out_specs=pl.BlockSpec((1, half, slab_rows), lambda i, j: (i, j, 0)),
        out_shape=kept((streams, chan_cols, slab_rows)),
        compiler_params=params(),
        cost_estimate=cost(0, 4 * weight.size),
        name="flip_weight",
    )(weight)


BLOCKS = 4


def block_angle(residue, block):
    return math.pi * (2 * residue + 1) * block / (2 * BLOCKS)


def frequencies(count, residue):
    steps = 2 * BLOCKS * np.arange(count // (2 * BLOCKS))
    return steps + residue, steps + 2 * BLOCKS - 1 - residue


def transform_tables(count):
    width = count // BLOCKS
    tables, phases = [], []
    for residue in range(BLOCKS):
        columns, rows = [], []
        for side, freq in zip((1.0, -1.0), frequencies(count, residue)):
            angles = math.pi / (4 * count) * (2 * np.arange(width)[:, None] + 1) * (2 * freq[None] + 1)
            cos, sin = np.cos(angles), np.sin(angles)
            columns += [np.concatenate([cos, side * sin]), np.concatenate([-sin, side * cos])]
            rows.append(math.pi / (4 * count) * (2 * freq + 1))
        tables.append(np.concatenate(columns, axis=1))
        rows = np.concatenate(rows)
        phases += [np.cos(rows), np.sin(rows)]
    return jnp.asarray(np.stack(tables), BF), jnp.asarray(np.stack(phases), F32)


def cut_kernel(core_ref, tokens_ref, out_ref, held_ref, in_sems, out_sems):
    slabs, half, width = held_ref.shape
    start = pl.multiple_of(core_ref[0] * half, half)
    inward = [
        pltpu.make_async_copy(
            tokens_ref.at[0, pl.ds(start, half), slice(slab * width, (slab + 1) * width)],
            held_ref.at[slab],
            in_sems.at[slab],
        )
        for slab in range(slabs)
    ]
    outward = [
        pltpu.make_async_copy(held_ref.at[slab], out_ref.at[slab], out_sems.at[slab])
        for slab in range(slabs)
    ]
    for copy in inward:
        copy.start()
    for slab in range(slabs):
        inward[slab].wait()
        outward[slab].start()
    for copy in outward:
        copy.wait()


def cut_tokens(core, tokens, slabs):
    _, rows, width = tokens.shape
    dims = (slabs, rows // 2, width // slabs)
    return pl.pallas_call(
        cut_kernel,
        in_specs=[pl.BlockSpec(memory_space=pltpu.SMEM), pl.BlockSpec(memory_space=pltpu.HBM)],
        out_specs=pl.BlockSpec(memory_space=pltpu.HBM),
        out_shape=kept(dims),
        scratch_shapes=[
            pltpu.VMEM(dims, BF),
            pltpu.SemaphoreType.DMA((slabs,)),
            pltpu.SemaphoreType.DMA((slabs,)),
        ],
        compiler_params=params(),
        cost_estimate=cost(0, 2 * tokens.size),
        name="cut_tokens",
    )(core, stay(tokens))


def in_order(core, mine_ref, theirs_ref, spread_ref):
    blocks, half, _ = mine_ref.shape
    for block in range(blocks):
        base = 2 * block * half
        spread_ref[pl.ds(pl.multiple_of(base + core * half, half), half)] = mine_ref[block]
        spread_ref[pl.ds(pl.multiple_of(base + (1 - core) * half, half), half)] = theirs_ref[block]


def project_kernel(pos_ref, mine_ref, theirs_ref, weight_ref, edge_ref, out_ref, spread_ref):
    step = pl.program_id(0)
    last = pl.num_programs(0) - 1

    @pl.when(step == 0)
    def _():
        in_order(pos_ref[1], mine_ref, theirs_ref, spread_ref)

    @pl.when(step < last)
    def _():
        result = matmul(weight_ref[0], spread_ref[...], NT).astype(BF)
        out_ref[...] = result.reshape(out_ref.shape)

    @pl.when(step == last)
    def _():
        out_ref[:, : edge_ref.shape[1]] = edge_ref[...]


def project(pos, mine, theirs, weight, edge):
    blocks, half, width = mine.shape
    streams, rows, _ = weight.shape
    slabs, edge_len, positions = edge.shape
    chans = rows // slabs
    return pl.pallas_call(
        project_kernel,
        grid_spec=pltpu.PrefetchScalarGridSpec(
            num_scalar_prefetch=1,
            grid=(streams + 1,),
            in_specs=[
                pl.BlockSpec(memory_space=pltpu.VMEM),
                pl.BlockSpec(memory_space=pltpu.VMEM),
                pl.BlockSpec((1, rows, width), lambda i, pos: (jnp.minimum(i, streams - 1), 0, 0)),
                pl.BlockSpec(edge.shape, lambda i, pos: (0, 0, 0)),
            ],
            out_specs=pl.BlockSpec((slabs, chans, positions), lambda i, pos: (0, i, 0)),
            scratch_shapes=[pltpu.VMEM((positions, width), BF)],
        ),
        out_shape=kept((slabs, streams * chans + edge_len, positions)),
        compiler_params=params(36 << 20),
        cost_estimate=cost(
            2 * positions * width * streams * rows,
            2 * (positions * width + weight.size + positions * streams * rows),
        ),
        name="project",
    )(pos, mine, theirs, stay(weight), stay(edge))


def turn_kernel(pos_ref, mine_ref, theirs_ref, out_ref, spread_ref):
    in_order(pos_ref[1], mine_ref, theirs_ref, spread_ref)
    out_ref[...] = jnp.transpose(spread_ref[...])


def turn_tokens(pos, mine, theirs):
    blocks, half, width = mine.shape
    positions = 2 * blocks * half
    part = width // 4
    block = pl.BlockSpec((blocks, half, part), lambda i, pos: (0, 0, i))
    return pl.pallas_call(
        turn_kernel,
        grid_spec=pltpu.PrefetchScalarGridSpec(
            num_scalar_prefetch=1,
            grid=(4,),
            in_specs=[block, block],
            out_specs=pl.BlockSpec((part, positions), lambda i, pos: (i, 0)),
            scratch_shapes=[pltpu.VMEM((positions, part), BF)],
        ),
        out_shape=kept((width, positions)),
        compiler_params=params(),
        cost_estimate=cost(0, 4 * positions * width),
        name="turn_tokens",
    )(pos, mine, theirs)


def turn_shares_kernel(tokens_ref, out_ref, spread_ref):
    chips, cores, blocks, rows, _ = tokens_ref.shape
    for block in range(blocks):
        for core in range(cores):
            for chip in range(chips):
                base = ((block * cores + core) * chips + chip) * rows
                spread_ref[base : base + rows] = tokens_ref[chip, core, block]
    out_ref[...] = jnp.transpose(spread_ref[...])


def turn_shares(tokens):
    chips, cores, blocks, rows, width = tokens.shape
    positions = chips * cores * blocks * rows
    part = width // 4
    return pl.pallas_call(
        turn_shares_kernel,
        grid=(4,),
        in_specs=[pl.BlockSpec((chips, cores, blocks, rows, part), lambda i: (0, 0, 0, 0, i))],
        out_specs=pl.BlockSpec((part, positions), lambda i: (i, 0)),
        out_shape=kept((width, positions)),
        scratch_shapes=[pltpu.VMEM((positions, part), BF)],
        compiler_params=params(),
        cost_estimate=cost(0, 4 * tokens.size),
        name="turn_shares",
    )(tokens)


def delayed(value, steps):
    if steps == 0:
        return value
    lane = lax.broadcasted_iota(jnp.int32, value.shape, 1)
    return jnp.where(lane < steps, 0.0, pltpu.roll(value, steps, 1))


def advanced(value, steps):
    if steps == 0:
        return value
    lanes = value.shape[1]
    lane = lax.broadcasted_iota(jnp.int32, value.shape, 1)
    return jnp.where(lane >= lanes - steps, 0.0, pltpu.roll(value, lanes - steps, 1))


def two_part(value, table, dims):
    rows = value.shape[0]
    result = matmul(jnp.concatenate(split(value), axis=0), table, dims)
    return result[:rows] + result[rows:]


def spectrum(value, residue, table):
    width = value.shape[1] // BLOCKS
    parts = [value[:, block * width : (block + 1) * width] for block in range(BLOCKS)]
    real = parts[0]
    imag = None
    for block in range(1, BLOCKS):
        angle = block_angle(residue, block)
        real = real + parts[block] * math.cos(angle)
        term = parts[block] * -math.sin(angle)
        imag = term if imag is None else imag + term
    result = two_part(jnp.concatenate([real, imag], axis=1), table, NN)
    steps = result.shape[1] // 4
    quarter = [result[:, i * steps : (i + 1) * steps] for i in range(4)]
    return jnp.concatenate([quarter[0], quarter[2]], axis=1), jnp.concatenate(
        [quarter[1], quarter[3]], axis=1
    )


def from_spectrum(real, imag, residue, table, totals):
    steps = real.shape[1] // 2
    value = jnp.concatenate(
        [real[:, :steps], imag[:, :steps], real[:, steps:], imag[:, steps:]], axis=1
    )
    result = two_part(value, table, NT)
    width = result.shape[1] // 2
    even, odd = result[:, :width], result[:, width:]
    for block in range(BLOCKS):
        angle = block_angle(residue, block)
        term = even if block == 0 else even * math.cos(angle) - odd * math.sin(angle)
        totals[block] = term if totals[block] is None else totals[block] + term


def operator_kernel(grad_scale, parts_ref, taps_ref, phase_ref, table_ref, grads_ref, out_ref, held_ref, sem):
    copy = pltpu.make_async_copy(table_ref, held_ref, sem)
    copy.start()
    sources, _, positions = parts_ref.shape
    block_len = out_ref.shape[2]
    chans = taps_ref.shape[0]
    streams = grads_ref.shape[0] // chans
    taps_len = (taps_ref.shape[1] - 1) // streams

    def tap(stream, pos):
        column = stream * taps_len + pos
        return taps_ref[:, column : column + 1]

    def summed(row):
        total = parts_ref[0, row : row + chans].astype(F32)
        for source in range(1, sources):
            total = total + parts_ref[source, row : row + chans].astype(F32)
        return total

    filtered = []
    for stream in range(streams):
        total = summed(stream * chans)
        acc = tap(stream, 0) * total
        for pos in range(1, taps_len):
            acc = acc + tap(stream, pos) * delayed(total, pos)
        filtered.append(acc)
    query, key, value = filtered
    skip = taps_ref[:, streams * taps_len : streams * taps_len + 1]
    edge = jnp.concatenate(
        [
            unfold(parts_ref[source, streams * chans :], block_len).astype(F32)
            for source in range(sources)
        ],
        axis=1,
    )
    cot, long_filter = edge[:chans], edge[chans:]
    gated = key * value
    d_conv = cot * query
    stacked = jnp.concatenate([gated, d_conv, long_filter], axis=0)
    rows = chans
    totals = [None] * BLOCKS
    copy.wait()
    for residue in range(BLOCKS):
        cos_all, sin_all = spectrum(stacked, residue, held_ref[residue])
        g_real, d_real, h_real = cos_all[:rows], cos_all[rows : 2 * rows], cos_all[2 * rows :]
        g_imag, d_imag, h_imag = sin_all[:rows], sin_all[rows : 2 * rows], sin_all[2 * rows :]
        cos_phase = phase_ref[2 * residue : 2 * residue + 1]
        sin_phase = phase_ref[2 * residue + 1 : 2 * residue + 2]
        f_real = h_real * cos_phase - h_imag * sin_phase
        f_imag = h_real * sin_phase + h_imag * cos_phase
        conv_real = g_real * f_real - g_imag * f_imag
        conv_imag = g_real * f_imag + g_imag * f_real
        back_real = f_real * d_real + f_imag * d_imag
        back_imag = f_real * d_imag - f_imag * d_real
        corr_real = g_real * d_real + g_imag * d_imag
        corr_imag = g_real * d_imag - g_imag * d_real
        lag_real = corr_real * cos_phase + corr_imag * sin_phase
        lag_imag = corr_imag * cos_phase - corr_real * sin_phase
        from_spectrum(
            jnp.concatenate([conv_real, back_real, lag_real], axis=0),
            jnp.concatenate([conv_imag, back_imag, lag_imag], axis=0),
            residue,
            held_ref[residue],
            totals,
        )
    result = jnp.concatenate(totals, axis=1)
    scale = 1.0 / positions
    conv_out = result[:rows] * scale + skip * gated
    d_gated = result[rows : 2 * rows] * scale + skip * d_conv
    filter_part = (result[2 * rows :] * (scale * grad_scale)).astype(BF)
    hyena_out = (query * conv_out).astype(BF)
    for block in range(sources):
        lanes = slice(block * block_len, (block + 1) * block_len)
        out_ref[block, :chans] = hyena_out[:, lanes]
        out_ref[block, chans:] = filter_part[:, lanes]
    for stream, grad in enumerate((cot * conv_out, d_gated * value, d_gated * key)):
        acc = tap(stream, 0) * grad
        for pos in range(1, taps_len):
            acc = acc + tap(stream, pos) * advanced(grad, pos)
        grads_ref[stream * chans : (stream + 1) * chans] = acc.astype(BF)


def operator(parts, taps, phase, table, grad_scale, streams, block_len):
    sources, _, positions = parts.shape
    chans = taps.shape[0]
    rows = streams * chans
    full = pl.BlockSpec(memory_space=pltpu.VMEM)
    return pl.pallas_call(
        functools.partial(operator_kernel, grad_scale),
        in_specs=[full, full, full, pl.BlockSpec(memory_space=pl.ANY)],
        out_shape=(kept((rows, positions)), kept((sources, 2 * chans, block_len))),
        scratch_shapes=[pltpu.VMEM(table.shape, BF), pltpu.SemaphoreType.DMA],
        compiler_params=params(40 << 20),
        cost_estimate=cost(8 * rows * positions * positions, 2 * (parts.size + table.size)),
        name="operator",
    )(parts, taps, phase, stay(table))


def near_kernel(weight_ref, out_ref, sem):
    copy = pltpu.make_async_copy(weight_ref, out_ref, sem)
    copy.start()
    copy.wait()


def near_weight(weight):
    return pl.pallas_call(
        near_kernel,
        in_specs=[pl.BlockSpec(memory_space=pltpu.HBM)],
        out_specs=pl.BlockSpec(memory_space=pltpu.VMEM),
        out_shape=pltpu.VMEM(weight.shape, weight.dtype),
        scratch_shapes=[pltpu.SemaphoreType.DMA],
        compiler_params=params(16 << 20),
        cost_estimate=cost(0, 4 * weight.size),
        name="near_weight",
    )(stay(weight))


def token_kernel(pos_ref, weight_ref, grads_ref, sent_ref, held_ref):
    streams, chips, _, rows, cols = weight_ref.shape
    part = sent_ref.shape[1]
    grads = [grads_ref[:, 0, stream].reshape(cols, part) for stream in range(streams)]
    lanes = pl.ds(pl.multiple_of(pl.program_id(0) * part, part), part)
    for own in (False, True):
        total = None
        side = pos_ref[1] if own else 1 - pos_ref[1]
        for stream in range(streams):
            weight = weight_ref[stream, :, pl.ds(side, 1)].reshape(chips * rows, cols)
            term = matmul(weight, grads[stream], NN)
            total = term if total is None else total + term
        if own:
            held_ref[:, lanes] = total.astype(BF)
        else:
            sent_ref[...] = total.astype(BF)


def token_part(pos, weight, grads):
    streams, chips, cores, rows, cols = weight.shape
    slabs, _, _, chans, positions = grads.shape
    part = positions // 2
    return pl.pallas_call(
        token_kernel,
        grid_spec=pltpu.PrefetchScalarGridSpec(
            num_scalar_prefetch=1,
            grid=(2,),
            in_specs=[
                pl.BlockSpec(memory_space=pltpu.VMEM),
                pl.BlockSpec((slabs, 1, streams, chans, part), lambda j, pos: (0, pos[0], 0, 0, j)),
            ],
            out_specs=[
                pl.BlockSpec((chips * rows, part), lambda j, pos: (0, j)),
                pl.BlockSpec(memory_space=pltpu.VMEM),
            ],
        ),
        out_shape=(kept((chips * rows, positions)), pltpu.VMEM((chips * rows, positions), BF)),
        compiler_params=params(40 << 20),
        cost_estimate=cost(2 * weight.size * positions, 8 * chips * rows * positions),
        name="token_part",
    )(pos, weight, stay(grads))


def pair_kernel(held_ref, received_ref, out_ref):
    out_ref[...] = (held_ref[...].astype(F32) + received_ref[...].astype(F32)).astype(BF)


def pair_sum(held, received):
    return pl.pallas_call(
        pair_kernel,
        in_specs=[pl.BlockSpec(memory_space=pltpu.VMEM)] * 2,
        out_shape=kept(held.shape),
        compiler_params=params(24 << 20),
        cost_estimate=cost(0, 6 * held.size),
        name="pair_sum",
    )(held, received)


def weight_kernel(grad_scale, pos_ref, own_ref, other_ref, own_grads_ref, other_grads_ref, out_ref):
    chan_cols = out_ref.shape[2]
    positions = own_ref.shape[1]
    own = own_grads_ref[...].reshape(chan_cols, positions)
    other = other_grads_ref[...].reshape(chan_cols, positions)
    total = matmul(own_ref[...], own, NT) + matmul(other_ref[...], other, NT)
    out_ref[0] = (total * grad_scale).astype(BF)


def weight_grad(pos, own, other, grads, grad_scale):
    slabs, _, streams, chans, positions = grads.shape
    slab_rows = own.shape[0]
    chan_cols = slabs * chans
    block = (slabs, 1, 1, chans, positions)
    return pl.pallas_call(
        functools.partial(weight_kernel, grad_scale),
        grid_spec=pltpu.PrefetchScalarGridSpec(
            num_scalar_prefetch=1,
            grid=(streams,),
            in_specs=[
                pl.BlockSpec(own.shape, lambda i, pos: (0, 0)),
                pl.BlockSpec(own.shape, lambda i, pos: (0, 0)),
                pl.BlockSpec(block, lambda i, pos: (0, pos[0], i, 0, 0)),
                pl.BlockSpec(block, lambda i, pos: (0, 1 - pos[0], i, 0, 0)),
            ],
            out_specs=pl.BlockSpec((1, slab_rows, chan_cols), lambda i, pos: (i, 0, 0)),
        ),
        out_shape=jax.ShapeDtypeStruct((streams, slab_rows, chan_cols), BF),
        compiler_params=params(),
        cost_estimate=cost(
            4 * streams * slab_rows * chan_cols * positions,
            2 * (2 * own.size + grads.size + streams * slab_rows * chan_cols),
        ),
        name="weight_grad",
    )(pos, own, other, grads, grads)


def total_kernel(parts_ref, out_ref):
    total = parts_ref[0].astype(F32)
    for pos in range(1, parts_ref.shape[0]):
        total = total + parts_ref[pos].astype(F32)
    out_ref[0] = jnp.transpose(total).astype(BF)


def token_total(parts):
    _, rows, positions = parts.shape
    return pl.pallas_call(
        total_kernel,
        out_shape=jax.ShapeDtypeStruct((1, positions, rows), BF),
        compiler_params=params(24 << 20),
        cost_estimate=cost(0, 2 * parts.size),
        name="token_total",
    )(parts)


def finish_kernel(own_ref, other_ref, out_ref, filter_ref):
    slabs, rows, block_len = own_ref.shape
    chans = rows // 2
    hyena = own_ref[:, :chans].astype(F32).reshape(slabs * chans, block_len)
    filters = own_ref[:, chans:].astype(F32) + other_ref[...].astype(F32)
    out_ref[0] = jnp.transpose(hyena).astype(BF)
    filter_ref[...] = jnp.transpose(filters.reshape(slabs * chans, block_len))


def finish(own, other):
    slabs, rows, block_len = own.shape
    chan_cols = slabs * rows // 2
    return pl.pallas_call(
        finish_kernel,
        out_shape=(
            jax.ShapeDtypeStruct((1, block_len, chan_cols), BF),
            jax.ShapeDtypeStruct((block_len, chan_cols), F32),
        ),
        compiler_params=params(24 << 20),
        cost_estimate=cost(0, 4 * own.size),
        name="finish",
    )(own, other)


def exchange(value, axis, groups=None):
    return lax.all_to_all(
        value, axis, split_axis=0, concat_axis=0, tiled=True, axis_index_groups=groups
    )


def local(tokens, in_weight, short_taps, long_filter, skip_gain, cotangent):
    seq_count = lax.axis_size("seq")
    dp_count = lax.axis_size("dp")
    dp_pos = lax.axis_index("dp").astype(jnp.int32)
    seq_pos = lax.axis_index("seq").astype(jnp.int32)
    chan_count = lax.axis_size("chan")
    chan_pos = lax.axis_index("chan").astype(jnp.int32)
    core = chan_pos % 2
    pos = jnp.stack([dp_pos, core])
    tok_rows = tokens.shape[1]
    slab_rows = in_weight.shape[0]
    chan_cols = in_weight.shape[2]
    streams, taps_len = short_taps.shape[:2]
    positions = seq_count * tok_rows
    chans = chan_cols // seq_count
    half = tok_rows // 2
    share = tok_rows // chan_count
    chips = chan_count // 2
    grad_scale = 1.0 / math.sqrt(dp_count * positions)
    batches = [(0, 1), (1, 0)]
    cores = [(i, i ^ 1) for i in range(chan_count)]
    weight = jnp.transpose(in_weight, (1, 0, 2))

    mine, edge, flipped = lax.optimization_barrier(
        (
            exchange(cut_tokens(core[None], tokens, seq_count), "seq"),
            edge_rows(cotangent, long_filter, seq_count, positions),
            flip_weight(weight),
        )
    )
    theirs = lax.ppermute(mine, "chan", cores)
    parts = project(pos, mine, theirs, flipped, edge)

    shares = lax.dynamic_slice_in_dim(mine, chan_pos // 2 * share, share, 1)
    shares = lax.ppermute(shares, "dp", batches)
    parts, shares, short_taps = lax.optimization_barrier((parts, shares, short_taps))
    shares = lax.all_gather(shares, "chan", axis=0)
    shares = shares.reshape(chips, 2, seq_count, share, slab_rows)
    taps = jnp.concatenate([short_taps.reshape(streams * taps_len, chan_cols), skip_gain[None]])
    taps = jnp.transpose(lax.dynamic_slice_in_dim(taps, seq_pos * chans, chans, 1))
    table, phase = transform_tables(positions)
    parts, taps = lax.optimization_barrier((exchange(parts, "seq"), taps))

    grads, outs = operator(parts, taps, phase, table, grad_scale, streams, tok_rows)
    grads, shares, mine, theirs = lax.optimization_barrier((grads, shares, mine, theirs))
    grads = lax.all_gather(grads, ("seq", "dp"), axis=0)
    outs = exchange(outs, "seq")
    finished = finish(outs, lax.ppermute(outs[:, chans:], "dp", batches))
    own, other, near, finished = lax.optimization_barrier(
        (
            turn_tokens(pos, mine, theirs),
            turn_shares(shares),
            weight.reshape(streams, chips, 2, slab_rows // chan_count, chan_cols),
            finished,
        )
    )
    near = near_weight(near)
    grads, finished, own, other = lax.optimization_barrier((grads, finished, own, other))
    hyena_out, grad_filter = finished

    grads = grads.reshape(seq_count, dp_count, streams, chans, positions)
    sent, held = token_part(pos, near, grads)
    token_block = pair_sum(held, lax.ppermute(sent, "chan", cores))
    token_block = exchange(
        token_block.reshape(chips, -1, positions),
        "chan",
        [[chip * 2 + side for chip in range(chips)] for side in range(2)],
    )
    grad_tokens = token_total(token_block)
    grad_weight = weight_grad(pos, own, other, grads, grad_scale)
    return (hyena_out, grad_tokens, jnp.transpose(grad_weight, (1, 0, 2)), grad_filter)


def solution(mesh):
    placed = (
        P("dp", "seq", None),
        P("seq", None, "chan"),
        P(None, None, "chan"),
        P("seq", "chan"),
        P("chan"),
        P("dp", "seq", "chan"),
    )
    return jax.shard_map(
        local,
        mesh=mesh,
        in_specs=placed,
        out_specs=(
            P("dp", "seq", "chan"),
            P("dp", None, ("seq", "chan")),
            P("seq", None, "chan"),
            P("seq", "chan"),
        ),
        check_vma=False,
    )
```

```python
import functools
import math

import jax
import jax.numpy as jnp
import numpy as np
from jax import lax
from jax.experimental import pallas as pl
from jax.experimental.pallas import tpu as pltpu
from jax.sharding import PartitionSpec as P

BF = jnp.bfloat16
F32 = jnp.float32
VMEM_BYTES = 60 << 20
NT = (((1,), (1,)), ((), ()))
NN = (((1,), (0,)), ((), ()))


def params(limit=VMEM_BYTES):
    return pltpu.CompilerParams(vmem_limit_bytes=limit)


def cost(flops, bytes_accessed):
    return pl.CostEstimate(flops=flops, bytes_accessed=bytes_accessed, transcendentals=0)


def kept(shape, dtype=BF):
    return pltpu.HBM(shape, dtype)


def stay(value):
    return pltpu.with_memory_space_constraint(value, pltpu.HBM)


def matmul(left, right, dims):
    return lax.dot_general(left, right, dims, preferred_element_type=F32)


def split(value):
    high = value.astype(BF)
    return high, (value - high.astype(F32)).astype(BF)


def edge_kernel(cot_ref, filter_ref, out_ref):
    slabs = out_ref.shape[0]
    chans = filter_ref.shape[1] // slabs
    taps = jnp.transpose(filter_ref[...]).astype(BF)
    cot = jnp.transpose(cot_ref[0].astype(F32)).astype(BF)
    for slab in range(slabs):
        part = slice(slab * chans, (slab + 1) * chans)
        fold(out_ref.at[slab], 0, jnp.concatenate([cot[part], taps[part]], axis=0))


def fold(out_ref, first, value):
    rows, block_len = value.shape
    count = rows * block_len // out_ref.shape[1]
    for pos in range(rows // count):
        out_ref[first : first + count, pos * block_len : (pos + 1) * block_len] = value[
            pos * count : (pos + 1) * count
        ]


def unfold(value, block_len):
    return jnp.concatenate(
        [value[:, at : at + block_len] for at in range(0, value.shape[1], block_len)], axis=0
    )


def edge_rows(cotangent, long_filter, slabs, lanes):
    _, tok_rows, chan_cols = cotangent.shape
    full = pl.BlockSpec(memory_space=pltpu.VMEM)
    return pl.pallas_call(
        edge_kernel,
        in_specs=[full, full],
        out_shape=kept((slabs, 2 * tok_rows * chan_cols // slabs // lanes, lanes)),
        compiler_params=params(),
        cost_estimate=cost(0, 8 * tok_rows * chan_cols),
        name="edge_rows",
    )(cotangent, long_filter)


def flip_kernel(weight_ref, out_ref):
    out_ref[0] = jnp.transpose(weight_ref[0])


def flip_weight(weight):
    streams, slab_rows, chan_cols = weight.shape
    half = chan_cols // 2
    return pl.pallas_call(
        flip_kernel,
        grid=(streams, 2),
        in_specs=[pl.BlockSpec((1, slab_rows, half), lambda i, j: (i, 0, j))],
        out_specs=pl.BlockSpec((1, half, slab_rows), lambda i, j: (i, j, 0)),
        out_shape=kept((streams, chan_cols, slab_rows)),
        compiler_params=params(),
        cost_estimate=cost(0, 4 * weight.size),
        name="flip_weight",
    )(weight)


BLOCKS = 4


def block_angle(residue, block):
    return math.pi * (2 * residue + 1) * block / (2 * BLOCKS)


def frequencies(count, residue):
    steps = 2 * BLOCKS * np.arange(count // (2 * BLOCKS))
    return steps + residue, steps + 2 * BLOCKS - 1 - residue


def transform_tables(count):
    width = count // BLOCKS
    tables, phases = [], []
    for residue in range(BLOCKS):
        columns, rows = [], []
        for side, freq in zip((1.0, -1.0), frequencies(count, residue)):
            angles = math.pi / (4 * count) * (2 * np.arange(width)[:, None] + 1) * (2 * freq[None] + 1)
            cos, sin = np.cos(angles), np.sin(angles)
            columns += [np.concatenate([cos, side * sin]), np.concatenate([-sin, side * cos])]
            rows.append(math.pi / (4 * count) * (2 * freq + 1))
        tables.append(np.concatenate(columns, axis=1))
        rows = np.concatenate(rows)
        phases += [np.cos(rows), np.sin(rows)]
    return jnp.asarray(np.stack(tables), BF), jnp.asarray(np.stack(phases), F32)


def cut_kernel(core_ref, tokens_ref, out_ref, held_ref, in_sems, out_sems):
    slabs, half, width = held_ref.shape
    start = pl.multiple_of(core_ref[0] * half, half)
    inward = [
        pltpu.make_async_copy(
            tokens_ref.at[0, pl.ds(start, half), slice(slab * width, (slab + 1) * width)],
            held_ref.at[slab],
            in_sems.at[slab],
        )
        for slab in range(slabs)
    ]
    outward = [
        pltpu.make_async_copy(held_ref.at[slab], out_ref.at[slab], out_sems.at[slab])
        for slab in range(slabs)
    ]
    for copy in inward:
        copy.start()
    for slab in range(slabs):
        inward[slab].wait()
        outward[slab].start()
    for copy in outward:
        copy.wait()


def cut_tokens(core, tokens, slabs):
    _, rows, width = tokens.shape
    dims = (slabs, rows // 2, width // slabs)
    return pl.pallas_call(
        cut_kernel,
        in_specs=[pl.BlockSpec(memory_space=pltpu.SMEM), pl.BlockSpec(memory_space=pltpu.HBM)],
        out_specs=pl.BlockSpec(memory_space=pltpu.HBM),
        out_shape=kept(dims),
        scratch_shapes=[
            pltpu.VMEM(dims, BF),
            pltpu.SemaphoreType.DMA((slabs,)),
            pltpu.SemaphoreType.DMA((slabs,)),
        ],
        compiler_params=params(),
        cost_estimate=cost(0, 2 * tokens.size),
        name="cut_tokens",
    )(core, stay(tokens))


def in_order(core, mine_ref, theirs_ref, spread_ref):
    blocks, half, _ = mine_ref.shape
    for block in range(blocks):
        base = 2 * block * half
        spread_ref[pl.ds(pl.multiple_of(base + core * half, half), half)] = mine_ref[block]
        spread_ref[pl.ds(pl.multiple_of(base + (1 - core) * half, half), half)] = theirs_ref[block]


def project_kernel(pos_ref, mine_ref, theirs_ref, weight_ref, edge_ref, out_ref, spread_ref):
    step = pl.program_id(0)
    last = pl.num_programs(0) - 1

    @pl.when(step == 0)
    def _():
        in_order(pos_ref[1], mine_ref, theirs_ref, spread_ref)

    @pl.when(step < last)
    def _():
        result = matmul(weight_ref[0], spread_ref[...], NT).astype(BF)
        out_ref[...] = result.reshape(out_ref.shape)

    @pl.when(step == last)
    def _():
        out_ref[:, : edge_ref.shape[1]] = edge_ref[...]


def project(pos, mine, theirs, weight, edge):
    blocks, half, width = mine.shape
    streams, rows, _ = weight.shape
    slabs, edge_len, positions = edge.shape
    chans = rows // slabs
    return pl.pallas_call(
        project_kernel,
        grid_spec=pltpu.PrefetchScalarGridSpec(
            num_scalar_prefetch=1,
            grid=(streams + 1,),
            in_specs=[
                pl.BlockSpec(memory_space=pltpu.VMEM),
                pl.BlockSpec(memory_space=pltpu.VMEM),
                pl.BlockSpec((1, rows, width), lambda i, pos: (jnp.minimum(i, streams - 1), 0, 0)),
                pl.BlockSpec(edge.shape, lambda i, pos: (0, 0, 0)),
            ],
            out_specs=pl.BlockSpec((slabs, chans, positions), lambda i, pos: (0, i, 0)),
            scratch_shapes=[pltpu.VMEM((positions, width), BF)],
        ),
        out_shape=kept((slabs, streams * chans + edge_len, positions)),
        compiler_params=params(36 << 20),
        cost_estimate=cost(
            2 * positions * width * streams * rows,
            2 * (positions * width + weight.size + positions * streams * rows),
        ),
        name="project",
    )(pos, mine, theirs, stay(weight), stay(edge))


def turn_kernel(pos_ref, mine_ref, theirs_ref, out_ref, spread_ref):
    in_order(pos_ref[1], mine_ref, theirs_ref, spread_ref)
    out_ref[...] = jnp.transpose(spread_ref[...])


def turn_tokens(pos, mine, theirs):
    blocks, half, width = mine.shape
    positions = 2 * blocks * half
    part = width // 4
    block = pl.BlockSpec((blocks, half, part), lambda i, pos: (0, 0, i))
    return pl.pallas_call(
        turn_kernel,
        grid_spec=pltpu.PrefetchScalarGridSpec(
            num_scalar_prefetch=1,
            grid=(4,),
            in_specs=[block, block],
            out_specs=pl.BlockSpec((part, positions), lambda i, pos: (i, 0)),
            scratch_shapes=[pltpu.VMEM((positions, part), BF)],
        ),
        out_shape=kept((width, positions)),
        compiler_params=params(),
        cost_estimate=cost(0, 4 * positions * width),
        name="turn_tokens",
    )(pos, mine, theirs)


def turn_shares_kernel(tokens_ref, out_ref, spread_ref):
    chips, cores, blocks, rows, _ = tokens_ref.shape
    for block in range(blocks):
        for core in range(cores):
            for chip in range(chips):
                base = ((block * cores + core) * chips + chip) * rows
                spread_ref[base : base + rows] = tokens_ref[chip, core, block]
    out_ref[...] = jnp.transpose(spread_ref[...])


def turn_shares(tokens):
    chips, cores, blocks, rows, width = tokens.shape
    positions = chips * cores * blocks * rows
    part = width // 4
    return pl.pallas_call(
        turn_shares_kernel,
        grid=(4,),
        in_specs=[pl.BlockSpec((chips, cores, blocks, rows, part), lambda i: (0, 0, 0, 0, i))],
        out_specs=pl.BlockSpec((part, positions), lambda i: (i, 0)),
        out_shape=kept((width, positions)),
        scratch_shapes=[pltpu.VMEM((positions, part), BF)],
        compiler_params=params(),
        cost_estimate=cost(0, 4 * tokens.size),
        name="turn_shares",
    )(tokens)


def delayed(value, steps):
    if steps == 0:
        return value
    lane = lax.broadcasted_iota(jnp.int32, value.shape, 1)
    return jnp.where(lane < steps, 0.0, pltpu.roll(value, steps, 1))


def advanced(value, steps):
    if steps == 0:
        return value
    lanes = value.shape[1]
    lane = lax.broadcasted_iota(jnp.int32, value.shape, 1)
    return jnp.where(lane >= lanes - steps, 0.0, pltpu.roll(value, lanes - steps, 1))


def two_part(value, table, dims):
    rows = value.shape[0]
    result = matmul(jnp.concatenate(split(value), axis=0), table, dims)
    return result[:rows] + result[rows:]


def spectrum(value, residue, table):
    width = value.shape[1] // BLOCKS
    parts = [value[:, block * width : (block + 1) * width] for block in range(BLOCKS)]
    real = parts[0]
    imag = None
    for block in range(1, BLOCKS):
        angle = block_angle(residue, block)
        real = real + parts[block] * math.cos(angle)
        term = parts[block] * -math.sin(angle)
        imag = term if imag is None else imag + term
    result = two_part(jnp.concatenate([real, imag], axis=1), table, NN)
    steps = result.shape[1] // 4
    quarter = [result[:, i * steps : (i + 1) * steps] for i in range(4)]
    return jnp.concatenate([quarter[0], quarter[2]], axis=1), jnp.concatenate(
        [quarter[1], quarter[3]], axis=1
    )


def from_spectrum(real, imag, residue, table, totals):
    steps = real.shape[1] // 2
    value = jnp.concatenate(
        [real[:, :steps], imag[:, :steps], real[:, steps:], imag[:, steps:]], axis=1
    )
    result = two_part(value, table, NT)
    width = result.shape[1] // 2
    even, odd = result[:, :width], result[:, width:]
    for block in range(BLOCKS):
        angle = block_angle(residue, block)
        term = even if block == 0 else even * math.cos(angle) - odd * math.sin(angle)
        totals[block] = term if totals[block] is None else totals[block] + term


def operator_kernel(grad_scale, parts_ref, taps_ref, phase_ref, table_ref, grads_ref, out_ref, held_ref, sem):
    copy = pltpu.make_async_copy(table_ref, held_ref, sem)
    copy.start()
    sources, _, positions = parts_ref.shape
    block_len = out_ref.shape[2]
    chans = taps_ref.shape[0]
    streams = grads_ref.shape[0] // chans
    taps_len = (taps_ref.shape[1] - 1) // streams

    def tap(stream, pos):
        column = stream * taps_len + pos
        return taps_ref[:, column : column + 1]

    def summed(row):
        total = parts_ref[0, row : row + chans].astype(F32)
        for source in range(1, sources):
            total = total + parts_ref[source, row : row + chans].astype(F32)
        return total

    filtered = []
    for stream in range(streams):
        total = summed(stream * chans)
        acc = tap(stream, 0) * total
        for pos in range(1, taps_len):
            acc = acc + tap(stream, pos) * delayed(total, pos)
        filtered.append(acc)
    query, key, value = filtered
    skip = taps_ref[:, streams * taps_len : streams * taps_len + 1]
    edge = jnp.concatenate(
        [
            unfold(parts_ref[source, streams * chans :], block_len).astype(F32)
            for source in range(sources)
        ],
        axis=1,
    )
    cot, long_filter = edge[:chans], edge[chans:]
    gated = key * value
    d_conv = cot * query
    stacked = jnp.concatenate([gated, d_conv, long_filter], axis=0)
    rows = chans
    totals = [None] * BLOCKS
    copy.wait()
    for residue in range(BLOCKS):
        cos_all, sin_all = spectrum(stacked, residue, held_ref[residue])
        g_real, d_real, h_real = cos_all[:rows], cos_all[rows : 2 * rows], cos_all[2 * rows :]
        g_imag, d_imag, h_imag = sin_all[:rows], sin_all[rows : 2 * rows], sin_all[2 * rows :]
        cos_phase = phase_ref[2 * residue : 2 * residue + 1]
        sin_phase = phase_ref[2 * residue + 1 : 2 * residue + 2]
        f_real = h_real * cos_phase - h_imag * sin_phase
        f_imag = h_real * sin_phase + h_imag * cos_phase
        conv_real = g_real * f_real - g_imag * f_imag
        conv_imag = g_real * f_imag + g_imag * f_real
        back_real = f_real * d_real + f_imag * d_imag
        back_imag = f_real * d_imag - f_imag * d_real
        corr_real = g_real * d_real + g_imag * d_imag
        corr_imag = g_real * d_imag - g_imag * d_real
        lag_real = corr_real * cos_phase + corr_imag * sin_phase
        lag_imag = corr_imag * cos_phase - corr_real * sin_phase
        from_spectrum(
            jnp.concatenate([conv_real, back_real, lag_real], axis=0),
            jnp.concatenate([conv_imag, back_imag, lag_imag], axis=0),
            residue,
            held_ref[residue],
            totals,
        )
    result = jnp.concatenate(totals, axis=1)
    scale = 1.0 / positions
    conv_out = result[:rows] * scale + skip * gated
    d_gated = result[rows : 2 * rows] * scale + skip * d_conv
    filter_part = (result[2 * rows :] * (scale * grad_scale)).astype(BF)
    hyena_out = (query * conv_out).astype(BF)
    for block in range(sources):
        lanes = slice(block * block_len, (block + 1) * block_len)
        out_ref[block, :chans] = hyena_out[:, lanes]
        out_ref[block, chans:] = filter_part[:, lanes]
    for stream, grad in enumerate((cot * conv_out, d_gated * value, d_gated * key)):
        acc = tap(stream, 0) * grad
        for pos in range(1, taps_len):
            acc = acc + tap(stream, pos) * advanced(grad, pos)
        grads_ref[stream * chans : (stream + 1) * chans] = acc.astype(BF)


def operator(parts, taps, phase, table, grad_scale, streams, block_len):
    sources, _, positions = parts.shape
    chans = taps.shape[0]
    rows = streams * chans
    full = pl.BlockSpec(memory_space=pltpu.VMEM)
    return pl.pallas_call(
        functools.partial(operator_kernel, grad_scale),
        in_specs=[full, full, full, pl.BlockSpec(memory_space=pl.ANY)],
        out_shape=(kept((rows, positions)), kept((sources, 2 * chans, block_len))),
        scratch_shapes=[pltpu.VMEM(table.shape, BF), pltpu.SemaphoreType.DMA],
        compiler_params=params(40 << 20),
        cost_estimate=cost(8 * rows * positions * positions, 2 * (parts.size + table.size)),
        name="operator",
    )(parts, taps, phase, stay(table))


def near_kernel(weight_ref, out_ref, sem):
    copy = pltpu.make_async_copy(weight_ref, out_ref, sem)
    copy.start()
    copy.wait()


def near_weight(weight):
    return pl.pallas_call(
        near_kernel,
        in_specs=[pl.BlockSpec(memory_space=pltpu.HBM)],
        out_specs=pl.BlockSpec(memory_space=pltpu.VMEM),
        out_shape=pltpu.VMEM(weight.shape, weight.dtype),
        scratch_shapes=[pltpu.SemaphoreType.DMA],
        compiler_params=params(16 << 20),
        cost_estimate=cost(0, 4 * weight.size),
        name="near_weight",
    )(stay(weight))


def token_kernel(pos_ref, weight_ref, grads_ref, sent_ref, held_ref):
    streams, chips, _, rows, cols = weight_ref.shape
    part = sent_ref.shape[1]
    grads = [grads_ref[:, 0, stream].reshape(cols, part) for stream in range(streams)]
    lanes = pl.ds(pl.multiple_of(pl.program_id(0) * part, part), part)
    for own in (False, True):
        total = None
        side = pos_ref[1] if own else 1 - pos_ref[1]
        for stream in range(streams):
            weight = weight_ref[stream, :, pl.ds(side, 1)].reshape(chips * rows, cols)
            term = matmul(weight, grads[stream], NN)
            total = term if total is None else total + term
        if own:
            held_ref[:, lanes] = total.astype(BF)
        else:
            sent_ref[...] = total.astype(BF)


def token_part(pos, weight, grads):
    streams, chips, cores, rows, cols = weight.shape
    slabs, _, _, chans, positions = grads.shape
    part = positions
    return pl.pallas_call(
        token_kernel,
        grid_spec=pltpu.PrefetchScalarGridSpec(
            num_scalar_prefetch=1,
            grid=(1,),
            in_specs=[
                pl.BlockSpec(memory_space=pltpu.VMEM),
                pl.BlockSpec((slabs, 1, streams, chans, part), lambda j, pos: (0, pos[0], 0, 0, j)),
            ],
            out_specs=[
                pl.BlockSpec((chips * rows, part), lambda j, pos: (0, j)),
                pl.BlockSpec(memory_space=pltpu.VMEM),
            ],
        ),
        out_shape=(kept((chips * rows, positions)), pltpu.VMEM((chips * rows, positions), BF)),
        compiler_params=params(40 << 20),
        cost_estimate=cost(2 * weight.size * positions, 8 * chips * rows * positions),
        name="token_part",
    )(pos, weight, stay(grads))


def pair_kernel(held_ref, received_ref, out_ref):
    out_ref[...] = (held_ref[...].astype(F32) + received_ref[...].astype(F32)).astype(BF)


def pair_sum(held, received):
    return pl.pallas_call(
        pair_kernel,
        in_specs=[pl.BlockSpec(memory_space=pltpu.VMEM)] * 2,
        out_shape=kept(held.shape),
        compiler_params=params(24 << 20),
        cost_estimate=cost(0, 6 * held.size),
        name="pair_sum",
    )(held, received)


def weight_kernel(grad_scale, pos_ref, own_ref, other_ref, own_grads_ref, other_grads_ref, out_ref):
    chan_cols = out_ref.shape[2]
    positions = own_ref.shape[1]
    own = own_grads_ref[...].reshape(chan_cols, positions)
    other = other_grads_ref[...].reshape(chan_cols, positions)
    total = matmul(own_ref[...], own, NT) + matmul(other_ref[...], other, NT)
    out_ref[0] = (total * grad_scale).astype(BF)


def weight_grad(pos, own, other, grads, grad_scale):
    slabs, _, streams, chans, positions = grads.shape
    slab_rows = own.shape[0]
    chan_cols = slabs * chans
    block = (slabs, 1, 1, chans, positions)
    return pl.pallas_call(
        functools.partial(weight_kernel, grad_scale),
        grid_spec=pltpu.PrefetchScalarGridSpec(
            num_scalar_prefetch=1,
            grid=(streams,),
            in_specs=[
                pl.BlockSpec(own.shape, lambda i, pos: (0, 0)),
                pl.BlockSpec(own.shape, lambda i, pos: (0, 0)),
                pl.BlockSpec(block, lambda i, pos: (0, pos[0], i, 0, 0)),
                pl.BlockSpec(block, lambda i, pos: (0, 1 - pos[0], i, 0, 0)),
            ],
            out_specs=pl.BlockSpec((1, slab_rows, chan_cols), lambda i, pos: (i, 0, 0)),
        ),
        out_shape=jax.ShapeDtypeStruct((streams, slab_rows, chan_cols), BF),
        compiler_params=params(),
        cost_estimate=cost(
            4 * streams * slab_rows * chan_cols * positions,
            2 * (2 * own.size + grads.size + streams * slab_rows * chan_cols),
        ),
        name="weight_grad",
    )(pos, own, other, grads, grads)


def total_kernel(parts_ref, out_ref):
    total = parts_ref[0].astype(F32)
    for pos in range(1, parts_ref.shape[0]):
        total = total + parts_ref[pos].astype(F32)
    out_ref[0] = jnp.transpose(total).astype(BF)


def token_total(parts):
    _, rows, positions = parts.shape
    return pl.pallas_call(
        total_kernel,
        out_shape=jax.ShapeDtypeStruct((1, positions, rows), BF),
        compiler_params=params(24 << 20),
        cost_estimate=cost(0, 2 * parts.size),
        name="token_total",
    )(parts)


def finish_kernel(own_ref, other_ref, out_ref, filter_ref):
    slabs, rows, block_len = own_ref.shape
    chans = rows // 2
    hyena = own_ref[:, :chans].astype(F32).reshape(slabs * chans, block_len)
    filters = own_ref[:, chans:].astype(F32) + other_ref[...].astype(F32)
    out_ref[0] = jnp.transpose(hyena).astype(BF)
    filter_ref[...] = jnp.transpose(filters.reshape(slabs * chans, block_len))


def finish(own, other):
    slabs, rows, block_len = own.shape
    chan_cols = slabs * rows // 2
    return pl.pallas_call(
        finish_kernel,
        out_shape=(
            jax.ShapeDtypeStruct((1, block_len, chan_cols), BF),
            jax.ShapeDtypeStruct((block_len, chan_cols), F32),
        ),
        compiler_params=params(24 << 20),
        cost_estimate=cost(0, 4 * own.size),
        name="finish",
    )(own, other)


def exchange(value, axis, groups=None):
    return lax.all_to_all(
        value, axis, split_axis=0, concat_axis=0, tiled=True, axis_index_groups=groups
    )


def local(tokens, in_weight, short_taps, long_filter, skip_gain, cotangent):
    seq_count = lax.axis_size("seq")
    dp_count = lax.axis_size("dp")
    dp_pos = lax.axis_index("dp").astype(jnp.int32)
    seq_pos = lax.axis_index("seq").astype(jnp.int32)
    chan_count = lax.axis_size("chan")
    chan_pos = lax.axis_index("chan").astype(jnp.int32)
    core = chan_pos % 2
    pos = jnp.stack([dp_pos, core])
    tok_rows = tokens.shape[1]
    slab_rows = in_weight.shape[0]
    chan_cols = in_weight.shape[2]
    streams, taps_len = short_taps.shape[:2]
    positions = seq_count * tok_rows
    chans = chan_cols // seq_count
    half = tok_rows // 2
    share = tok_rows // chan_count
    chips = chan_count // 2
    grad_scale = 1.0 / math.sqrt(dp_count * positions)
    batches = [(0, 1), (1, 0)]
    cores = [(i, i ^ 1) for i in range(chan_count)]
    weight = jnp.transpose(in_weight, (1, 0, 2))

    mine, edge, flipped = lax.optimization_barrier(
        (
            exchange(cut_tokens(core[None], tokens, seq_count), "seq"),
            edge_rows(cotangent, long_filter, seq_count, positions),
            flip_weight(weight),
        )
    )
    theirs = lax.ppermute(mine, "chan", cores)
    parts = project(pos, mine, theirs, flipped, edge)

    shares = lax.dynamic_slice_in_dim(mine, chan_pos // 2 * share, share, 1)
    shares = lax.ppermute(shares, "dp", batches)
    parts, shares, short_taps = lax.optimization_barrier((parts, shares, short_taps))
    shares = lax.all_gather(shares, "chan", axis=0)
    shares = shares.reshape(chips, 2, seq_count, share, slab_rows)
    taps = jnp.concatenate([short_taps.reshape(streams * taps_len, chan_cols), skip_gain[None]])
    taps = jnp.transpose(lax.dynamic_slice_in_dim(taps, seq_pos * chans, chans, 1))
    table, phase = transform_tables(positions)
    parts, taps = lax.optimization_barrier((exchange(parts, "seq"), taps))

    grads, outs = operator(parts, taps, phase, table, grad_scale, streams, tok_rows)
    grads, shares, mine, theirs = lax.optimization_barrier((grads, shares, mine, theirs))
    grads = lax.all_gather(grads, ("seq", "dp"), axis=0)
    outs = exchange(outs, "seq")
    finished = finish(outs, lax.ppermute(outs[:, chans:], "dp", batches))
    own, other, near, finished = lax.optimization_barrier(
        (
            turn_tokens(pos, mine, theirs),
            turn_shares(shares),
            weight.reshape(streams, chips, 2, slab_rows // chan_count, chan_cols),
            finished,
        )
    )
    near = near_weight(near)
    grads, finished, own, other = lax.optimization_barrier((grads, finished, own, other))
    hyena_out, grad_filter = finished

    grads = grads.reshape(seq_count, dp_count, streams, chans, positions)
    sent, held = token_part(pos, near, grads)
    token_block = pair_sum(held, lax.ppermute(sent, "chan", cores))
    token_block = exchange(
        token_block.reshape(chips, -1, positions),
        "chan",
        [[chip * 2 + side for chip in range(chips)] for side in range(2)],
    )
    grad_tokens = token_total(token_block)
    grad_weight = weight_grad(pos, own, other, grads, grad_scale)
    return (hyena_out, grad_tokens, jnp.transpose(grad_weight, (1, 0, 2)), grad_filter)


def solution(mesh):
    placed = (
        P("dp", "seq", None),
        P("seq", None, "chan"),
        P(None, None, "chan"),
        P("seq", "chan"),
        P("chan"),
        P("dp", "seq", "chan"),
    )
    return jax.shard_map(
        local,
        mesh=mesh,
        in_specs=placed,
        out_specs=(
            P("dp", "seq", "chan"),
            P("dp", None, ("seq", "chan")),
            P("seq", None, "chan"),
            P("seq", "chan"),
        ),
        check_vma=False,
    )
```
